128 devices in a mesh: gx: 2 (over core), gy: 2 (over x_lo), gz: 32 (over z, y, x_hi).
Axes of the slice: x: 4 (x_hi: 2, x_lo: 2; x = x_hi * 2 + x_lo), y: 4, z: 4, core: 2. Of those that a mesh axis runs over, the one named last changes fastest.
Arguments:
- a_diag: bfloat16 [8, 12, 256, 4096], P('gx', 'gy', 'gz'), may hold values from -0.75 to 0.75
- a_face: bfloat16 [3, 8, 12, 256, 4096], P(None, 'gx', 'gy', 'gz'), may hold values from -0.75 to 0.75
- prolong: bfloat16 [8, 12, 256, 4096], P('gx', 'gy', 'gz'), may hold values from -0.75 to 0.75
- aggregate: int32 [8, 12, 256], P('gx', 'gy', 'gz'), may hold values from 0 to 23
- pair_slot: int32 [7, 8, 12, 256], P(None, 'gx', 'gy', 'gz'), may hold values from 0 to 6
- row_owner: int32 [3072], P(('gx', 'gy', 'gz')), may hold values from 0 to 31, as said below
Outputs:
- coarse: bfloat16 [2, 2, 32, 64, 7, 4096], P('gx', 'gy', 'gz')
The draws below stay inside these ranges and needn't reach their ends.
Inputs may be any that keep to these rules, and one draw needn't show every extreme that they name: `row_owner`: all rows of a device go to owners in its own (gx, gy) column. From each device at most 2 rows go to one owner, and in each column one owner receives exactly 2 rows from every device, so at most 64 rows reach one owner.
All inputs are finite; a program needn't handle non-finite values.
Results may differ from the reference program's by a relative error of at most 0.0049.
Values may be sent and summed in bfloat16 or wider, within the bound.
A program may use at most 256 MiB of HBM per device.

```python
import jax
import jax.numpy as jnp
from jax import lax

NODES = 64
BLOCK = 4096
SLOTS = 7
BX = 4
BY = 6
BZ = 8
AGG_DEV = 24
NX = 8
NY = 12
NZ = 256
NC = 3072
RECV = 64
N_GX = 2
N_GY = 2
N_GZ = 32
DEVICES = 128


def draw_row_owner(key, part):
    capacity = max(2, (AGG_DEV + N_GZ - 1) // N_GZ)
    columns = DEVICES // N_GZ
    key_hot, key_order, key_perm = jax.random.split(key, 3)
    hot = jax.random.randint(key_hot, (columns,), 0, N_GZ)
    hot_dev = jnp.repeat(hot, N_GZ)
    scores = jax.random.randint(key_order, (DEVICES, AGG_DEV), 0, 1 << 20) * AGG_DEV + jnp.arange(AGG_DEV, dtype=jnp.int32)[None, :]
    order = jnp.argsort(scores, axis=1)
    position = jnp.argsort(order, axis=1).astype(jnp.int32)
    others = max(N_GZ - 1, 1)
    perm_scores = jax.random.randint(key_perm, (DEVICES, others), 0, 1 << 20) * others + jnp.arange(others, dtype=jnp.int32)[None, :]
    perm = jnp.argsort(perm_scores, axis=1).astype(jnp.int32)
    group = jnp.clip((position - capacity) // capacity, 0, others - 1)
    offset = jnp.take_along_axis(perm, group, axis=1)
    other = (hot_dev[:, None] + 1 + offset) % N_GZ
    chosen = jnp.where(position < capacity, hot_dev[:, None], other)
    return chosen.reshape(-1).astype(jnp.int32)


def with_ends(drawn, key, smallest, largest):
    longest = drawn.shape.index(max(drawn.shape))
    spots = []
    for shift in (0, 1):
        where = [jax.random.randint(jax.random.fold_in(key, axis), (), 0, length) for axis, length in enumerate(drawn.shape)]
        where[longest] = (where[longest] + shift) % drawn.shape[longest]
        spots.append(tuple(where))
    return drawn.at[spots[0]].set(smallest).at[spots[1]].set(largest)


def steps_of(key, dims, cuts, least, top_value):
    gain, own = 1.0, jax.random.fold_in(key, 6)
    for dim, parts in cuts:
        steps = jnp.exp(jax.random.uniform(jax.random.fold_in(own, dim), (parts,), jnp.float32, least / len(cuts), top_value / len(cuts)))
        gain = gain * jnp.repeat(steps, dims[dim] // parts).reshape([-1 if axis == dim else 1 for axis in range(len(dims))])
    return gain


def bell_draw(stream_key, dims, width, limit, cuts=(), held_as=jnp.bfloat16):
    level = steps_of(stream_key, dims, cuts, -0.22, 0.18) if cuts else 1.0
    drawn = jax.random.normal(stream_key, dims, jnp.float32) * width * level
    return jnp.minimum(jnp.maximum(drawn, -limit), limit).astype(held_as)


def setup_inputs(seed: int = 0) -> dict:
    key_list = jax.random.split(jax.random.key(seed), 7)
    return {
        "a_diag": bell_draw(key_list[0], (NX, NY, NZ, BLOCK), NODES ** -0.5, 0.75, ((0, 2), (1, 2), (2, 32))),
        "a_face": bell_draw(key_list[1], (3, NX, NY, NZ, BLOCK), NODES ** -0.5, 0.75, ((1, 2), (2, 2), (3, 32))),
        "prolong": bell_draw(key_list[2], (NX, NY, NZ, BLOCK), NODES ** -0.5, 0.75, ((0, 2), (1, 2), (2, 32))),
        "aggregate": with_ends(jax.random.randint(key_list[3], (NX, NY, NZ), 0, AGG_DEV), jax.random.fold_in(key_list[3], 1), 0, AGG_DEV - 1).astype(jnp.int32),
        "pair_slot": with_ends(jax.random.randint(key_list[4], (7, NX, NY, NZ), 0, SLOTS), jax.random.fold_in(key_list[4], 1), 0, SLOTS - 1).astype(jnp.int32),
        "row_owner": draw_row_owner(jax.random.fold_in(key_list[6], 71), 0),
    }


def reference(a_diag, a_face, prolong, aggregate, pair_slot, row_owner):
    nodes = NODES
    block = BLOCK
    pad_p = jnp.pad(prolong, ((1, 1), (1, 1), (1, 1), (0, 0)))
    pad_fx = jnp.pad(a_face[0], ((1, 0), (0, 0), (0, 0), (0, 0)))
    jy = jnp.arange(NY, dtype=jnp.int32)
    kz = jnp.arange(NZ, dtype=jnp.int32)

    def mats(x):
        return x.astype(jnp.float32).reshape(NY, NZ, nodes, nodes)

    def forward(a, p):
        return jnp.einsum("yzab,yzbc->yzac", mats(a), mats(p), precision=lax.Precision.HIGHEST)

    def backward(a, p):
        return jnp.einsum("yzba,yzbc->yzac", mats(a), mats(p), precision=lax.Precision.HIGHEST)

    def plane(total, index):
        window = lax.dynamic_slice_in_dim(pad_p, index, 3, 0)
        center = window[1, 1:-1, 1:-1]
        diag_here = lax.dynamic_index_in_dim(a_diag, index, 0, False)
        face_x = lax.dynamic_index_in_dim(a_face[0], index, 0, False)
        face_y = lax.dynamic_index_in_dim(a_face[1], index, 0, False)
        face_z = lax.dynamic_index_in_dim(a_face[2], index, 0, False)
        back_x = lax.dynamic_index_in_dim(pad_fx, index, 0, False)
        back_y = jnp.pad(face_y, ((1, 0), (0, 0), (0, 0)))[:-1]
        back_z = jnp.pad(face_z, ((0, 0), (1, 0), (0, 0)))[:, :-1]
        couple = jnp.stack([
            forward(diag_here, center),
            backward(back_x, window[0, 1:-1, 1:-1]),
            forward(face_x, window[2, 1:-1, 1:-1]),
            backward(back_y, window[1, :-2, 1:-1]),
            forward(face_y, window[1, 2:, 1:-1]),
            backward(back_z, window[1, 1:-1, :-2]),
            forward(face_z, window[1, 1:-1, 2:]),
        ], axis=0).astype(jnp.bfloat16)
        couple = lax.optimization_barrier(couple).astype(jnp.float32)
        terms = jnp.einsum("yzba,fyzbc->fyzac", mats(center), couple, precision=lax.Precision.HIGHEST)
        device = ((index // BX) * N_GY + jy[:, None] // BY) * N_GZ + kz[None, :] // BZ
        rowid = device * AGG_DEV + lax.dynamic_index_in_dim(aggregate, index, 0, False)
        slots = lax.dynamic_index_in_dim(pair_slot, index, 1, False)
        keys = rowid[None] * SLOTS + slots
        total = total + jax.ops.segment_sum(terms.reshape(-1, block), keys.reshape(-1).astype(jnp.int32), NC * SLOTS)
        return total, None

    start = jnp.zeros((NC * SLOTS, block), jnp.float32)
    rows, _ = lax.scan(plane, start, jnp.arange(NX, dtype=jnp.int32))
    columns = N_GX * N_GY
    per_col = N_GZ * AGG_DEV
    rounded = rows.astype(jnp.bfloat16).reshape(columns, per_col, SLOTS, block)
    owners = row_owner.reshape(columns, per_col)
    onehot = (owners[:, :, None] == jnp.arange(N_GZ, dtype=jnp.int32)[None, None, :]).astype(jnp.int32)
    ranks = jnp.cumsum(onehot, axis=1) - 1
    placed = jnp.take_along_axis(ranks, owners[:, :, None], axis=2)[:, :, 0]
    column_ids = jnp.broadcast_to(jnp.arange(columns, dtype=jnp.int32)[:, None], (columns, per_col))
    result = jnp.zeros((columns, N_GZ, RECV, SLOTS, block), jnp.bfloat16)
    result = result.at[column_ids, owners, placed].set(rounded)
    return result.reshape(N_GX, N_GY, N_GZ, RECV, SLOTS, block)
```

```python
import jax
import jax.numpy as jnp
from jax import lax
from jax.experimental import pallas as pl
from jax.experimental.pallas import tpu as pltpu
from jax.sharding import PartitionSpec as P

NODES = 64
SLOTS = 7
AGG_DEV = 24
BX, BY, BZ = 4, 6, 8
LINES = BX * BY
PLACES = 2
ROW = SLOTS * NODES * NODES // 128
PACK = PLACES * ROW + 16
KEYS = AGG_DEV * SLOTS
F32 = jnp.float32
BF16 = jnp.bfloat16


def lane_low(shape):
    return lax.broadcasted_iota(jnp.int32, shape, 1) < 64


def spread(line, scratch):
    values = line.astype(F32)
    for tile in range(32):
        scratch[pl.ds(tile, 8, stride=32), :] = values[:, tile * 128 : tile * 128 + 128]


def spread_twice(line, natural, by_parity):
    values = line.astype(F32)
    low = lane_low((8, 128))
    for tile in range(32):
        here = values[:, tile * 128 : tile * 128 + 128]
        swapped = pltpu.roll(here, 64, axis=1)
        even = jnp.where(low, here, swapped)
        odd = jnp.where(low, swapped, here)
        if natural is not None:
            natural[pl.ds(2 * tile, 8, stride=64), :] = even
            natural[pl.ds(2 * tile + 1, 8, stride=64), :] = odd
        if by_parity is not None:
            by_parity[pl.ds(tile, 8, stride=64), :] = even
            by_parity[pl.ds(32 + tile, 8, stride=64), :] = odd


def compute_kernel(
    agg, slot, owner,
    a_diag, a_face, prolong, rim_x, rim_y, rim_z,
    p_xm, p_xp, p_ym, p_yp, p_zm, p_zp,
    send,
    ra_d, ra_x, ra_y, ra_z, right, left, work_a, work_b, work_c,
    acc_f, acc_b, rows, counts, tally, sems, count_sem,
):
    def store_spread(line, dest, base):
        spread(line, work_a)
        dest[pl.ds(pl.multiple_of(base, 32), 256), :] = work_a[...].astype(BF16)

    right_xp, right_yp, right_zp = LINES, LINES + BY, LINES + BY + BX
    left_xm, left_ym, left_zm = LINES, LINES + BY, LINES + BY + BX

    def store_right(base):
        right[pl.ds(pl.multiple_of(base * 512, 512), 512), :] = work_b[...].astype(BF16)

    def store_left(base):
        low = lane_low((64, 128))
        for pair in range(4):
            first = work_c[pair * 128 : pair * 128 + 64, :]
            second = work_c[pair * 128 + 64 : pair * 128 + 128, :]
            flipped = jnp.where(low, first, second).T
            left[pl.ds(pl.multiple_of(base * 512 + pair * 128, 128), 128), :] = flipped.astype(BF16)

    acc_f[...] = jnp.zeros_like(acc_f)
    acc_b[...] = jnp.zeros_like(acc_b)

    @pl.loop(0, LINES)
    def _(line):
        spread_twice(prolong[line], work_b, work_c)
        store_right(line)
        store_left(line)
        store_spread(a_diag[line], ra_d, line * 256)
        store_spread(a_face[0, line], ra_x, (line + BY) * 256)
        store_spread(a_face[1, line], ra_y, (line + line // BY + 1) * 256)
        store_spread(a_face[2, line], ra_z, line * 288 + 32)

    @pl.loop(0, BY)
    def _(line):
        store_spread(rim_x[line], ra_x, line * 256)
        spread_twice(p_xm[line], None, work_c)
        store_left(left_xm + line)
        spread_twice(p_xp[line], work_b, None)
        store_right(right_xp + line)

    @pl.loop(0, BX)
    def _(line):
        store_spread(rim_y[line], ra_y, line * (BY + 1) * 256)
        spread_twice(p_ym[line], None, work_c)
        store_left(left_ym + line)
        spread_twice(p_yp[line], work_b, None)
        store_right(right_yp + line)

    @pl.loop(0, LINES // 8)
    def _(line):
        spread(rim_z[line], work_a)
        for k in range(8):
            at = (line * 8 + k) * 288
            ra_z[pl.ds(pl.multiple_of(at, 32), 32), :] = work_a[k * 32 : k * 32 + 32, :].astype(BF16)
        spread_twice(p_zm[line], None, work_c)
        store_left(left_zm + line)
        spread_twice(p_zp[line], work_b, None)
        store_right(right_zp + line)

    def products(cell, blocks):
        low = lane_low((64, 128))
        block = right[pl.ds(pl.multiple_of(cell * 64, 64), 64), :]
        zero = jnp.zeros_like(block)
        weight = jnp.concatenate([jnp.where(low, block, zero), jnp.where(low, zero, block)], axis=0)
        stack = [ref[pl.ds(pl.multiple_of(at, 32), 32), :] for ref, at, _, _, _ in blocks]
        stack = jnp.concatenate(stack, axis=0) if len(stack) > 1 else stack[0]
        both = jnp.dot(stack, weight, preferred_element_type=F32)
        turned = pltpu.roll(both, 64, axis=1)
        for number, (_, _, flip, key_f, key_b) in enumerate(blocks):
            part = slice(number * 32, number * 32 + 32)
            couple = jnp.concatenate([both[part], turned[part]], axis=0).astype(BF16)
            lhs = left[pl.ds(pl.multiple_of(flip * 64, 64), 64), :]
            term = jnp.dot(lhs, couple, preferred_element_type=F32)
            if key_f is not None:
                acc_f[key_f] += term
            if key_b is not None:
                acc_b[key_b] += term

    def key(e, number):
        return agg[e] * SLOTS + slot[number, e]

    @pl.loop(0, LINES)
    def _(line):
        x, y = line // BY, line % BY
        flip_x = jnp.where(x > 0, (line - BY) * 8, (left_xm + y) * 8)
        flip_y = jnp.where(y > 0, (line - 1) * 8, (left_ym + x) * 8)
        for z in range(BZ):
            n = line * BZ + z
            back_x = jnp.where(x > 0, n - BY * BZ, 0)
            back_y = jnp.where(y > 0, n - BZ, 0)
            key_x = jnp.where(x > 0, key(back_x, 2), KEYS)
            key_y = jnp.where(y > 0, key(back_y, 4), KEYS)
            products(
                n,
                [
                    (ra_d, n * 32, n, key(n, 0), None),
                    (ra_x, n * 32, flip_x + z, key_x, key(n, 1)),
                    (ra_y, (line + x) * 256 + z * 32, flip_y + z, key_y, key(n, 3)),
                    (
                        ra_z,
                        line * 288 + z * 32,
                        left_zm * 8 + line if z == 0 else n - 1,
                        None if z == 0 else key(n - 1, 6),
                        key(n, 5),
                    ),
                ],
            )
        e = line * BZ + BZ - 1
        products(right_zp * 8 + line, [(ra_z, line * 288 + BZ * 32, e, key(e, 6), None)])

    @pl.loop(0, BY)
    def _(y):
        for z in range(BZ):
            e = ((BX - 1) * BY + y) * BZ + z
            at = (BX * BY + y) * 256 + z * 32
            products((right_xp + y) * 8 + z, [(ra_x, at, e, key(e, 2), None)])

    @pl.loop(0, BX)
    def _(x):
        for z in range(BZ):
            e = (x * BY + BY - 1) * BZ + z
            at = (x * (BY + 1) + BY) * 256 + z * 32
            products((right_yp + x) * 8 + z, [(ra_y, at, e, key(e, 4), None)])

    depth = send.shape[0]

    @pl.loop(0, depth)
    def _(c):
        tally[c] = 0

    @pl.loop(0, AGG_DEV)
    def _(r):
        low = lane_low((32, 128))
        for s in range(SLOTS):
            k = r * SLOTS + s
            work_b[0:64, 0:64] = acc_f[k, :, 0:64] + acc_b[k].T[0:64, :]
            even = work_b[pl.ds(0, 32, stride=2), :]
            odd = work_b[pl.ds(1, 32, stride=2), :]
            row = jnp.where(low, even, pltpu.roll(odd, 64, axis=1)).astype(BF16)
            rows[pl.ds(pl.multiple_of(r * ROW + s * 32, 32), 32), :] = row
        c = owner[r]
        place = tally[c]
        tally[c] = place + 1
        pltpu.make_async_copy(
            rows.at[pl.ds(pl.multiple_of(r * ROW, 32), ROW)],
            send.at[c, pl.ds(pl.multiple_of(place * ROW, 32), ROW)],
            sems.at[r],
        ).start()

    @pl.loop(0, depth)
    def _(c):
        counts[c] = jnp.full((16, 128), tally[c], jnp.int32).astype(F32).astype(BF16)

    told = pltpu.make_async_copy(counts, send.at[:, pl.ds(PLACES * ROW, 16)], count_sem)
    told.start()
    told.wait()

    @pl.loop(0, AGG_DEV)
    def _(r):
        pltpu.make_async_copy(rows.at[pl.ds(0, ROW)], send.at[0, pl.ds(0, ROW)], sems.at[r]).wait()


def coarse_rows(agg, slot, owner, arrays, depth):
    smem = pl.BlockSpec(memory_space=pltpu.SMEM)
    vmem = pl.BlockSpec(memory_space=pltpu.VMEM)
    lines_right = LINES + BY + BX + LINES // 8
    return pl.pallas_call(
        compute_kernel,
        out_shape=jax.ShapeDtypeStruct((depth, PACK, 128), BF16),
        in_specs=[smem] * 3 + [vmem] * len(arrays),
        out_specs=pl.BlockSpec(memory_space=pl.ANY),
        scratch_shapes=[
            pltpu.VMEM((LINES * 256, 128), BF16),
            pltpu.VMEM(((LINES + BY) * 256, 128), BF16),
            pltpu.VMEM((BX * (BY + 1) * 256, 128), BF16),
            pltpu.VMEM((LINES * 288, 128), BF16),
            pltpu.VMEM((lines_right * 512, 128), BF16),
            pltpu.VMEM((lines_right * 512, 64), BF16),
            pltpu.VMEM((256, 128), F32),
            pltpu.VMEM((512, 128), F32),
            pltpu.VMEM((512, 128), F32),
            pltpu.VMEM((KEYS + 1, 64, 128), F32),
            pltpu.VMEM((KEYS + 1, 64, 128), F32),
            pltpu.VMEM((AGG_DEV * ROW, 128), BF16),
            pltpu.VMEM((depth, 16, 128), BF16),
            pltpu.SMEM((depth,), jnp.int32),
            pltpu.SemaphoreType.DMA((AGG_DEV,)),
            pltpu.SemaphoreType.DMA,
        ],
        compiler_params=pltpu.CompilerParams(vmem_limit_bytes=63 << 20),
        name="coarse_rows",
    )(agg, slot, owner, *arrays)


GROUP = 8


def place_kernel(source, total, taken, out, work):
    step = pl.program_id(0)
    for k in range(GROUP):
        t = step * GROUP + k

        @pl.when(t < total[0])
        def _():
            at = source[t]
            row = taken[at // PLACES, pl.ds(pl.multiple_of(at % PLACES * ROW, 32), ROW), :]
            work[k, 0:ROW, :] = row.astype(F32)
            for tile in range(32):
                piece = work[k, pl.ds(tile, SLOTS, stride=32), :]
                out[k, :, tile * 128 : tile * 128 + 128] = piece.astype(BF16)

        @pl.when(t >= total[0])
        def _():
            out[k] = jnp.zeros((SLOTS, NODES * NODES), BF16)


def place_rows(source, total, taken):
    count = source.shape[0]
    return pl.pallas_call(
        place_kernel,
        out_shape=jax.ShapeDtypeStruct((count, SLOTS, NODES * NODES), BF16),
        grid_spec=pltpu.PrefetchScalarGridSpec(
            num_scalar_prefetch=2,
            grid=(count // GROUP,),
            in_specs=[pl.BlockSpec(memory_space=pltpu.VMEM)],
            out_specs=pl.BlockSpec((GROUP, SLOTS, NODES * NODES), lambda i, s, n: (i, 0, 0)),
            scratch_shapes=[pltpu.VMEM((GROUP, 256, 128), F32)],
        ),
        compiler_params=pltpu.CompilerParams(vmem_limit_bytes=40 << 20),
        name="place_rows",
    )(source, total, taken)


def to_next(block, axis):
    count = lax.axis_size(axis)
    return lax.ppermute(block, axis, [(i, i + 1) for i in range(count - 1)])


def to_previous(block, axis):
    count = lax.axis_size(axis)
    return lax.ppermute(block, axis, [(i + 1, i) for i in range(count - 1)])


def shards(a_diag, a_face, prolong, aggregate, pair_slot, row_owner):
    block = a_diag.shape[-1]
    depth = lax.axis_size("gz")
    holding = PLACES * depth

    def face_z(cells):
        return cells.reshape(LINES // 8, 8, block)

    arrays = [
        a_diag.reshape(LINES, BZ, block),
        a_face.reshape(3, LINES, BZ, block),
        prolong.reshape(LINES, BZ, block),
        to_next(a_face[0, BX - 1], "gx"),
        to_next(a_face[1, :, BY - 1], "gy"),
        to_next(face_z(a_face[2, :, :, BZ - 1]), "gz"),
        to_next(prolong[BX - 1], "gx"),
        to_previous(prolong[0], "gx"),
        to_next(prolong[:, BY - 1], "gy"),
        to_previous(prolong[:, 0], "gy"),
        to_next(face_z(prolong[:, :, BZ - 1]), "gz"),
        to_previous(face_z(prolong[:, :, 0]), "gz"),
    ]
    send = coarse_rows(
        aggregate.reshape(-1), pair_slot.reshape(SLOTS, -1), row_owner, arrays, depth
    )
    taken = lax.all_to_all(send, "gz", 0, 0, tiled=True)
    count = taken[:, PLACES * ROW, 0].astype(jnp.int32)
    ends = jnp.cumsum(count)
    spot = jnp.arange(holding, dtype=jnp.int32)
    origin = jnp.sum((ends[None, :] <= spot[:, None]).astype(jnp.int32), axis=1)
    starts = jnp.sum(
        jnp.where(jnp.arange(depth)[None, :] < origin[:, None], count[None, :], 0), axis=1
    )
    source = jnp.minimum(origin * PLACES + (spot - starts), holding - 1)
    coarse = place_rows(source, ends[-1:], taken)
    return coarse.reshape(1, 1, 1, holding, SLOTS, block)


def solution(mesh):
    return jax.shard_map(
        shards,
        mesh=mesh,
        in_specs=(
            P("gx", "gy", "gz", None),
            P(None, "gx", "gy", "gz", None),
            P("gx", "gy", "gz", None),
            P("gx", "gy", "gz"),
            P(None, "gx", "gy", "gz"),
            P(("gx", "gy", "gz")),
        ),
        out_specs=P("gx", "gy", "gz", None, None, None),
        check_vma=False,
    )
```

```python
import jax
import jax.numpy as jnp
from jax import lax
from jax.experimental import pallas as pl
from jax.experimental.pallas import tpu as pltpu
from jax.sharding import PartitionSpec as P

NODES = 64
SLOTS = 7
AGG_DEV = 24
BX, BY, BZ = 4, 6, 8
LINES = BX * BY
PLACES = 2
ROW = SLOTS * NODES * NODES // 128
PACK = PLACES * ROW + 16
KEYS = AGG_DEV * SLOTS
F32 = jnp.float32
BF16 = jnp.bfloat16


def lane_low(shape):
    return lax.broadcasted_iota(jnp.int32, shape, 1) < 64


def spread(line, scratch):
    values = line.astype(F32)
    for tile in range(32):
        scratch[pl.ds(tile, 8, stride=32), :] = values[:, tile * 128 : tile * 128 + 128]


def spread_twice(line, natural, by_parity):
    values = line.astype(F32)
    low = lane_low((8, 128))
    for tile in range(32):
        here = values[:, tile * 128 : tile * 128 + 128]
        swapped = pltpu.roll(here, 64, axis=1)
        even = jnp.where(low, here, swapped)
        odd = jnp.where(low, swapped, here)
        if natural is not None:
            natural[pl.ds(2 * tile, 8, stride=64), :] = even
            natural[pl.ds(2 * tile + 1, 8, stride=64), :] = odd
        if by_parity is not None:
            by_parity[pl.ds(tile, 8, stride=64), :] = even
            by_parity[pl.ds(32 + tile, 8, stride=64), :] = odd


def compute_kernel(
    agg, slot, owner,
    a_diag, a_face, prolong, rim_x, rim_y, rim_z,
    p_xm, p_xp, p_ym, p_yp, p_zm, p_zp,
    send,
    ra_d, ra_x, ra_y, ra_z, right, left, couple, work_a, work_b, work_c,
    acc_f, acc_b, rows, counts, tally, sems, count_sem,
):
    def store_spread(line, dest, base, bench):
        work = work_a.at[bench]
        spread(line, work)
        dest[pl.ds(pl.multiple_of(base, 32), 256), :] = work[...].astype(BF16)

    right_xp, right_yp, right_zp = LINES, LINES + BY, LINES + BY + BX
    left_xm, left_ym, left_zm = LINES, LINES + BY, LINES + BY + BX

    def store_right(base, work):
        right[pl.ds(pl.multiple_of(base * 512, 512), 512), :] = work[...].astype(BF16)

    def store_left(base, work):
        low = lane_low((64, 128))
        zero = jnp.zeros((64, 128), F32)
        for pair in range(4):
            first = work[pair * 128 : pair * 128 + 64, :]
            second = work[pair * 128 + 64 : pair * 128 + 128, :]
            block = jnp.concatenate([jnp.where(low, first, zero), jnp.where(low, zero, second)], axis=0)
            at = pl.multiple_of(base * 512 + pair * 128, 128)
            left[pl.ds(at, 128), :] = block.astype(BF16).T

    acc_f[...] = jnp.zeros_like(acc_f)
    acc_b[...] = jnp.zeros_like(acc_b)

    @pl.loop(0, LINES // 2)
    def _(half):
        for k in range(2):
            line = half * 2 + k
            natural, by_parity = work_b.at[k], work_c.at[k]
            spread_twice(prolong[line], natural, by_parity)
            store_right(line, natural)
            store_left(line, by_parity)
            store_spread(a_diag[line], ra_d, line * 256, 0)
            store_spread(a_face[0, line], ra_x, (line + BY) * 256, 1)
            store_spread(a_face[1, line], ra_y, (line + line // BY + 1) * 256, 2)
            store_spread(a_face[2, line], ra_z, line * 288 + 32, 3)

    @pl.loop(0, BY // 2)
    def _(half):
        for k in range(2):
            line = half * 2 + k
            store_spread(rim_x[line], ra_x, line * 256, k)
            spread_twice(p_xm[line], None, work_c.at[k])
            store_left(left_xm + line, work_c.at[k])
            spread_twice(p_xp[line], work_b.at[k], None)
            store_right(right_xp + line, work_b.at[k])

    @pl.loop(0, BX // 2)
    def _(half):
        for k in range(2):
            line = half * 2 + k
            store_spread(rim_y[line], ra_y, line * (BY + 1) * 256, k)
            spread_twice(p_ym[line], None, work_c.at[k])
            store_left(left_ym + line, work_c.at[k])
            spread_twice(p_yp[line], work_b.at[k], None)
            store_right(right_yp + line, work_b.at[k])

    for line in range(LINES // 8):
        work = work_a.at[line]
        spread(rim_z[line], work)
        for k in range(8):
            at = (line * 8 + k) * 288
            ra_z[at : at + 32, :] = work[k * 32 : k * 32 + 32, :].astype(BF16)
        spread_twice(p_zm[line], None, work_c.at[line % 2])
        store_left(left_zm + line, work_c.at[line % 2])
        spread_twice(p_zp[line], work_b.at[line % 2], None)
        store_right(right_zp + line, work_b.at[line % 2])

    def couples(cell, blocks):
        low = lane_low((64, 128))
        zero = jnp.zeros((64, 128), BF16)
        wide = jnp.zeros((128, 128), BF16)
        columns = []
        for k in range(2):
            block = right[pl.ds(pl.multiple_of((cell + k) * 64, 64), 64), :]
            corner = jnp.concatenate([jnp.where(low, block, zero), jnp.where(low, zero, block)], axis=0)
            columns.append(jnp.concatenate([corner, wide] if k == 0 else [wide, corner], axis=0))
        weight = jnp.concatenate(columns, axis=1)
        stack = [
            jnp.concatenate([ref[pl.ds(pl.multiple_of(at, 32), 32), :] for at in ats], axis=1)
            for _, ref, ats, _ in blocks
        ]
        stack = jnp.concatenate(stack, axis=0) if len(stack) > 1 else stack[0]
        both = jnp.dot(stack, weight, preferred_element_type=F32)
        for number, (f, _, _, cells) in enumerate(blocks):
            for k in range(2):
                part = both[number * 32 : number * 32 + 32, k * 128 : k * 128 + 128]
                turned = pltpu.roll(part, 64, axis=1)
                side = f % 2 * 64
                for p in range(2):
                    value = (part if p == f % 2 else turned)[:, side : side + 64]
                    at = pl.multiple_of(cells[k] * 64 + p * 32, 32)
                    couple[pl.ds(at, 32), f * 64 : f * 64 + 64] = value.astype(BF16)

    def add(ref, at, low_side, value):
        low = lane_low((64, 128))
        zero = jnp.zeros((64, 128), F32)
        ref[at] += jnp.where(low, value, zero) if low_side else jnp.where(low, zero, value)

    def terms(cell, keys, tiles):
        at = pl.multiple_of(cell * 64, 128)
        first, last = tiles
        out = jnp.dot(
            left[pl.ds(at, 128), :],
            couple[pl.ds(at, 128), first * 128 : last * 128],
            preferred_element_type=F32,
        )
        for k in range(2):
            for f, (key_f, key_b) in keys[k].items():
                tile = f // 2 - first
                term = out[k * 64 : k * 64 + 64, tile * 128 : tile * 128 + 128]
                if key_f is not None:
                    add(acc_f, key_f, f % 2 == 0, term)
                if key_b is not None:
                    add(acc_b, key_b, f % 2 == 0, term)

    def key(e, number):
        return agg[e] * SLOTS + slot[number, e]

    cells_xm, cells_ym, cells_zm = left_xm * 8, left_ym * 8, left_zm * 8

    @pl.loop(0, LINES)
    def _(line):
        x, y = line // BY, line % BY
        into_x = jnp.where(x > 0, (line - BY) * 8, cells_xm + y * 8)
        into_y = jnp.where(y > 0, (line - 1) * 8, cells_ym + x * 8)
        for z in range(0, BZ, 2):
            n = line * BZ + z
            couples(
                n,
                [
                    (0, ra_d, [(n + k) * 32 for k in range(2)], [n, n + 1]),
                    (1, ra_x, [(n + k) * 32 for k in range(2)], [into_x + z, into_x + z + 1]),
                    (
                        2,
                        ra_y,
                        [(line + x) * 256 + (z + k) * 32 for k in range(2)],
                        [into_y + z, into_y + z + 1],
                    ),
                    (
                        3,
                        ra_z,
                        [line * 288 + (z + k) * 32 for k in range(2)],
                        [cells_zm + line if z == 0 else n - 1, n],
                    ),
                ],
            )

    @pl.loop(0, BY)
    def _(y):
        for z in range(0, BZ, 2):
            e = ((BX - 1) * BY + y) * BZ + z
            at = (BX * BY + y) * 256 + z * 32
            couples((right_xp + y) * 8 + z, [(1, ra_x, [at, at + 32], [e, e + 1])])

    @pl.loop(0, BX)
    def _(x):
        for z in range(0, BZ, 2):
            e = (x * BY + BY - 1) * BZ + z
            at = (x * (BY + 1) + BY) * 256 + z * 32
            couples((right_yp + x) * 8 + z, [(2, ra_y, [at, at + 32], [e, e + 1])])

    @pl.loop(0, LINES // 2)
    def _(half):
        line = half * 2
        e = line * BZ + BZ - 1
        at = line * 288 + BZ * 32
        couples(right_zp * 8 + line, [(3, ra_z, [at, at + 288], [e, e + BZ])])

    @pl.loop(0, LINES)
    def _(line):
        x, y = line // BY, line % BY
        for z in range(0, BZ, 2):
            keys = []
            for k in range(2):
                e = line * BZ + z + k
                next_x = jnp.where(x < BX - 1, e + BY * BZ, 0)
                next_y = jnp.where(y < BY - 1, e + BZ, 0)
                keys.append(
                    {
                        0: (key(e, 0), None),
                        1: (key(e, 2), jnp.where(x < BX - 1, key(next_x, 1), KEYS)),
                        2: (key(e, 4), jnp.where(y < BY - 1, key(next_y, 3), KEYS)),
                        3: (key(e, 6), key(e + 1, 5) if z + k < BZ - 1 else None),
                    }
                )
            terms(line * BZ + z, keys, (0, 2))

    @pl.loop(0, BY)
    def _(y):
        for z in range(0, BZ, 2):
            n = y * BZ + z
            terms(cells_xm + n, [{1: (None, key(n + k, 1))} for k in range(2)], (0, 1))

    @pl.loop(0, BX)
    def _(x):
        for z in range(0, BZ, 2):
            n = x * BY * BZ + z
            keys = [{2: (None, key(n + k, 3))} for k in range(2)]
            terms(cells_ym + x * BZ + z, keys, (1, 2))

    @pl.loop(0, LINES // 2)
    def _(half):
        n = half * 2 * BZ
        keys = [{3: (None, key(n + k * BZ, 5))} for k in range(2)]
        terms(cells_zm + half * 2, keys, (1, 2))

    depth = send.shape[0]

    @pl.loop(0, depth)
    def _(c):
        tally[c] = 0

    @pl.loop(0, AGG_DEV)
    def _(r):
        low, low_half = lane_low((64, 128)), lane_low((32, 128))

        def folded(ref, s):
            value = ref[r * SLOTS + s]
            return value + pltpu.roll(value, 64, axis=1)

        for s in range(0, SLOTS, 2):
            first = folded(acc_b, s)
            pair = jnp.where(low, first, folded(acc_b, s + 1)) if s + 1 < SLOTS else first
            flipped = pair.T
            for k in range(min(2, SLOTS - s)):
                work = work_b.at[(s + k) // 4, pl.ds((s + k) % 4 * 64, 64)]
                work[:, 0:64] = folded(acc_f, s + k)[:, 0:64] + flipped[k * 64 : k * 64 + 64]
                even = work[pl.ds(0, 32, stride=2), :]
                odd = work[pl.ds(1, 32, stride=2), :]
                row = jnp.where(low_half, even, pltpu.roll(odd, 64, axis=1)).astype(BF16)
                rows[pl.ds(pl.multiple_of(r * ROW + (s + k) * 32, 32), 32), :] = row
        c = owner[r]
        place = tally[c]
        tally[c] = place + 1
        pltpu.make_async_copy(
            rows.at[pl.ds(pl.multiple_of(r * ROW, 32), ROW)],
            send.at[c, pl.ds(pl.multiple_of(place * ROW, 32), ROW)],
            sems.at[r],
        ).start()

    @pl.loop(0, depth)
    def _(c):
        counts[c] = jnp.full((16, 128), tally[c], jnp.int32).astype(F32).astype(BF16)

    told = pltpu.make_async_copy(counts, send.at[:, pl.ds(PLACES * ROW, 16)], count_sem)
    told.start()
    told.wait()

    @pl.loop(0, AGG_DEV)
    def _(r):
        pltpu.make_async_copy(rows.at[pl.ds(0, ROW)], send.at[0, pl.ds(0, ROW)], sems.at[r]).wait()


def coarse_rows(agg, slot, owner, arrays, depth):
    smem = pl.BlockSpec(memory_space=pltpu.SMEM)
    vmem = pl.BlockSpec(memory_space=pltpu.VMEM)
    lines_right = LINES + BY + BX + LINES // 8
    return pl.pallas_call(
        compute_kernel,
        out_shape=jax.ShapeDtypeStruct((depth, PACK, 128), BF16),
        in_specs=[smem] * 3 + [vmem] * len(arrays),
        out_specs=pl.BlockSpec(memory_space=pl.ANY),
        scratch_shapes=[
            pltpu.VMEM((LINES * 256, 128), BF16),
            pltpu.VMEM(((LINES + BY) * 256, 128), BF16),
            pltpu.VMEM((BX * (BY + 1) * 256, 128), BF16),
            pltpu.VMEM((LINES * 288, 128), BF16),
            pltpu.VMEM((lines_right * 512, 128), BF16),
            pltpu.VMEM((lines_right * 512, 128), BF16),
            pltpu.VMEM((lines_right * 512, 256), BF16),
            pltpu.VMEM((4, 256, 128), F32),
            pltpu.VMEM((2, 512, 128), F32),
            pltpu.VMEM((2, 512, 128), F32),
            pltpu.VMEM((KEYS + 1, 64, 128), F32),
            pltpu.VMEM((KEYS + 1, 64, 128), F32),
            pltpu.VMEM((AGG_DEV * ROW, 128), BF16),
            pltpu.VMEM((depth, 16, 128), BF16),
            pltpu.SMEM((depth,), jnp.int32),
            pltpu.SemaphoreType.DMA((AGG_DEV,)),
            pltpu.SemaphoreType.DMA,
        ],
        compiler_params=pltpu.CompilerParams(vmem_limit_bytes=63 << 20),
        name="coarse_rows",
    )(agg, slot, owner, *arrays)


GROUP = 8


def place_kernel(source, total, taken, out, work):
    step = pl.program_id(0)
    for k in range(GROUP):
        t = step * GROUP + k

        @pl.when(t < total[0])
        def _():
            at = source[t]
            row = taken[at // PLACES, pl.ds(pl.multiple_of(at % PLACES * ROW, 32), ROW), :]
            work[k, 0:ROW, :] = row.astype(F32)
            for tile in range(32):
                piece = work[k, pl.ds(tile, SLOTS, stride=32), :]
                out[k, :, tile * 128 : tile * 128 + 128] = piece.astype(BF16)

        @pl.when(t >= total[0])
        def _():
            out[k] = jnp.zeros((SLOTS, NODES * NODES), BF16)


def place_rows(source, total, taken):
    count = source.shape[0]
    return pl.pallas_call(
        place_kernel,
        out_shape=jax.ShapeDtypeStruct((count, SLOTS, NODES * NODES), BF16),
        grid_spec=pltpu.PrefetchScalarGridSpec(
            num_scalar_prefetch=2,
            grid=(count // GROUP,),
            in_specs=[pl.BlockSpec(memory_space=pltpu.VMEM)],
            out_specs=pl.BlockSpec((GROUP, SLOTS, NODES * NODES), lambda i, s, n: (i, 0, 0)),
            scratch_shapes=[pltpu.VMEM((GROUP, 256, 128), F32)],
        ),
        compiler_params=pltpu.CompilerParams(vmem_limit_bytes=40 << 20),
        name="place_rows",
    )(source, total, taken)


def to_next(block, axis):
    count = lax.axis_size(axis)
    return lax.ppermute(block, axis, [(i, i + 1) for i in range(count - 1)])


def to_previous(block, axis):
    count = lax.axis_size(axis)
    return lax.ppermute(block, axis, [(i + 1, i) for i in range(count - 1)])


def shards(a_diag, a_face, prolong, aggregate, pair_slot, row_owner):
    block = a_diag.shape[-1]
    depth = lax.axis_size("gz")
    holding = PLACES * depth

    def face_z(cells):
        return cells.reshape(LINES // 8, 8, block)

    arrays = [
        a_diag.reshape(LINES, BZ, block),
        a_face.reshape(3, LINES, BZ, block),
        prolong.reshape(LINES, BZ, block),
        to_next(a_face[0, BX - 1], "gx"),
        to_next(a_face[1, :, BY - 1], "gy"),
        to_next(face_z(a_face[2, :, :, BZ - 1]), "gz"),
        to_next(prolong[BX - 1], "gx"),
        to_previous(prolong[0], "gx"),
        to_next(prolong[:, BY - 1], "gy"),
        to_previous(prolong[:, 0], "gy"),
        to_next(face_z(prolong[:, :, BZ - 1]), "gz"),
        to_previous(face_z(prolong[:, :, 0]), "gz"),
    ]
    send = coarse_rows(
        aggregate.reshape(-1), pair_slot.reshape(SLOTS, -1), row_owner, arrays, depth
    )
    taken = lax.all_to_all(send, "gz", 0, 0, tiled=True)
    count = taken[:, PLACES * ROW, 0].astype(jnp.int32)
    ends = jnp.cumsum(count)
    spot = jnp.arange(holding, dtype=jnp.int32)
    origin = jnp.sum((ends[None, :] <= spot[:, None]).astype(jnp.int32), axis=1)
    starts = jnp.sum(
        jnp.where(jnp.arange(depth)[None, :] < origin[:, None], count[None, :], 0), axis=1
    )
    source = jnp.minimum(origin * PLACES + (spot - starts), holding - 1)
    coarse = place_rows(source, ends[-1:], taken)
    return coarse.reshape(1, 1, 1, holding, SLOTS, block)


def solution(mesh):
    return jax.shard_map(
        shards,
        mesh=mesh,
        in_specs=(
            P("gx", "gy", "gz", None),
            P(None, "gx", "gy", "gz", None),
            P("gx", "gy", "gz", None),
            P("gx", "gy", "gz"),
            P(None, "gx", "gy", "gz"),
            P(("gx", "gy", "gz")),
        ),
        out_specs=P("gx", "gy", "gz", None, None, None),
        check_vma=False,
    )
```

```python
import jax
import jax.numpy as jnp
from jax import lax
from jax.experimental import pallas as pl
from jax.experimental.pallas import tpu as pltpu
from jax.sharding import PartitionSpec as P

NODES = 64
SLOTS = 7
AGG_DEV = 24
BX, BY, BZ = 4, 6, 8
LINES = BX * BY
PLACES = 2
ROW = SLOTS * NODES * NODES // 128
PACK = PLACES * ROW + 16
KEYS = AGG_DEV * SLOTS
STEP, STEP_TWICE = 36, 68
F32 = jnp.float32
BF16 = jnp.bfloat16


def lane_low(shape):
    return lax.broadcasted_iota(jnp.int32, shape, 1) < 64


def spread(line, scratch):
    values = line.astype(F32)
    for tile in range(32):
        scratch[pl.ds(tile, 8, stride=STEP), :] = values[:, tile * 128 : tile * 128 + 128]


def spread_twice(line, natural, by_parity):
    values = line.astype(F32)
    low = lane_low((8, 128))
    for tile in range(32):
        here = values[:, tile * 128 : tile * 128 + 128]
        swapped = pltpu.roll(here, 64, axis=1)
        even = jnp.where(low, here, swapped)
        odd = jnp.where(low, swapped, here)
        if natural is not None:
            natural[pl.ds(2 * tile, 8, stride=STEP_TWICE), :] = even
            natural[pl.ds(2 * tile + 1, 8, stride=STEP_TWICE), :] = odd
        if by_parity is not None:
            by_parity[pl.ds(tile, 8, stride=STEP_TWICE), :] = even
            by_parity[pl.ds(32 + tile, 8, stride=STEP_TWICE), :] = odd


def compute_kernel(
    keys, onward, owner,
    a_diag, a_face, prolong, rim_x, rim_y, rim_z,
    p_xm, p_xp, p_ym, p_yp, p_zm, p_zp,
    send,
    ra_d, ra_x, ra_y, ra_z, right, left, couple, work_a, work_b, work_c,
    acc_f, acc_b, rows, counts, tally, sems, count_sem,
):
    def store_spread(line, dest, base, bench):
        work = work_a.at[bench]
        spread(line, work)
        for z in range(8):
            at = pl.multiple_of(base + z * 32, 32)
            dest[pl.ds(at, 32), :] = work[z * STEP : z * STEP + 32, :].astype(BF16)

    right_xp, right_yp, right_zp = LINES, LINES + BY, LINES + BY + BX
    left_xm, left_ym, left_zm = LINES, LINES + BY, LINES + BY + BX

    def store_right(base, work):
        for z in range(8):
            at = pl.multiple_of(base * 512 + z * 64, 64)
            right[pl.ds(at, 64), :] = work[z * STEP_TWICE : z * STEP_TWICE + 64, :].astype(BF16)

    def store_left(base, work):
        low = lane_low((64, 128))
        zero = jnp.zeros((64, 128), F32)
        for pair in range(4):
            first, second = (work[z * STEP_TWICE : z * STEP_TWICE + 64, :] for z in (2 * pair, 2 * pair + 1))
            block = jnp.concatenate([jnp.where(low, first, zero), jnp.where(low, zero, second)], axis=0)
            at = pl.multiple_of(base * 512 + pair * 128, 128)
            left[pl.ds(at, 128), :] = block.astype(BF16).T

    acc_f[...] = jnp.zeros_like(acc_f)
    acc_b[...] = jnp.zeros_like(acc_b)

    @pl.loop(0, LINES // 2)
    def _(half):
        for k in range(2):
            line = half * 2 + k
            natural, by_parity = work_b.at[k], work_c.at[k]
            spread_twice(prolong[line], natural, by_parity)
            store_right(line, natural)
            store_left(line, by_parity)
            store_spread(a_diag[line], ra_d, line * 256, 0)
            store_spread(a_face[0, line], ra_x, (line + BY) * 256, 1)
            store_spread(a_face[1, line], ra_y, (line + line // BY + 1) * 256, 2)
            store_spread(a_face[2, line], ra_z, line * 288 + 32, 3)

    @pl.loop(0, BY // 2)
    def _(half):
        for k in range(2):
            line = half * 2 + k
            store_spread(rim_x[line], ra_x, line * 256, k)
            spread_twice(p_xm[line], None, work_c.at[k])
            store_left(left_xm + line, work_c.at[k])
            spread_twice(p_xp[line], work_b.at[k], None)
            store_right(right_xp + line, work_b.at[k])

    @pl.loop(0, BX // 2)
    def _(half):
        for k in range(2):
            line = half * 2 + k
            store_spread(rim_y[line], ra_y, line * (BY + 1) * 256, k)
            spread_twice(p_ym[line], None, work_c.at[k])
            store_left(left_ym + line, work_c.at[k])
            spread_twice(p_yp[line], work_b.at[k], None)
            store_right(right_yp + line, work_b.at[k])

    for line in range(LINES // 8):
        work = work_a.at[line]
        spread(rim_z[line], work)
        for k in range(8):
            at = (line * 8 + k) * 288
            ra_z[at : at + 32, :] = work[k * STEP : k * STEP + 32, :].astype(BF16)
        spread_twice(p_zm[line], None, work_c.at[line % 2])
        store_left(left_zm + line, work_c.at[line % 2])
        spread_twice(p_zp[line], work_b.at[line % 2], None)
        store_right(right_zp + line, work_b.at[line % 2])

    def couples(cell, blocks):
        low = lane_low((64, 128))
        zero = jnp.zeros((64, 128), BF16)
        wide = jnp.zeros((128, 128), BF16)
        columns = []
        for k in range(2):
            block = right[pl.ds(pl.multiple_of((cell + k) * 64, 64), 64), :]
            corner = jnp.concatenate([jnp.where(low, block, zero), jnp.where(low, zero, block)], axis=0)
            columns.append(jnp.concatenate([corner, wide] if k == 0 else [wide, corner], axis=0))
        weight = jnp.concatenate(columns, axis=1)
        stack = [
            jnp.concatenate([ref[pl.ds(pl.multiple_of(at, 32), 32), :] for at in ats], axis=1)
            for _, ref, ats, _ in blocks
        ]
        stack = jnp.concatenate(stack, axis=0) if len(stack) > 1 else stack[0]
        both = jnp.dot(stack, weight, preferred_element_type=F32)
        for number, (f, _, _, cells) in enumerate(blocks):
            for k in range(2):
                part = both[number * 32 : number * 32 + 32, k * 128 : k * 128 + 128]
                turned = pltpu.roll(part, 64, axis=1)
                side = f % 2 * 64
                for p in range(2):
                    value = (part if p == f % 2 else turned)[:, side : side + 64]
                    at = pl.multiple_of(cells[k] * 64 + p * 32, 32)
                    couple[pl.ds(at, 32), f * 64 : f * 64 + 64] = value.astype(BF16)

    def add(ref, at, low_side, value):
        low = lane_low((64, 128))
        zero = jnp.zeros((64, 128), F32)
        ref[at] += jnp.where(low, value, zero) if low_side else jnp.where(low, zero, value)

    def terms(cell, places, tiles):
        at = pl.multiple_of(cell * 64, 128)
        first, last = tiles
        out = jnp.dot(
            left[pl.ds(at, 128), :],
            couple[pl.ds(at, 128), first * 128 : last * 128],
            preferred_element_type=F32,
        )
        for k in range(2):
            for f, (key_f, key_b) in places[k].items():
                tile = f // 2 - first
                term = out[k * 64 : k * 64 + 64, tile * 128 : tile * 128 + 128]
                if key_f is not None:
                    add(acc_f, key_f, f % 2 == 0, term)
                if key_b is not None:
                    add(acc_b, key_b, f % 2 == 0, term)

    cells_xm, cells_ym, cells_zm = left_xm * 8, left_ym * 8, left_zm * 8

    @pl.loop(0, LINES)
    def _(line):
        x, y = line // BY, line % BY
        into_x = jnp.where(x > 0, (line - BY) * 8, cells_xm + y * 8)
        into_y = jnp.where(y > 0, (line - 1) * 8, cells_ym + x * 8)
        for z in range(0, BZ, 2):
            n = line * BZ + z
            couples(
                n,
                [
                    (0, ra_d, [(n + k) * 32 for k in range(2)], [n, n + 1]),
                    (1, ra_x, [(n + k) * 32 for k in range(2)], [into_x + z, into_x + z + 1]),
                    (
                        2,
                        ra_y,
                        [(line + x) * 256 + (z + k) * 32 for k in range(2)],
                        [into_y + z, into_y + z + 1],
                    ),
                    (
                        3,
                        ra_z,
                        [line * 288 + (z + k) * 32 for k in range(2)],
                        [cells_zm + line if z == 0 else n - 1, n],
                    ),
                ],
            )

    @pl.loop(0, BY)
    def _(y):
        for z in range(0, BZ, 2):
            e = ((BX - 1) * BY + y) * BZ + z
            at = (BX * BY + y) * 256 + z * 32
            couples((right_xp + y) * 8 + z, [(1, ra_x, [at, at + 32], [e, e + 1])])

    @pl.loop(0, BX)
    def _(x):
        for z in range(0, BZ, 2):
            e = (x * BY + BY - 1) * BZ + z
            at = (x * (BY + 1) + BY) * 256 + z * 32
            couples((right_yp + x) * 8 + z, [(2, ra_y, [at, at + 32], [e, e + 1])])

    @pl.loop(0, LINES // 2)
    def _(half):
        line = half * 2
        e = line * BZ + BZ - 1
        at = line * 288 + BZ * 32
        couples(right_zp * 8 + line, [(3, ra_z, [at, at + 288], [e, e + BZ])])

    @pl.loop(0, LINES)
    def _(line):
        for z in range(0, BZ, 2):
            places = []
            for k in range(2):
                e = line * BZ + z + k
                places.append(
                    {
                        0: (keys[0, e], None),
                        1: (keys[2, e], onward[0, e]),
                        2: (keys[4, e], onward[1, e]),
                        3: (keys[6, e], onward[2, e] if z + k < BZ - 1 else None),
                    }
                )
            terms(line * BZ + z, places, (0, 2))

    @pl.loop(0, BY)
    def _(y):
        for z in range(0, BZ, 2):
            n = y * BZ + z
            terms(cells_xm + n, [{1: (None, keys[1, n + k])} for k in range(2)], (0, 1))

    @pl.loop(0, BX)
    def _(x):
        for z in range(0, BZ, 2):
            n = x * BY * BZ + z
            places = [{2: (None, keys[3, n + k])} for k in range(2)]
            terms(cells_ym + x * BZ + z, places, (1, 2))

    @pl.loop(0, LINES // 2)
    def _(half):
        n = half * 2 * BZ
        places = [{3: (None, keys[5, n + k * BZ])} for k in range(2)]
        terms(cells_zm + half * 2, places, (1, 2))

    depth = send.shape[0]

    @pl.loop(0, depth)
    def _(c):
        tally[c] = 0

    @pl.loop(0, AGG_DEV)
    def _(r):
        low, low_half = lane_low((64, 128)), lane_low((32, 128))

        for s in range(0, SLOTS, 2):
            first = acc_b[r * SLOTS + s]
            second = acc_b[r * SLOTS + s + 1] if s + 1 < SLOTS else first
            pair = jnp.where(low, first, second)
            pair += pltpu.roll(jnp.where(low, second, first), 64, axis=1)
            flipped = pair.T
            for k in range(min(2, SLOTS - s)):
                acc_f[r * SLOTS + s + k, :, 0:64] += flipped[k * 64 : k * 64 + 64]
        for s in range(SLOTS):
            total = acc_f.at[r * SLOTS + s]
            even = total[pl.ds(0, 32, stride=2), :]
            odd = total[pl.ds(1, 32, stride=2), :]
            row = jnp.where(low_half, even, odd)
            row += pltpu.roll(jnp.where(low_half, odd, even), 64, axis=1)
            rows[pl.ds(pl.multiple_of(r * ROW + s * 32, 32), 32), :] = row.astype(BF16)
        c = owner[r]
        place = tally[c]
        tally[c] = place + 1
        pltpu.make_async_copy(
            rows.at[pl.ds(pl.multiple_of(r * ROW, 32), ROW)],
            send.at[c, pl.ds(pl.multiple_of(place * ROW, 32), ROW)],
            sems.at[r],
        ).start()

    @pl.loop(0, depth)
    def _(c):
        counts[c] = jnp.full((16, 128), tally[c], jnp.int32).astype(F32).astype(BF16)

    told = pltpu.make_async_copy(counts, send.at[:, pl.ds(PLACES * ROW, 16)], count_sem)
    told.start()
    told.wait()

    @pl.loop(0, AGG_DEV)
    def _(r):
        pltpu.make_async_copy(rows.at[pl.ds(0, ROW)], send.at[0, pl.ds(0, ROW)], sems.at[r]).wait()


def coarse_rows(keys, onward, owner, arrays, depth):
    smem = pl.BlockSpec(memory_space=pltpu.SMEM)
    vmem = pl.BlockSpec(memory_space=pltpu.VMEM)
    lines_right = LINES + BY + BX + LINES // 8
    return pl.pallas_call(
        compute_kernel,
        out_shape=jax.ShapeDtypeStruct((depth, PACK, 128), BF16),
        in_specs=[smem] * 3 + [vmem] * len(arrays),
        out_specs=pl.BlockSpec(memory_space=pl.ANY),
        scratch_shapes=[
            pltpu.VMEM((LINES * 256, 128), BF16),
            pltpu.VMEM(((LINES + BY) * 256, 128), BF16),
            pltpu.VMEM((BX * (BY + 1) * 256, 128), BF16),
            pltpu.VMEM((LINES * 288, 128), BF16),
            pltpu.VMEM((lines_right * 512, 128), BF16),
            pltpu.VMEM((lines_right * 512, 128), BF16),
            pltpu.VMEM((lines_right * 512, 256), BF16),
            pltpu.VMEM((4, 8 * STEP, 128), F32),
            pltpu.VMEM((2, 8 * STEP_TWICE, 128), F32),
            pltpu.VMEM((2, 8 * STEP_TWICE, 128), F32),
            pltpu.VMEM((KEYS + 1, 64, 128), F32),
            pltpu.VMEM((KEYS + 1, 64, 128), F32),
            pltpu.VMEM((AGG_DEV * ROW, 128), BF16),
            pltpu.VMEM((depth, 16, 128), BF16),
            pltpu.SMEM((depth,), jnp.int32),
            pltpu.SemaphoreType.DMA((AGG_DEV,)),
            pltpu.SemaphoreType.DMA,
        ],
        compiler_params=pltpu.CompilerParams(vmem_limit_bytes=63 << 20),
        name="coarse_rows",
    )(keys, onward, owner, *arrays)


GROUP = 8


def place_kernel(source, total, taken, out, work):
    step = pl.program_id(0)
    for k in range(GROUP):
        t = step * GROUP + k

        @pl.when(t < total[0])
        def _():
            at = source[t]
            row = taken[at // PLACES, pl.ds(pl.multiple_of(at % PLACES * ROW, 32), ROW), :]
            for s in range(SLOTS):
                work[k, s * STEP : s * STEP + 32, :] = row[s * 32 : s * 32 + 32].astype(F32)
            for tile in range(32):
                piece = work[k, pl.ds(tile, SLOTS, stride=STEP), :]
                out[k, :, tile * 128 : tile * 128 + 128] = piece.astype(BF16)

        @pl.when(t >= total[0])
        def _():
            out[k] = jnp.zeros((SLOTS, NODES * NODES), BF16)


def place_rows(source, total, taken):
    count = source.shape[0]
    return pl.pallas_call(
        place_kernel,
        out_shape=jax.ShapeDtypeStruct((count, SLOTS, NODES * NODES), BF16),
        grid_spec=pltpu.PrefetchScalarGridSpec(
            num_scalar_prefetch=2,
            grid=(count // GROUP,),
            in_specs=[pl.BlockSpec(memory_space=pltpu.VMEM)],
            out_specs=pl.BlockSpec((GROUP, SLOTS, NODES * NODES), lambda i, s, n: (i, 0, 0)),
            scratch_shapes=[pltpu.VMEM((GROUP, 256, 128), F32)],
        ),
        compiler_params=pltpu.CompilerParams(vmem_limit_bytes=40 << 20),
        name="place_rows",
    )(source, total, taken)


def to_next(block, axis):
    count = lax.axis_size(axis)
    return lax.ppermute(block, axis, [(i, i + 1) for i in range(count - 1)])


def to_previous(block, axis):
    count = lax.axis_size(axis)
    return lax.ppermute(block, axis, [(i + 1, i) for i in range(count - 1)])


def shards(a_diag, a_face, prolong, aggregate, pair_slot, row_owner):
    block = a_diag.shape[-1]
    depth = lax.axis_size("gz")
    holding = PLACES * depth

    def face_z(cells):
        return cells.reshape(LINES // 8, 8, block)

    arrays = [
        a_diag.reshape(LINES, BZ, block),
        a_face.reshape(3, LINES, BZ, block),
        prolong.reshape(LINES, BZ, block),
        to_next(a_face[0, BX - 1], "gx"),
        to_next(a_face[1, :, BY - 1], "gy"),
        to_next(face_z(a_face[2, :, :, BZ - 1]), "gz"),
        to_next(prolong[BX - 1], "gx"),
        to_previous(prolong[0], "gx"),
        to_next(prolong[:, BY - 1], "gy"),
        to_previous(prolong[:, 0], "gy"),
        to_next(face_z(prolong[:, :, BZ - 1]), "gz"),
        to_previous(face_z(prolong[:, :, 0]), "gz"),
    ]
    keys = aggregate[None] * SLOTS + pair_slot
    onward = jnp.stack(
        [
            jnp.pad(keys[1, 1:], ((0, 1), (0, 0), (0, 0)), constant_values=KEYS),
            jnp.pad(keys[3, :, 1:], ((0, 0), (0, 1), (0, 0)), constant_values=KEYS),
            jnp.pad(keys[5, :, :, 1:], ((0, 0), (0, 0), (0, 1)), constant_values=KEYS),
        ]
    )
    send = coarse_rows(keys.reshape(SLOTS, -1), onward.reshape(3, -1), row_owner, arrays, depth)
    taken = lax.all_to_all(send, "gz", 0, 0, tiled=True)
    count = taken[:, PLACES * ROW, 0].astype(jnp.int32)
    ends = jnp.cumsum(count)
    spot = jnp.arange(holding, dtype=jnp.int32)
    origin = jnp.sum((ends[None, :] <= spot[:, None]).astype(jnp.int32), axis=1)
    starts = jnp.sum(
        jnp.where(jnp.arange(depth)[None, :] < origin[:, None], count[None, :], 0), axis=1
    )
    source = jnp.minimum(origin * PLACES + (spot - starts), holding - 1)
    coarse = place_rows(source, ends[-1:], taken)
    return coarse.reshape(1, 1, 1, holding, SLOTS, block)


def solution(mesh):
    return jax.shard_map(
        shards,
        mesh=mesh,
        in_specs=(
            P("gx", "gy", "gz", None),
            P(None, "gx", "gy", "gz", None),
            P("gx", "gy", "gz", None),
            P("gx", "gy", "gz"),
            P(None, "gx", "gy", "gz"),
            P(("gx", "gy", "gz")),
        ),
        out_specs=P("gx", "gy", "gz", None, None, None),
        check_vma=False,
    )
```

```python
import jax
import jax.numpy as jnp
from jax import lax
from jax.experimental import pallas as pl
from jax.experimental.pallas import tpu as pltpu
from jax.sharding import PartitionSpec as P

NODES = 64
SLOTS = 7
AGG_DEV = 24
BX, BY, BZ = 4, 6, 8
LINES = BX * BY
PLACES = 2
ROW = SLOTS * NODES * NODES // 128
PACK = PLACES * ROW + 16
KEYS = AGG_DEV * SLOTS
STEP, STEP_TWICE = 36, 68
F32 = jnp.float32
BF16 = jnp.bfloat16


def lane_low(shape):
    return lax.broadcasted_iota(jnp.int32, shape, 1) < 64


def spread(line, scratch):
    values = line.astype(F32)
    for tile in range(32):
        scratch[pl.ds(tile, 8, stride=STEP), :] = values[:, tile * 128 : tile * 128 + 128]


def spread_twice(line, natural, by_parity):
    values = line.astype(F32)
    low = lane_low((8, 128))
    for tile in range(32):
        here = values[:, tile * 128 : tile * 128 + 128]
        swapped = pltpu.roll(here, 64, axis=1)
        even = jnp.where(low, here, swapped)
        odd = jnp.where(low, swapped, here)
        if natural is not None:
            natural[pl.ds(2 * tile, 8, stride=STEP_TWICE), :] = even
            natural[pl.ds(2 * tile + 1, 8, stride=STEP_TWICE), :] = odd
        if by_parity is not None:
            by_parity[pl.ds(tile, 8, stride=STEP_TWICE), :] = even
            by_parity[pl.ds(32 + tile, 8, stride=STEP_TWICE), :] = odd


MESH = pl.DeviceIdType.MESH


def halo_kernel(
    prolong, a_face,
    rim_x, rim_y, rim_z, p_xm, p_xp, p_ym, p_yp, p_zm, p_zp,
    cells, faces, work, zero, zero_z, out_az, out_p_last, out_p_first, load_sems, send_sems, recv_sems, zero_sems,
):
    depth = lax.axis_size("gz")
    gx, gy, gz = (lax.axis_index(axis) for axis in ("gx", "gy", "gz"))
    next_z, previous_z = lax.rem(gz + 1, depth), lax.rem(gz + depth - 1, depth)
    barrier = pltpu.get_barrier_semaphore()
    for target in ({"gx": 1 - gx}, {"gy": 1 - gy}, {"gz": next_z}, {"gz": previous_z}):
        pl.semaphore_signal(barrier, inc=1, device_id=target, device_id_type=MESH)
    loads = [
        pltpu.make_async_copy(prolong, cells, load_sems.at[0]),
        pltpu.make_async_copy(a_face.at[2], faces, load_sems.at[1]),
    ]
    for load in loads:
        load.start()
    zero[...] = jnp.zeros_like(zero)
    zero_z[...] = jnp.zeros_like(zero_z)
    pl.semaphore_wait(barrier, 4)

    def exchange(number, source, dest, target, sends, receives, blank):
        copy = pltpu.make_async_remote_copy(
            source, dest, send_sems.at[number], recv_sems.at[number], device_id=target, device_id_type=MESH
        )
        fill = pltpu.make_async_copy(blank, dest, zero_sems.at[number])

        @pl.when(sends)
        def _():
            copy.start()

        @pl.when(jnp.logical_not(receives))
        def _():
            fill.start()

        def finish():
            @pl.when(sends)
            def _():
                copy.wait_send()

            @pl.when(receives)
            def _():
                copy.wait_recv()

            @pl.when(jnp.logical_not(receives))
            def _():
                fill.wait()

        return finish

    ends = []
    for number, axis, here, last, first, pairs in (
        (0, "gx", gx, lambda ref: ref.at[BX - 1], lambda ref: ref.at[0], (p_xm, p_xp, rim_x)),
        (3, "gy", gy, lambda ref: ref.at[:, BY - 1], lambda ref: ref.at[:, 0], (p_ym, p_yp, rim_y)),
    ):
        count = lax.axis_size(axis)
        up, down = {axis: lax.rem(here + 1, count)}, {axis: lax.rem(here + count - 1, count)}
        before, after = here > 0, here < count - 1
        blank = zero.at[pl.ds(0, pairs[0].shape[0])]
        ends += [
            exchange(number, last(prolong), pairs[0], up, after, before, blank),
            exchange(number + 1, first(prolong), pairs[1], down, before, after, blank),
            exchange(number + 2, last(a_face.at[number // 3]), pairs[2], up, after, before, blank),
        ]
    for load in loads:
        load.wait()

    @pl.loop(0, LINES)
    def _(line):
        at = pl.ds(pl.multiple_of(line * 32, 32), 32)
        x, y = line // BY, line % BY
        spread(cells[x, y], work.at[0])
        out_p_first[at, :] = work[0, 0:32, :].astype(BF16)
        out_p_last[at, :] = work[0, 7 * STEP : 7 * STEP + 32, :].astype(BF16)
        spread(faces[x, y], work.at[1])
        out_az[at, :] = work[1, 7 * STEP : 7 * STEP + 32, :].astype(BF16)

    before, after = gz > 0, gz < depth - 1
    ends += [
        exchange(6, out_p_last, p_zm, {"gz": next_z}, after, before, zero_z),
        exchange(7, out_p_first, p_zp, {"gz": previous_z}, before, after, zero_z),
        exchange(8, out_az, rim_z, {"gz": next_z}, after, before, zero_z),
    ]
    for finish in ends:
        finish()


def halo(prolong, a_face):
    any_space = pl.BlockSpec(memory_space=pl.ANY)
    x_face, y_face, z_face = (BY, BZ, NODES * NODES), (BX, BZ, NODES * NODES), (LINES * 32, 128)
    shapes = (x_face, y_face, z_face, x_face, x_face, y_face, y_face, z_face, z_face)
    return pl.pallas_call(
        halo_kernel,
        out_shape=[jax.ShapeDtypeStruct(shape, BF16) for shape in shapes],
        in_specs=[any_space] * 2,
        out_specs=[any_space] * len(shapes),
        scratch_shapes=[
            pltpu.VMEM(prolong.shape, BF16),
            pltpu.VMEM(prolong.shape, BF16),
            pltpu.VMEM((2, 8 * STEP, 128), F32),
            pltpu.VMEM(x_face, BF16),
            pltpu.VMEM(z_face, BF16),
            pltpu.VMEM(z_face, BF16),
            pltpu.VMEM(z_face, BF16),
            pltpu.VMEM(z_face, BF16),
            pltpu.SemaphoreType.DMA((2,)),
            pltpu.SemaphoreType.DMA((9,)),
            pltpu.SemaphoreType.DMA((9,)),
            pltpu.SemaphoreType.DMA((9,)),
        ],
        compiler_params=pltpu.CompilerParams(collective_id=0, has_side_effects=True, vmem_limit_bytes=63 << 20),
        name="halo",
    )(prolong, a_face)


def compute_kernel(
    aggregate, slot, owner,
    a_diag, a_face, prolong, rim_x, rim_y, rim_z,
    p_xm, p_xp, p_ym, p_yp, p_zm, p_zp,
    send, keys, key_work, key_sem,
    ra_d, ra_x, ra_y, ra_z, right, left, couple, work_a, work_b, work_c,
    acc_f, acc_b, rows, counts, tally, sems, count_sem,
):
    def store_spread(line, dest, base, bench):
        work = work_a.at[bench]
        spread(line, work)
        for z in range(8):
            at = pl.multiple_of(base + z * 32, 32)
            dest[pl.ds(at, 32), :] = work[z * STEP : z * STEP + 32, :].astype(BF16)

    right_xp, right_yp, right_zp = LINES, LINES + BY, LINES + BY + BX
    left_xm, left_ym, left_zm = LINES, LINES + BY, LINES + BY + BX

    def store_right(base, work):
        for z in range(8):
            at = pl.multiple_of(base * 512 + z * 64, 64)
            right[pl.ds(at, 64), :] = work[z * STEP_TWICE : z * STEP_TWICE + 64, :].astype(BF16)

    def store_left(base, work):
        low = lane_low((64, 128))
        zero = jnp.zeros((64, 128), F32)
        for pair in range(4):
            first, second = (work[z * STEP_TWICE : z * STEP_TWICE + 64, :] for z in (2 * pair, 2 * pair + 1))
            block = jnp.concatenate([jnp.where(low, first, zero), jnp.where(low, zero, second)], axis=0)
            at = pl.multiple_of(base * 512 + pair * 128, 128)
            left[pl.ds(at, 128), :] = block.astype(BF16).T

    key_work[...] = aggregate[...][None] * SLOTS + slot[...]
    told_keys = pltpu.make_async_copy(key_work, keys, key_sem)
    told_keys.start()
    acc_f[...] = jnp.zeros_like(acc_f)
    acc_b[...] = jnp.zeros_like(acc_b)

    @pl.loop(0, LINES // 2)
    def _(half):
        for k in range(2):
            line = half * 2 + k
            natural, by_parity = work_b.at[k], work_c.at[k]
            spread_twice(prolong[line], natural, by_parity)
            store_right(line, natural)
            store_left(line, by_parity)
            store_spread(a_diag[line], ra_d, line * 256, 0)
            store_spread(a_face[0, line], ra_x, (line + BY) * 256, 1)
            store_spread(a_face[1, line], ra_y, (line + line // BY + 1) * 256, 2)
            store_spread(a_face[2, line], ra_z, line * 288 + 32, 3)

    @pl.loop(0, BY // 2)
    def _(half):
        for k in range(2):
            line = half * 2 + k
            store_spread(rim_x[line], ra_x, line * 256, k)
            spread_twice(p_xm[line], None, work_c.at[k])
            store_left(left_xm + line, work_c.at[k])
            spread_twice(p_xp[line], work_b.at[k], None)
            store_right(right_xp + line, work_b.at[k])

    @pl.loop(0, BX // 2)
    def _(half):
        for k in range(2):
            line = half * 2 + k
            store_spread(rim_y[line], ra_y, line * (BY + 1) * 256, k)
            spread_twice(p_ym[line], None, work_c.at[k])
            store_left(left_ym + line, work_c.at[k])
            spread_twice(p_yp[line], work_b.at[k], None)
            store_right(right_yp + line, work_b.at[k])

    @pl.loop(0, LINES // 2)
    def _(half):
        low = lane_low((32, 128))
        blocks = []
        for k in range(2):
            line = half * 2 + k
            at = pl.ds(pl.multiple_of(line * 32, 32), 32)
            ra_z[pl.ds(pl.multiple_of(line * 288, 32), 32), :] = rim_z[at, :]
            here = p_zp[at, :].astype(F32)
            turned = pltpu.roll(here, 64, axis=1)
            work = work_b.at[k]
            work[pl.ds(0, 32, stride=2), :] = jnp.where(low, here, turned)
            work[pl.ds(1, 32, stride=2), :] = jnp.where(low, turned, here)
            at_right = pl.multiple_of((right_zp * 8 + line) * 64, 64)
            right[pl.ds(at_right, 64), :] = work[0:64, :].astype(BF16)
            here = p_zm[at, :].astype(F32)
            turned = pltpu.roll(here, 64, axis=1)
            zero = jnp.zeros_like(here)
            if k == 0:
                blocks += [jnp.where(low, here, zero), jnp.where(low, turned, zero)]
            else:
                blocks += [jnp.where(low, zero, turned), jnp.where(low, zero, here)]
        block = jnp.concatenate(blocks, axis=0).astype(BF16)
        left[pl.ds(pl.multiple_of((left_zm * 8 + half * 2) * 64, 128), 128), :] = block.T

    def couples(cell, blocks):
        low = lane_low((64, 128))
        zero = jnp.zeros((64, 128), BF16)
        wide = jnp.zeros((128, 128), BF16)
        columns = []
        for k in range(2):
            block = right[pl.ds(pl.multiple_of((cell + k) * 64, 64), 64), :]
            corner = jnp.concatenate([jnp.where(low, block, zero), jnp.where(low, zero, block)], axis=0)
            columns.append(jnp.concatenate([corner, wide] if k == 0 else [wide, corner], axis=0))
        weight = jnp.concatenate(columns, axis=1)
        stack = [
            jnp.concatenate([ref[pl.ds(pl.multiple_of(at, 32), 32), :] for at in ats], axis=1)
            for _, ref, ats, _ in blocks
        ]
        stack = jnp.concatenate(stack, axis=0) if len(stack) > 1 else stack[0]
        both = jnp.dot(stack, weight, preferred_element_type=F32)
        for number, (f, _, _, cells) in enumerate(blocks):
            for k in range(2):
                part = both[number * 32 : number * 32 + 32, k * 128 : k * 128 + 128]
                turned = pltpu.roll(part, 64, axis=1)
                side = f % 2 * 64
                for p in range(2):
                    value = (part if p == f % 2 else turned)[:, side : side + 64]
                    at = pl.multiple_of(cells[k] * 64 + p * 32, 32)
                    couple[pl.ds(at, 32), f * 64 : f * 64 + 64] = value.astype(BF16)

    def add(ref, at, low_side, value):
        low = lane_low((64, 128))
        zero = jnp.zeros((64, 128), F32)
        ref[at] += jnp.where(low, value, zero) if low_side else jnp.where(low, zero, value)

    def terms(cell, places, tiles):
        at = pl.multiple_of(cell * 64, 128)
        first, last = tiles
        out = jnp.dot(
            left[pl.ds(at, 128), :],
            couple[pl.ds(at, 128), first * 128 : last * 128],
            preferred_element_type=F32,
        )
        for k in range(2):
            for f, (key_f, key_b) in places[k].items():
                tile = f // 2 - first
                term = out[k * 64 : k * 64 + 64, tile * 128 : tile * 128 + 128]
                if key_f is not None:
                    add(acc_f, key_f, f % 2 == 0, term)
                if key_b is not None:
                    add(acc_b, key_b, f % 2 == 0, term)

    cells_xm, cells_ym, cells_zm = left_xm * 8, left_ym * 8, left_zm * 8
    told_keys.wait()

    @pl.loop(0, LINES)
    def _(line):
        x, y = line // BY, line % BY
        into_x = jnp.where(x > 0, (line - BY) * 8, cells_xm + y * 8)
        into_y = jnp.where(y > 0, (line - 1) * 8, cells_ym + x * 8)
        for z in range(0, BZ, 2):
            n = line * BZ + z
            couples(
                n,
                [
                    (0, ra_d, [(n + k) * 32 for k in range(2)], [n, n + 1]),
                    (1, ra_x, [(n + k) * 32 for k in range(2)], [into_x + z, into_x + z + 1]),
                    (
                        2,
                        ra_y,
                        [(line + x) * 256 + (z + k) * 32 for k in range(2)],
                        [into_y + z, into_y + z + 1],
                    ),
                    (
                        3,
                        ra_z,
                        [line * 288 + (z + k) * 32 for k in range(2)],
                        [cells_zm + line if z == 0 else n - 1, n],
                    ),
                ],
            )

    @pl.loop(0, BY)
    def _(y):
        for z in range(0, BZ, 2):
            e = ((BX - 1) * BY + y) * BZ + z
            at = (BX * BY + y) * 256 + z * 32
            couples((right_xp + y) * 8 + z, [(1, ra_x, [at, at + 32], [e, e + 1])])

    @pl.loop(0, BX)
    def _(x):
        for z in range(0, BZ, 2):
            e = (x * BY + BY - 1) * BZ + z
            at = (x * (BY + 1) + BY) * 256 + z * 32
            couples((right_yp + x) * 8 + z, [(2, ra_y, [at, at + 32], [e, e + 1])])

    @pl.loop(0, LINES // 2)
    def _(half):
        line = half * 2
        e = line * BZ + BZ - 1
        at = line * 288 + BZ * 32
        couples(right_zp * 8 + line, [(3, ra_z, [at, at + 288], [e, e + BZ])])

    @pl.loop(0, LINES)
    def _(line):
        x, y = line // BY, line % BY
        next_x, next_y = jnp.minimum(x + 1, BX - 1), jnp.minimum(y + 1, BY - 1)
        for z in range(0, BZ, 2):
            places = []
            for k in range(z, z + 2):
                onward_x = jnp.where(x < BX - 1, keys[1, y, next_x, k], KEYS)
                onward_y = jnp.where(y < BY - 1, keys[3, next_y, x, k], KEYS)
                places.append(
                    {
                        0: (keys[0, y, x, k], None),
                        1: (keys[2, y, x, k], onward_x),
                        2: (keys[4, y, x, k], onward_y),
                        3: (keys[6, y, x, k], keys[5, y, x, k + 1] if k < BZ - 1 else None),
                    }
                )
            terms(line * BZ + z, places, (0, 2))

    @pl.loop(0, BY)
    def _(y):
        for z in range(0, BZ, 2):
            n = y * BZ + z
            terms(cells_xm + n, [{1: (None, keys[1, y, 0, z + k])} for k in range(2)], (0, 1))

    @pl.loop(0, BX)
    def _(x):
        for z in range(0, BZ, 2):
            places = [{2: (None, keys[3, 0, x, z + k])} for k in range(2)]
            terms(cells_ym + x * BZ + z, places, (1, 2))

    @pl.loop(0, LINES // 2)
    def _(half):
        line = half * 2
        places = [{3: (None, keys[5, line % BY + k, line // BY, 0])} for k in range(2)]
        terms(cells_zm + half * 2, places, (1, 2))

    depth = send.shape[0]

    @pl.loop(0, depth)
    def _(c):
        tally[c] = 0

    @pl.loop(0, AGG_DEV)
    def _(r):
        low, low_half = lane_low((64, 128)), lane_low((32, 128))

        for s in range(0, SLOTS, 2):
            first = acc_b[r * SLOTS + s]
            second = acc_b[r * SLOTS + s + 1] if s + 1 < SLOTS else first
            pair = jnp.where(low, first, second)
            pair += pltpu.roll(jnp.where(low, second, first), 64, axis=1)
            flipped = pair.T
            for k in range(min(2, SLOTS - s)):
                acc_f[r * SLOTS + s + k, :, 0:64] += flipped[k * 64 : k * 64 + 64]
        for s in range(SLOTS):
            total = acc_f.at[r * SLOTS + s]
            even = total[pl.ds(0, 32, stride=2), :]
            odd = total[pl.ds(1, 32, stride=2), :]
            row = jnp.where(low_half, even, odd)
            row += pltpu.roll(jnp.where(low_half, odd, even), 64, axis=1)
            rows[pl.ds(pl.multiple_of(r * ROW + s * 32, 32), 32), :] = row.astype(BF16)
        c = owner[r]
        place = tally[c]
        tally[c] = place + 1
        pltpu.make_async_copy(
            rows.at[pl.ds(pl.multiple_of(r * ROW, 32), ROW)],
            send.at[c, pl.ds(pl.multiple_of(place * ROW, 32), ROW)],
            sems.at[r],
        ).start()

    @pl.loop(0, depth)
    def _(c):
        counts[c] = jnp.full((16, 128), tally[c], jnp.int32).astype(F32).astype(BF16)

    told = pltpu.make_async_copy(counts, send.at[:, pl.ds(PLACES * ROW, 16)], count_sem)
    told.start()
    told.wait()

    @pl.loop(0, AGG_DEV)
    def _(r):
        pltpu.make_async_copy(rows.at[pl.ds(0, ROW)], send.at[0, pl.ds(0, ROW)], sems.at[r]).wait()


def coarse_rows(aggregate, slot, owner, arrays, depth):
    smem = pl.BlockSpec(memory_space=pltpu.SMEM)
    vmem = pl.BlockSpec(memory_space=pltpu.VMEM)
    lines_right = LINES + BY + BX + LINES // 8
    return pl.pallas_call(
        compute_kernel,
        out_shape=jax.ShapeDtypeStruct((depth, PACK, 128), BF16),
        in_specs=[vmem, vmem, smem] + [vmem] * len(arrays),
        out_specs=pl.BlockSpec(memory_space=pl.ANY),
        scratch_shapes=[
            pltpu.SMEM((SLOTS, BY, BX, BZ), jnp.int32),
            pltpu.VMEM((SLOTS, BY, BX, BZ), jnp.int32),
            pltpu.SemaphoreType.DMA,
            pltpu.VMEM((LINES * 256, 128), BF16),
            pltpu.VMEM(((LINES + BY) * 256, 128), BF16),
            pltpu.VMEM((BX * (BY + 1) * 256, 128), BF16),
            pltpu.VMEM((LINES * 288, 128), BF16),
            pltpu.VMEM((lines_right * 512, 128), BF16),
            pltpu.VMEM((lines_right * 512, 128), BF16),
            pltpu.VMEM((lines_right * 512, 256), BF16),
            pltpu.VMEM((4, 8 * STEP, 128), F32),
            pltpu.VMEM((2, 8 * STEP_TWICE, 128), F32),
            pltpu.VMEM((2, 8 * STEP_TWICE, 128), F32),
            pltpu.VMEM((KEYS + 1, 64, 128), F32),
            pltpu.VMEM((KEYS + 1, 64, 128), F32),
            pltpu.VMEM((AGG_DEV * ROW, 128), BF16),
            pltpu.VMEM((depth, 16, 128), BF16),
            pltpu.SMEM((depth,), jnp.int32),
            pltpu.SemaphoreType.DMA((AGG_DEV,)),
            pltpu.SemaphoreType.DMA,
        ],
        compiler_params=pltpu.CompilerParams(vmem_limit_bytes=63 << 20),
        name="coarse_rows",
    )(aggregate, slot, owner, *arrays)


GROUP, ROW_STEP = 8, ROW + 4


def place_kernel(taken, out, told, counts, tally, source, held, work, shaped, sems, row_sems, out_sems):
    depth, count = taken.shape[0], out.shape[1]
    load = pltpu.make_async_copy(taken.at[:, pl.ds(PLACES * ROW, 16)], told, sems.at[0])
    load.start()

    @pl.loop(0, count + PLACES)
    def _(t):
        source[t] = 0

    load.wait()
    for c in range(depth):
        counts[c : c + 1, :] = told[c, 0:1, :].astype(F32).astype(jnp.int32)
    move = pltpu.make_async_copy(counts, tally, sems.at[1])
    move.start()
    move.wait()

    def order(c, total):
        for k in range(PLACES):
            source[total + k] = c * PLACES + k
        return total + tally[c, 0]

    total = lax.fori_loop(0, depth, order, 0)

    def row_copy(t):
        at = source[t]
        place = pl.multiple_of(lax.rem(at, PLACES) * ROW, 32)
        return pltpu.make_async_copy(taken.at[at // PLACES, pl.ds(place, ROW)], held.at[t], row_sems.at[t])

    @pl.loop(0, count)
    def _(t):
        @pl.when(t >= total)
        def _():
            source[t] = 0

        row_copy(t).start()

    def out_copy(group):
        rows = pl.ds(pl.multiple_of(group * GROUP, GROUP), GROUP)
        return pltpu.make_async_copy(shaped.at[group], out.at[:, rows, :], out_sems.at[group])

    @pl.loop(0, count // GROUP)
    def _(group):
        for k in range(GROUP):
            t = group * GROUP + k
            row_copy(t).wait()
            row = held[t].astype(F32)
            work[k * ROW_STEP : k * ROW_STEP + ROW, :] = jnp.where(t < total, row, jnp.zeros_like(row))
        for s in range(SLOTS):
            for tile in range(32):
                piece = work[pl.ds(s * 32 + tile, GROUP, stride=ROW_STEP), :]
                shaped[group, s, :, tile * 128 : tile * 128 + 128] = piece.astype(BF16)
        out_copy(group).start()

    @pl.loop(0, count // GROUP)
    def _(group):
        out_copy(group).wait()


def place_rows(taken):
    depth = taken.shape[0]
    count = depth * PLACES
    any_space = pl.BlockSpec(memory_space=pl.ANY)
    return pl.pallas_call(
        place_kernel,
        out_shape=jax.ShapeDtypeStruct((SLOTS, count, NODES * NODES), BF16),
        in_specs=[any_space],
        out_specs=any_space,
        scratch_shapes=[
            pltpu.VMEM((depth, 16, 128), BF16),
            pltpu.VMEM((depth, 128), jnp.int32),
            pltpu.SMEM((depth, 128), jnp.int32),
            pltpu.SMEM((count + PLACES,), jnp.int32),
            pltpu.VMEM((count, ROW, 128), BF16),
            pltpu.VMEM((GROUP * ROW_STEP, 128), F32),
            pltpu.VMEM((count // GROUP, SLOTS, GROUP, NODES * NODES), BF16),
            pltpu.SemaphoreType.DMA((2,)),
            pltpu.SemaphoreType.DMA((count,)),
            pltpu.SemaphoreType.DMA((count // GROUP,)),
        ],
        compiler_params=pltpu.CompilerParams(vmem_limit_bytes=63 << 20),
        name="place_rows",
    )(taken)


def shards(a_diag, a_face, prolong, aggregate, pair_slot, row_owner):
    block = a_diag.shape[-1]
    depth = lax.axis_size("gz")
    holding = PLACES * depth

    arrays = [
        a_diag.reshape(LINES, BZ, block),
        a_face.reshape(3, LINES, BZ, block),
        prolong.reshape(LINES, BZ, block),
        *halo(prolong, a_face),
    ]
    send = coarse_rows(
        aggregate.transpose(1, 0, 2), pair_slot.transpose(0, 2, 1, 3), row_owner, arrays, depth
    )
    taken = lax.all_to_all(send, "gz", 0, 0, tiled=True)
    coarse = place_rows(taken).transpose(1, 0, 2)
    return coarse.reshape(1, 1, 1, holding, SLOTS, block)


def solution(mesh):
    return jax.shard_map(
        shards,
        mesh=mesh,
        in_specs=(
            P("gx", "gy", "gz", None),
            P(None, "gx", "gy", "gz", None),
            P("gx", "gy", "gz", None),
            P("gx", "gy", "gz"),
            P(None, "gx", "gy", "gz"),
            P(("gx", "gy", "gz")),
        ),
        out_specs=P("gx", "gy", "gz", None, None, None),
        check_vma=False,
    )
```

```python
import jax
import jax.numpy as jnp
from jax import lax
from jax.experimental import pallas as pl
from jax.experimental.pallas import tpu as pltpu
from jax.sharding import PartitionSpec as P

NODES = 64
SLOTS = 7
AGG_DEV = 24
BX, BY, BZ = 4, 6, 8
LINES = BX * BY
PLACES = 2
ROW = SLOTS * NODES * NODES // 128
PACK = PLACES * ROW + 16
KEYS = AGG_DEV * SLOTS
STEP, STEP_TWICE = 36, 68
F32 = jnp.float32
BF16 = jnp.bfloat16


def lane_low(shape):
    return lax.broadcasted_iota(jnp.int32, shape, 1) < 64


def spread(line, scratch):
    values = line.astype(F32)
    for tile in range(32):
        scratch[pl.ds(tile, 8, stride=STEP), :] = values[:, tile * 128 : tile * 128 + 128]


def spread_twice(line, natural, by_parity):
    values = line.astype(F32)
    low = lane_low((8, 128))
    for tile in range(32):
        here = values[:, tile * 128 : tile * 128 + 128]
        swapped = pltpu.roll(here, 64, axis=1)
        even = jnp.where(low, here, swapped)
        odd = jnp.where(low, swapped, here)
        if natural is not None:
            natural[pl.ds(2 * tile, 8, stride=STEP_TWICE), :] = even
            natural[pl.ds(2 * tile + 1, 8, stride=STEP_TWICE), :] = odd
        if by_parity is not None:
            by_parity[pl.ds(tile, 8, stride=STEP_TWICE), :] = even
            by_parity[pl.ds(32 + tile, 8, stride=STEP_TWICE), :] = odd


MESH = pl.DeviceIdType.MESH


def couples(right, cell, stride, couple, blocks):
    low = lane_low((64, 128))
    zero = jnp.zeros((64, 128), BF16)
    wide = jnp.zeros((128, 128), BF16)
    columns = []
    for k in range(2):
        block = right[pl.ds(pl.multiple_of((cell + k * stride) * 64, 64), 64), :]
        corner = jnp.concatenate([jnp.where(low, block, zero), jnp.where(low, zero, block)], axis=0)
        columns.append(jnp.concatenate([corner, wide] if k == 0 else [wide, corner], axis=0))
    weight = jnp.concatenate(columns, axis=1)
    stack = [
        jnp.concatenate([ref[pl.ds(pl.multiple_of(at, 32), 32), :] for at in ats], axis=1)
        for _, ref, ats, _ in blocks
    ]
    stack = jnp.concatenate(stack, axis=0) if len(stack) > 1 else stack[0]
    both = jnp.dot(stack, weight, preferred_element_type=F32)
    for number, (f, _, _, cells) in enumerate(blocks):
        for k in range(2):
            part = both[number * 32 : number * 32 + 32, k * 128 : k * 128 + 128]
            turned = pltpu.roll(part, 64, axis=1)
            side = f % 2 * 64
            for p in range(2):
                value = (part if p == f % 2 else turned)[:, side : side + 64]
                at = pl.multiple_of(cells[k] * 64 + p * 32, 32)
                couple[pl.ds(at, 32), f * 64 : f * 64 + 64] = value.astype(BF16)


def store_spread(line, dest, base, work):
    spread(line, work)
    for z in range(8):
        at = pl.multiple_of(base + z * 32, 32)
        dest[pl.ds(at, 32), :] = work[z * STEP : z * STEP + 32, :].astype(BF16)


def store_right(right, base, work):
    for z in range(8):
        at = pl.multiple_of(base * 512 + z * 64, 64)
        right[pl.ds(at, 64), :] = work[z * STEP_TWICE : z * STEP_TWICE + 64, :].astype(BF16)


def store_left(left, base, work):
    low = lane_low((64, 128))
    zero = jnp.zeros((64, 128), F32)
    for pair in range(4):
        first, second = (work[z * STEP_TWICE : z * STEP_TWICE + 64, :] for z in (2 * pair, 2 * pair + 1))
        block = jnp.concatenate([jnp.where(low, first, zero), jnp.where(low, zero, second)], axis=0)
        at = pl.multiple_of(base * 512 + pair * 128, 128)
        left[pl.ds(at, 128), :] = block.astype(BF16).T


CELLS = LINES * BZ


def inner_kernel(
    prolong, a_face, a_diag,
    rim_x, rim_y, rim_z, p_xm, p_xp, p_ym, p_yp, p_zm, p_zp,
    couple_out, left_out, right_x, right_y, right_z, face_x, face_y, face_z,
    in_p, in_d, in_f, zero, zero_z, out_az, out_p_last, out_p_first,
    ra_d, ra_x, ra_y, ra_z, right, first_z, left, couple, work_a, work_b, work_c,
    load_sems, send_sems, recv_sems, zero_sems, out_sems,
):
    depth = lax.axis_size("gz")
    gx, gy, gz = (lax.axis_index(axis) for axis in ("gx", "gy", "gz"))
    next_z, previous_z = lax.rem(gz + 1, depth), lax.rem(gz + depth - 1, depth)
    barrier = pltpu.get_barrier_semaphore()
    for target in ({"gx": 1 - gx}, {"gy": 1 - gy}, {"gz": next_z}, {"gz": previous_z}):
        pl.semaphore_signal(barrier, inc=1, device_id=target, device_id_type=MESH)
    loads = [
        pltpu.make_async_copy(prolong, in_p, load_sems.at[0]),
        pltpu.make_async_copy(a_face.at[2], in_f.at[2], load_sems.at[1]),
        pltpu.make_async_copy(a_diag, in_d, load_sems.at[2]),
        pltpu.make_async_copy(a_face.at[pl.ds(0, 2)], in_f.at[pl.ds(0, 2)], load_sems.at[3]),
    ]
    for load in loads:
        load.start()
    zero[...] = jnp.zeros_like(zero)
    zero_z[...] = jnp.zeros_like(zero_z)
    pl.semaphore_wait(barrier, 4)

    def exchange(number, source, dest, target, sends, receives, blank):
        copy = pltpu.make_async_remote_copy(
            source, dest, send_sems.at[number], recv_sems.at[number], device_id=target, device_id_type=MESH
        )
        fill = pltpu.make_async_copy(blank, dest, zero_sems.at[number])

        @pl.when(sends)
        def _():
            copy.start()

        @pl.when(jnp.logical_not(receives))
        def _():
            fill.start()

        def finish():
            @pl.when(sends)
            def _():
                copy.wait_send()

            @pl.when(receives)
            def _():
                copy.wait_recv()

            @pl.when(jnp.logical_not(receives))
            def _():
                fill.wait()

        return finish

    ends = []
    for number, axis, here, last, first, pairs in (
        (3, "gy", gy, lambda ref: ref.at[:, BY - 1], lambda ref: ref.at[:, 0], (p_ym, p_yp, rim_y)),
        (0, "gx", gx, lambda ref: ref.at[BX - 1], lambda ref: ref.at[0], (p_xm, p_xp, rim_x)),
    ):
        count = lax.axis_size(axis)
        up, down = {axis: lax.rem(here + 1, count)}, {axis: lax.rem(here + count - 1, count)}
        before, after = here > 0, here < count - 1
        blank = zero.at[pl.ds(0, pairs[0].shape[0])]
        ends += [
            exchange(number, last(prolong), pairs[0], up, after, before, blank),
            exchange(number + 1, first(prolong), pairs[1], down, before, after, blank),
            exchange(number + 2, last(a_face.at[number // 3]), pairs[2], up, after, before, blank),
        ]

    loads[0].wait()
    loads[1].wait()

    @pl.loop(0, LINES // 2)
    def _(half):
        low = lane_low((32, 128))
        for k in range(2):
            line = half * 2 + k
            x, y = line // BY, line % BY
            at = pl.ds(pl.multiple_of(line * 32, 32), 32)
            natural, by_parity, work = work_b.at[k], work_c.at[k], work_a.at[k]
            spread_twice(in_p[x, y], natural, by_parity)
            for z, dest in ((0, out_p_first), (BZ - 1, out_p_last)):
                even, odd = (by_parity[z * STEP_TWICE + p * 32 : z * STEP_TWICE + p * 32 + 32, :] for p in range(2))
                dest[at, :] = jnp.where(low, even, odd).astype(BF16)
            store_spread(in_f[2, x, y], ra_z, line * 288 + 32, work)
            out_az[at, :] = work[(BZ - 1) * STEP : (BZ - 1) * STEP + 32, :].astype(BF16)
            ra_z[pl.ds(pl.multiple_of(line * 288, 32), 32), :] = jnp.zeros((32, 128), BF16)
            store_right(right, line, natural)
            first_z[pl.ds(pl.multiple_of(line * 64, 64), 64), :] = natural[0:64, :].astype(BF16)
            store_left(left, line, by_parity)

    before, after = gz > 0, gz < depth - 1
    ends += [
        exchange(6, out_p_last, p_zm, {"gz": next_z}, after, before, zero_z),
        exchange(7, out_p_first, p_zp, {"gz": previous_z}, before, after, zero_z),
        exchange(8, out_az, rim_z, {"gz": next_z}, after, before, zero_z),
    ]
    loads[2].wait()
    loads[3].wait()

    @pl.loop(0, LINES)
    def _(line):
        x, y = line // BY, line % BY
        store_spread(in_d[x, y], ra_d, line * 256, work_a.at[0])
        store_spread(in_f[0, x, y], ra_x, line * 256, work_a.at[1])
        store_spread(in_f[1, x, y], ra_y, line * 256, work_a.at[2])

    moves = []

    def put(source, dest):
        copy = pltpu.make_async_copy(source, dest, out_sems.at[len(moves)])
        copy.start()
        moves.append(copy)

    put(left, left_out)
    put(right.at[pl.ds(0, BY * 512)], right_x)
    put(first_z, right_z)
    put(ra_x.at[pl.ds((LINES - BY) * 256, BY * 256)], face_x)
    put(out_az, face_z)
    for x in range(BX):
        put(right.at[pl.ds(x * BY * 512, 512)], right_y.at[pl.ds(x * 512, 512)])
        put(ra_y.at[pl.ds((x * BY + BY - 1) * 256, 256)], face_y.at[pl.ds(x * 256, 256)])

    for x in range(BX):

        @pl.loop(0, BY)
        def _(y):
            line = x * BY + y
            from_y = jnp.where(y > 0, line - 1, line)
            into_y = jnp.where(y > 0, (line - 1) * BZ, CELLS)
            for z in range(0, BZ, 2):
                n = line * BZ + z
                both = range(2)
                blocks = [
                    (0, ra_d, [(n + k) * 32 for k in both], [n, n + 1]),
                    (2, ra_y, [from_y * 256 + (z + k) * 32 for k in both], [into_y + z, into_y + z + 1]),
                    (3, ra_z, [line * 288 + (z + k) * 32 for k in both], [CELLS if z == 0 else n - 1, n]),
                ]
                if x > 0:
                    e = n - BY * BZ
                    blocks.append((1, ra_x, [(e + k) * 32 for k in both], [e, e + 1]))
                couples(right, n, 1, couple, blocks)

        if x > 0:
            rows = pl.ds((x - 1) * BY * BZ * 64, BY * BZ * 64)
            put(couple.at[rows], couple_out.at[rows])
    rows = pl.ds((BX - 1) * BY * BZ * 64, BY * BZ * 64)
    put(couple.at[rows], couple_out.at[rows])
    for finish in ends:
        finish()
    for copy in moves:
        copy.wait()


def inner(prolong, a_face, a_diag):
    any_space = pl.BlockSpec(memory_space=pl.ANY)
    x_face, y_face, z_face = (BY, BZ, NODES * NODES), (BX, BZ, NODES * NODES), (LINES * 32, 128)
    shapes = (
        x_face, y_face, z_face, x_face, x_face, y_face, y_face, z_face, z_face,
        (CELLS * 64, 256), (CELLS * 64, 128),
        (BY * 512, 128), (BX * 512, 128), (LINES * 64, 128),
        (BY * 256, 128), (BX * 256, 128), z_face,
    )
    return pl.pallas_call(
        inner_kernel,
        out_shape=[jax.ShapeDtypeStruct(shape, BF16) for shape in shapes],
        in_specs=[any_space] * 3,
        out_specs=[any_space] * len(shapes),
        scratch_shapes=[
            pltpu.VMEM(prolong.shape, BF16),
            pltpu.VMEM(a_diag.shape, BF16),
            pltpu.VMEM(a_face.shape, BF16),
            pltpu.VMEM(x_face, BF16),
            pltpu.VMEM(z_face, BF16),
            pltpu.VMEM(z_face, BF16),
            pltpu.VMEM(z_face, BF16),
            pltpu.VMEM(z_face, BF16),
            pltpu.VMEM((LINES * 256, 128), BF16),
            pltpu.VMEM((LINES * 256, 128), BF16),
            pltpu.VMEM((LINES * 256, 128), BF16),
            pltpu.VMEM((LINES * 288, 128), BF16),
            pltpu.VMEM((CELLS * 64, 128), BF16),
            pltpu.VMEM((LINES * 64, 128), BF16),
            pltpu.VMEM((CELLS * 64, 128), BF16),
            pltpu.VMEM(((CELLS + BZ) * 64, 256), BF16),
            pltpu.VMEM((3, 8 * STEP, 128), F32),
            pltpu.VMEM((2, 8 * STEP_TWICE, 128), F32),
            pltpu.VMEM((2, 8 * STEP_TWICE, 128), F32),
            pltpu.SemaphoreType.DMA((4,)),
            pltpu.SemaphoreType.DMA((9,)),
            pltpu.SemaphoreType.DMA((9,)),
            pltpu.SemaphoreType.DMA((9,)),
            pltpu.SemaphoreType.DMA((5 + 3 * BX,)),
        ],
        compiler_params=pltpu.CompilerParams(collective_id=0, has_side_effects=True, vmem_limit_bytes=63 << 20),
        name="inner",
    )(prolong, a_face, a_diag)


def compute_kernel(
    aggregate, slot, owner,
    rim_x, rim_y, rim_z, p_xm, p_xp, p_ym, p_yp, p_zm, p_zp,
    couple_in, left_in, right_x, right_y, right_z, face_x, face_y, face_z,
    send, keys, key_work, key_sem, in_sems, edge, right, left, couple, work_a, work_b, work_c,
    acc_f, acc_b, rows, counts, tally, sems, count_sem,
):
    plane = BY * BZ * 64
    brought = []
    for x in range(BX):
        at = pl.ds(x * plane, plane)
        for k, (source, dest) in enumerate(((couple_in, couple), (left_in, left))):
            copy = pltpu.make_async_copy(source.at[at], dest.at[at], in_sems.at[x, k])
            copy.start()
            brought.append(copy)

    key_work[...] = aggregate[...][None] * SLOTS + slot[...]
    told_keys = pltpu.make_async_copy(key_work, keys, key_sem)
    told_keys.start()
    acc_f[...] = jnp.zeros_like(acc_f)
    acc_b[...] = jnp.zeros_like(acc_b)

    right_xp, right_yp, right_zp = 0, BY, BY + BX
    left_xm, left_ym, left_zm = LINES, LINES + BY, LINES + BY + BX
    cells_xm, cells_ym, cells_zm = left_xm * 8, left_ym * 8, left_zm * 8

    for count, rim, before, after, near, base in (
        (BY, rim_x, p_xm, p_xp, left_xm, right_xp),
        (BX, rim_y, p_ym, p_yp, left_ym, right_yp),
    ):

        @pl.loop(0, count // 2)
        def _(half):
            for k in range(2):
                line = half * 2 + k
                store_spread(rim[line], edge, (base + line) * 256, work_a.at[k])
                spread_twice(before[line], None, work_c.at[k])
                store_left(left, near + line, work_c.at[k])
                spread_twice(after[line], work_b.at[k], None)
                store_right(right, base + line, work_b.at[k])

    @pl.loop(0, LINES // 2)
    def _(half):
        low = lane_low((32, 128))
        blocks = []
        for k in range(2):
            line = half * 2 + k
            at = pl.ds(pl.multiple_of(line * 32, 32), 32)
            here = p_zp[at, :].astype(F32)
            turned = pltpu.roll(here, 64, axis=1)
            work = work_b.at[k]
            work[pl.ds(0, 32, stride=2), :] = jnp.where(low, here, turned)
            work[pl.ds(1, 32, stride=2), :] = jnp.where(low, turned, here)
            at_right = pl.multiple_of((right_zp * 8 + line) * 64, 64)
            right[pl.ds(at_right, 64), :] = work[0:64, :].astype(BF16)
            here = p_zm[at, :].astype(F32)
            turned = pltpu.roll(here, 64, axis=1)
            zero = jnp.zeros_like(here)
            if k == 0:
                blocks += [jnp.where(low, here, zero), jnp.where(low, turned, zero)]
            else:
                blocks += [jnp.where(low, zero, turned), jnp.where(low, zero, here)]
        block = jnp.concatenate(blocks, axis=0).astype(BF16)
        left[pl.ds(pl.multiple_of((left_zm * 8 + half * 2) * 64, 128), 128), :] = block.T

    for count, f, base, beyond, weights in ((BY, 1, right_xp, cells_xm, right_x), (BX, 2, right_yp, cells_ym, right_y)):

        @pl.loop(0, count)
        def _(line):
            for z in range(0, BZ, 2):
                at = (base + line) * 256 + z * 32
                e = beyond + line * BZ + z
                couples(weights, line * BZ + z, 1, couple, [(f, edge, [at, at + 32], [e, e + 1])])

    @pl.loop(0, LINES // 2)
    def _(half):
        line = half * 2
        e = cells_zm + line
        couples(right_z, line, 1, couple, [(3, rim_z, [line * 32, line * 32 + 32], [e, e + 1])])

    for copy in brought:
        copy.wait()

    @pl.loop(0, BY)
    def _(y):
        for z in range(0, BZ, 2):
            e = ((BX - 1) * BY + y) * BZ + z
            at = y * 256 + z * 32
            couples(right, (right_xp + y) * 8 + z, 1, couple, [(1, face_x, [at, at + 32], [e, e + 1])])

    @pl.loop(0, BX)
    def _(x):
        for z in range(0, BZ, 2):
            e = (x * BY + BY - 1) * BZ + z
            at = x * 256 + z * 32
            couples(right, (right_yp + x) * 8 + z, 1, couple, [(2, face_y, [at, at + 32], [e, e + 1])])

    @pl.loop(0, LINES // 2)
    def _(half):
        line = half * 2
        e = line * BZ + BZ - 1
        couples(right, right_zp * 8 + line, 1, couple, [(3, face_z, [line * 32, line * 32 + 32], [e, e + BZ])])

    def add(ref, at, low_side, value):
        low = lane_low((64, 128))
        zero = jnp.zeros((64, 128), F32)
        ref[at] += jnp.where(low, value, zero) if low_side else jnp.where(low, zero, value)

    def terms(cell, places, tiles):
        at = pl.multiple_of(cell * 64, 128)
        first, last = tiles
        out = jnp.dot(
            left[pl.ds(at, 128), :],
            couple[pl.ds(at, 128), first * 128 : last * 128],
            preferred_element_type=F32,
        )
        for k in range(2):
            for f, (key_f, key_b) in places[k].items():
                tile = f // 2 - first
                term = out[k * 64 : k * 64 + 64, tile * 128 : tile * 128 + 128]
                if key_f is not None:
                    add(acc_f, key_f, f % 2 == 0, term)
                if key_b is not None:
                    add(acc_b, key_b, f % 2 == 0, term)

    told_keys.wait()

    @pl.loop(0, LINES)
    def _(line):
        x, y = line // BY, line % BY
        next_x, next_y = jnp.minimum(x + 1, BX - 1), jnp.minimum(y + 1, BY - 1)
        for z in range(0, BZ, 2):
            places = []
            for k in range(z, z + 2):
                onward_x = jnp.where(x < BX - 1, keys[1, y, next_x, k], KEYS)
                onward_y = jnp.where(y < BY - 1, keys[3, next_y, x, k], KEYS)
                places.append(
                    {
                        0: (keys[0, y, x, k], None),
                        1: (keys[2, y, x, k], onward_x),
                        2: (keys[4, y, x, k], onward_y),
                        3: (keys[6, y, x, k], keys[5, y, x, k + 1] if k < BZ - 1 else None),
                    }
                )
            terms(line * BZ + z, places, (0, 2))

    @pl.loop(0, BY)
    def _(y):
        for z in range(0, BZ, 2):
            n = y * BZ + z
            terms(cells_xm + n, [{1: (None, keys[1, y, 0, z + k])} for k in range(2)], (0, 1))

    @pl.loop(0, BX)
    def _(x):
        for z in range(0, BZ, 2):
            places = [{2: (None, keys[3, 0, x, z + k])} for k in range(2)]
            terms(cells_ym + x * BZ + z, places, (1, 2))

    @pl.loop(0, LINES // 2)
    def _(half):
        line = half * 2
        places = [{3: (None, keys[5, line % BY + k, line // BY, 0])} for k in range(2)]
        terms(cells_zm + half * 2, places, (1, 2))

    depth = send.shape[0]

    @pl.loop(0, depth)
    def _(c):
        tally[c] = 0

    @pl.loop(0, AGG_DEV)
    def _(r):
        low, low_half = lane_low((64, 128)), lane_low((32, 128))

        for s in range(0, SLOTS, 2):
            first = acc_b[r * SLOTS + s]
            second = acc_b[r * SLOTS + s + 1] if s + 1 < SLOTS else first
            pair = jnp.where(low, first, second)
            pair += pltpu.roll(jnp.where(low, second, first), 64, axis=1)
            flipped = pair.T
            for k in range(min(2, SLOTS - s)):
                acc_f[r * SLOTS + s + k, :, 0:64] += flipped[k * 64 : k * 64 + 64]
        for s in range(SLOTS):
            total = acc_f.at[r * SLOTS + s]
            even = total[pl.ds(0, 32, stride=2), :]
            odd = total[pl.ds(1, 32, stride=2), :]
            row = jnp.where(low_half, even, odd)
            row += pltpu.roll(jnp.where(low_half, odd, even), 64, axis=1)
            rows[pl.ds(pl.multiple_of(r * ROW + s * 32, 32), 32), :] = row.astype(BF16)
        c = owner[r]
        place = tally[c]
        tally[c] = place + 1
        pltpu.make_async_copy(
            rows.at[pl.ds(pl.multiple_of(r * ROW, 32), ROW)],
            send.at[c, pl.ds(pl.multiple_of(place * ROW, 32), ROW)],
            sems.at[r],
        ).start()

    @pl.loop(0, depth)
    def _(c):
        counts[c] = jnp.full((16, 128), tally[c], jnp.int32).astype(F32).astype(BF16)

    told = pltpu.make_async_copy(counts, send.at[:, pl.ds(PLACES * ROW, 16)], count_sem)
    told.start()
    told.wait()

    @pl.loop(0, AGG_DEV)
    def _(r):
        pltpu.make_async_copy(rows.at[pl.ds(0, ROW)], send.at[0, pl.ds(0, ROW)], sems.at[r]).wait()


def coarse_rows(aggregate, slot, owner, arrays, depth):
    smem = pl.BlockSpec(memory_space=pltpu.SMEM)
    vmem = pl.BlockSpec(memory_space=pltpu.VMEM)
    any_space = pl.BlockSpec(memory_space=pl.ANY)
    beyond = BY + BX + LINES // 8
    return pl.pallas_call(
        compute_kernel,
        out_shape=jax.ShapeDtypeStruct((depth, PACK, 128), BF16),
        in_specs=[vmem, vmem, smem] + [vmem] * 9 + [any_space] * 2 + [vmem] * 6,
        out_specs=any_space,
        scratch_shapes=[
            pltpu.SMEM((SLOTS, BY, BX, BZ), jnp.int32),
            pltpu.VMEM((SLOTS, BY, BX, BZ), jnp.int32),
            pltpu.SemaphoreType.DMA,
            pltpu.SemaphoreType.DMA((BX, 2)),
            pltpu.VMEM(((BY + BX) * 256, 128), BF16),
            pltpu.VMEM((beyond * 512, 128), BF16),
            pltpu.VMEM(((LINES + beyond) * 512, 128), BF16),
            pltpu.VMEM(((LINES + beyond) * 512, 256), BF16),
            pltpu.VMEM((2, 8 * STEP, 128), F32),
            pltpu.VMEM((2, 8 * STEP_TWICE, 128), F32),
            pltpu.VMEM((2, 8 * STEP_TWICE, 128), F32),
            pltpu.VMEM((KEYS + 1, 64, 128), F32),
            pltpu.VMEM((KEYS + 1, 64, 128), F32),
            pltpu.VMEM((AGG_DEV * ROW, 128), BF16),
            pltpu.VMEM((depth, 16, 128), BF16),
            pltpu.SMEM((depth,), jnp.int32),
            pltpu.SemaphoreType.DMA((AGG_DEV,)),
            pltpu.SemaphoreType.DMA,
        ],
        compiler_params=pltpu.CompilerParams(vmem_limit_bytes=63 << 20),
        name="coarse_rows",
    )(aggregate, slot, owner, *arrays)


GROUP, ROW_STEP = 8, ROW + 4


def place_kernel(taken, out, told, counts, tally, source, held, work, shaped, sems, row_sems, out_sems):
    depth, count = taken.shape[0], out.shape[1]
    load = pltpu.make_async_copy(taken.at[:, pl.ds(PLACES * ROW, 16)], told, sems.at[0])
    load.start()

    @pl.loop(0, count + PLACES)
    def _(t):
        source[t] = 0

    load.wait()
    for c in range(depth):
        counts[c : c + 1, :] = told[c, 0:1, :].astype(F32).astype(jnp.int32)
    move = pltpu.make_async_copy(counts, tally, sems.at[1])
    move.start()
    move.wait()

    def order(c, total):
        for k in range(PLACES):
            source[total + k] = c * PLACES + k
        return total + tally[c, 0]

    total = lax.fori_loop(0, depth, order, 0)

    def row_copy(t):
        at = source[t]
        place = pl.multiple_of(lax.rem(at, PLACES) * ROW, 32)
        return pltpu.make_async_copy(taken.at[at // PLACES, pl.ds(place, ROW)], held.at[t], row_sems.at[t])

    @pl.loop(0, count)
    def _(t):
        @pl.when(t >= total)
        def _():
            source[t] = 0

        row_copy(t).start()

    def out_copy(group):
        rows = pl.ds(pl.multiple_of(group * GROUP, GROUP), GROUP)
        return pltpu.make_async_copy(shaped.at[group], out.at[:, rows, :], out_sems.at[group])

    @pl.loop(0, count // GROUP)
    def _(group):
        for k in range(GROUP):
            t = group * GROUP + k
            row_copy(t).wait()
            row = held[t].astype(F32)
            work[k * ROW_STEP : k * ROW_STEP + ROW, :] = jnp.where(t < total, row, jnp.zeros_like(row))
        for s in range(SLOTS):
            for tile in range(32):
                piece = work[pl.ds(s * 32 + tile, GROUP, stride=ROW_STEP), :]
                shaped[group, s, :, tile * 128 : tile * 128 + 128] = piece.astype(BF16)
        out_copy(group).start()

    @pl.loop(0, count // GROUP)
    def _(group):
        out_copy(group).wait()


def place_rows(taken):
    depth = taken.shape[0]
    count = depth * PLACES
    any_space = pl.BlockSpec(memory_space=pl.ANY)
    return pl.pallas_call(
        place_kernel,
        out_shape=jax.ShapeDtypeStruct((SLOTS, count, NODES * NODES), BF16),
        in_specs=[any_space],
        out_specs=any_space,
        scratch_shapes=[
            pltpu.VMEM((depth, 16, 128), BF16),
            pltpu.VMEM((depth, 128), jnp.int32),
            pltpu.SMEM((depth, 128), jnp.int32),
            pltpu.SMEM((count + PLACES,), jnp.int32),
            pltpu.VMEM((count, ROW, 128), BF16),
            pltpu.VMEM((GROUP * ROW_STEP, 128), F32),
            pltpu.VMEM((count // GROUP, SLOTS, GROUP, NODES * NODES), BF16),
            pltpu.SemaphoreType.DMA((2,)),
            pltpu.SemaphoreType.DMA((count,)),
            pltpu.SemaphoreType.DMA((count // GROUP,)),
        ],
        compiler_params=pltpu.CompilerParams(vmem_limit_bytes=63 << 20),
        name="place_rows",
    )(taken)


def shards(a_diag, a_face, prolong, aggregate, pair_slot, row_owner):
    block = a_diag.shape[-1]
    depth = lax.axis_size("gz")
    holding = PLACES * depth

    arrays = inner(prolong, a_face, a_diag)
    send = coarse_rows(
        aggregate.transpose(1, 0, 2), pair_slot.transpose(0, 2, 1, 3), row_owner, arrays, depth
    )
    taken = lax.all_to_all(send, "gz", 0, 0, tiled=True)
    coarse = place_rows(taken).transpose(1, 0, 2)
    return coarse.reshape(1, 1, 1, holding, SLOTS, block)


def solution(mesh):
    return jax.shard_map(
        shards,
        mesh=mesh,
        in_specs=(
            P("gx", "gy", "gz", None),
            P(None, "gx", "gy", "gz", None),
            P("gx", "gy", "gz", None),
            P("gx", "gy", "gz"),
            P(None, "gx", "gy", "gz"),
            P(("gx", "gy", "gz")),
        ),
        out_specs=P("gx", "gy", "gz", None, None, None),
        check_vma=False,
    )
```

```python
import jax
import jax.numpy as jnp
from jax import lax
from jax.experimental import pallas as pl
from jax.experimental.pallas import tpu as pltpu
from jax.sharding import PartitionSpec as P

NODES = 64
SLOTS = 7
AGG_DEV = 24
BX, BY, BZ = 4, 6, 8
LINES = BX * BY
PLACES = 2
ROW = SLOTS * NODES * NODES // 128
PACK = PLACES * ROW
KEYS = AGG_DEV * SLOTS
STEP, STEP_TWICE = 36, 68
F32 = jnp.float32
BF16 = jnp.bfloat16


def lane_low(shape):
    return lax.broadcasted_iota(jnp.int32, shape, 1) < 64


def spread(line, scratch):
    values = line.astype(F32)
    for tile in range(32):
        scratch[pl.ds(tile, 8, stride=STEP), :] = values[:, tile * 128 : tile * 128 + 128]


def spread_twice(line, natural, by_parity):
    values = line.astype(F32)
    low = lane_low((8, 128))
    for tile in range(32):
        here = values[:, tile * 128 : tile * 128 + 128]
        swapped = pltpu.roll(here, 64, axis=1)
        even = jnp.where(low, here, swapped)
        odd = jnp.where(low, swapped, here)
        if natural is not None:
            natural[pl.ds(2 * tile, 8, stride=STEP_TWICE), :] = even
            natural[pl.ds(2 * tile + 1, 8, stride=STEP_TWICE), :] = odd
        if by_parity is not None:
            by_parity[pl.ds(tile, 8, stride=STEP_TWICE), :] = even
            by_parity[pl.ds(32 + tile, 8, stride=STEP_TWICE), :] = odd


MESH = pl.DeviceIdType.MESH


def couples(right, cell, stride, couple, blocks):
    low = lane_low((64, 128))
    zero = jnp.zeros((64, 128), BF16)
    wide = jnp.zeros((128, 128), BF16)
    columns = []
    for k in range(2):
        block = right[pl.ds(pl.multiple_of((cell + k * stride) * 64, 64), 64), :]
        corner = jnp.concatenate([jnp.where(low, block, zero), jnp.where(low, zero, block)], axis=0)
        columns.append(jnp.concatenate([corner, wide] if k == 0 else [wide, corner], axis=0))
    weight = jnp.concatenate(columns, axis=1)
    stack = [
        jnp.concatenate([ref[pl.ds(pl.multiple_of(at, 32), 32), :] for at in ats], axis=1)
        for _, ref, ats, _ in blocks
    ]
    stack = jnp.concatenate(stack, axis=0) if len(stack) > 1 else stack[0]
    both = jnp.dot(stack, weight, preferred_element_type=F32)
    for number, (f, _, _, cells) in enumerate(blocks):
        for k in range(2):
            part = both[number * 32 : number * 32 + 32, k * 128 : k * 128 + 128]
            turned = pltpu.roll(part, 64, axis=1)
            side = f % 2 * 64
            for p in range(2):
                value = (part if p == f % 2 else turned)[:, side : side + 64]
                at = pl.multiple_of(cells[k] * 64 + p * 32, 32)
                couple[pl.ds(at, 32), f * 64 : f * 64 + 64] = value.astype(BF16)


def store_spread(line, dest, base, work):
    spread(line, work)
    for z in range(8):
        at = pl.multiple_of(base + z * 32, 32)
        dest[pl.ds(at, 32), :] = work[z * STEP : z * STEP + 32, :].astype(BF16)


def store_right(right, base, work):
    for z in range(8):
        at = pl.multiple_of(base * 512 + z * 64, 64)
        right[pl.ds(at, 64), :] = work[z * STEP_TWICE : z * STEP_TWICE + 64, :].astype(BF16)


def store_left(left, base, work):
    low = lane_low((64, 128))
    zero = jnp.zeros((64, 128), F32)
    for pair in range(4):
        first, second = (work[z * STEP_TWICE : z * STEP_TWICE + 64, :] for z in (2 * pair, 2 * pair + 1))
        block = jnp.concatenate([jnp.where(low, first, zero), jnp.where(low, zero, second)], axis=0)
        at = pl.multiple_of(base * 512 + pair * 128, 128)
        left[pl.ds(at, 128), :] = block.astype(BF16).T


CELLS = LINES * BZ


def inner_kernel(
    prolong, a_face, a_diag,
    m_x, m_y, m_z, p_xp, p_yp, p_zp,
    couple_out, left_out, right_x, right_y, right_z, face_x, face_y, face_z,
    in_p, in_d, in_f, zero, zero_m, out_mx, out_my, out_mz, out_az, out_p_first,
    ra_d, ra_x, ra_y, ra_z, right, first_z, left, couple, work_a, work_b, work_c,
    load_sems, send_sems, recv_sems, zero_sems, out_sems,
):
    depth = lax.axis_size("gz")
    gx, gy, gz = (lax.axis_index(axis) for axis in ("gx", "gy", "gz"))
    next_z, previous_z = lax.rem(gz + 1, depth), lax.rem(gz + depth - 1, depth)
    barrier = pltpu.get_barrier_semaphore()
    for target in ({"gx": 1 - gx}, {"gy": 1 - gy}, {"gz": next_z}, {"gz": previous_z}):
        pl.semaphore_signal(barrier, inc=1, device_id=target, device_id_type=MESH)
    last_x, inner_x = pl.ds(BX - 1, 1), pl.ds(0, BX - 1)
    load_parts = (
        (prolong, in_p),
        (a_face.at[0, last_x], in_f.at[0, last_x]),
        (a_face.at[1], in_f.at[1]),
        (a_face.at[2], in_f.at[2]),
        (a_diag, in_d),
        (a_face.at[0, inner_x], in_f.at[0, inner_x]),
    )
    loads = [pltpu.make_async_copy(*part, load_sems.at[k]) for k, part in enumerate(load_parts)]
    for load in loads:
        load.start()
    zero[...] = jnp.zeros_like(zero)
    zero_m[...] = jnp.zeros_like(zero_m)
    pl.semaphore_wait(barrier, 4)

    def exchange(number, source, dest, target, sends, receives, blank):
        copy = pltpu.make_async_remote_copy(
            source, dest, send_sems.at[number], recv_sems.at[number], device_id=target, device_id_type=MESH
        )
        fill = pltpu.make_async_copy(blank, dest, zero_sems.at[number])

        @pl.when(sends)
        def _():
            copy.start()

        @pl.when(jnp.logical_not(receives))
        def _():
            fill.start()

        def finish():
            @pl.when(sends)
            def _():
                copy.wait_send()

            @pl.when(receives)
            def _():
                copy.wait_recv()

            @pl.when(jnp.logical_not(receives))
            def _():
                fill.wait()

        return finish

    def to_line(axis, step):
        here, count = lax.axis_index(axis), lax.axis_size(axis)
        return {axis: lax.rem(here + (step + count), count)}

    def has_line(axis, step):
        here, count = lax.axis_index(axis), lax.axis_size(axis)
        return here > 0 if step < 0 else here < count - 1

    def pass_up(number, axis, source, dest, blank):
        return exchange(number, source, dest, to_line(axis, 1), has_line(axis, 1), has_line(axis, -1), blank)

    def pass_down(number, axis, source, dest, blank):
        return exchange(number, source, dest, to_line(axis, -1), has_line(axis, -1), has_line(axis, 1), blank)

    ends = [
        pass_down(0, "gy", prolong.at[:, 0], p_yp, zero.at[pl.ds(0, BX)]),
        pass_down(1, "gx", prolong.at[0], p_xp, zero),
    ]
    loads[0].wait()

    @pl.loop(0, LINES // 2)
    def _(half):
        low = lane_low((32, 128))
        for k in range(2):
            line = half * 2 + k
            x, y = line // BY, line % BY
            at = pl.ds(pl.multiple_of(line * 32, 32), 32)
            natural, by_parity = work_b.at[k], work_c.at[k]
            spread_twice(in_p[x, y], natural, by_parity)
            even, odd = by_parity[0:32, :], by_parity[32:64, :]
            out_p_first[at, :] = jnp.where(low, even, odd).astype(BF16)
            ra_z[pl.ds(pl.multiple_of(line * 288, 32), 32), :] = jnp.zeros((32, 128), BF16)
            store_right(right, line, natural)
            first_z[pl.ds(pl.multiple_of(line * 64, 64), 64), :] = natural[0:64, :].astype(BF16)
            store_left(left, line, by_parity)

    ends.append(pass_down(2, "gz", out_p_first, p_zp, zero_m.at[pl.ds(0, LINES * 32)]))
    loads[1].wait()
    loads[2].wait()
    loads[3].wait()

    def outgoing(work, pair, line):
        blocks = []
        for z in (2 * pair, 2 * pair + 1):
            block = work[z * STEP : z * STEP + 32, :]
            blocks += [block, pltpu.roll(block, 64, axis=1)]
        block = jnp.concatenate(blocks, axis=0).astype(BF16)
        at = pl.multiple_of(line * 512 + pair * 128, 128)
        return jnp.dot(left[pl.ds(at, 128), :], block, preferred_element_type=F32)

    def side_by_side(first, second):
        return jnp.where(lane_low((64, 128)), first, pltpu.roll(second, 64, axis=1)).astype(BF16)

    for f, count, out, line_of in (
        (0, BY, out_mx, lambda k: (BX - 1) * BY + k),
        (1, BX, out_my, lambda k: k * BY + BY - 1),
    ):

        @pl.loop(0, count // 2)
        def _(half):
            for k in range(2):
                row = half * 2 + k
                line = line_of(row)
                work = work_a.at[k]
                store_spread(in_f[f, line // BY, line % BY], (ra_x, ra_y)[f], line * 256, work)
                for pair in range(4):
                    both = outgoing(work, pair, line)
                    at = pl.multiple_of(row * 256 + pair * 64, 64)
                    out[pl.ds(at, 64), :] = side_by_side(both[0:64], both[64:128])

    @pl.loop(0, LINES // 2)
    def _(half):
        last = []
        for k in range(2):
            line = half * 2 + k
            work = work_a.at[k]
            store_spread(in_f[2, line // BY, line % BY], ra_z, line * 288 + 32, work)
            at = pl.ds(pl.multiple_of(line * 32, 32), 32)
            out_az[at, :] = work[(BZ - 1) * STEP : (BZ - 1) * STEP + 32, :].astype(BF16)
            last.append(outgoing(work, BZ // 2 - 1, line)[64:128])
        out_mz[pl.ds(pl.multiple_of(half * 64, 64), 64), :] = side_by_side(*last)

    for number, axis, source, dest in ((3, "gy", out_my, m_y), (4, "gz", out_mz, m_z), (5, "gx", out_mx, m_x)):
        ends.append(pass_up(number, axis, source, dest, zero_m.at[pl.ds(0, source.shape[0])]))
    loads[4].wait()
    loads[5].wait()

    @pl.loop(0, LINES // 2)
    def _(half):
        for k in range(2):
            line = half * 2 + k
            store_spread(in_d[line // BY, line % BY], ra_d, line * 256, work_a.at[k])

    @pl.loop(0, (LINES - BY) // 2)
    def _(half):
        for k in range(2):
            line = half * 2 + k
            store_spread(in_f[0, line // BY, line % BY], ra_x, line * 256, work_a.at[k])

    @pl.loop(0, BX)
    def _(x):
        for y in range(BY - 1):
            store_spread(in_f[1, x, y], ra_y, (x * BY + y) * 256, work_a.at[y % 3])

    moves = []

    def put(source, dest):
        copy = pltpu.make_async_copy(source, dest, out_sems.at[len(moves)])
        copy.start()
        moves.append(copy)

    put(left, left_out)
    put(right.at[pl.ds(0, BY * 512)], right_x)
    put(first_z, right_z)
    put(ra_x.at[pl.ds((LINES - BY) * 256, BY * 256)], face_x)
    put(out_az, face_z)
    for x in range(BX):
        put(right.at[pl.ds(x * BY * 512, 512)], right_y.at[pl.ds(x * 512, 512)])
        put(ra_y.at[pl.ds((x * BY + BY - 1) * 256, 256)], face_y.at[pl.ds(x * 256, 256)])

    for x in range(BX):

        @pl.loop(0, BY)
        def _(y):
            line = x * BY + y
            from_y = jnp.where(y > 0, line - 1, line)
            into_y = jnp.where(y > 0, (line - 1) * BZ, CELLS)
            for z in range(0, BZ, 2):
                n = line * BZ + z
                both = range(2)
                blocks = [
                    (0, ra_d, [(n + k) * 32 for k in both], [n, n + 1]),
                    (2, ra_y, [from_y * 256 + (z + k) * 32 for k in both], [into_y + z, into_y + z + 1]),
                    (3, ra_z, [line * 288 + (z + k) * 32 for k in both], [CELLS if z == 0 else n - 1, n]),
                ]
                if x > 0:
                    e = n - BY * BZ
                    blocks.append((1, ra_x, [(e + k) * 32 for k in both], [e, e + 1]))
                couples(right, n, 1, couple, blocks)

        if x > 0:
            rows = pl.ds((x - 1) * BY * BZ * 64, BY * BZ * 64)
            put(couple.at[rows], couple_out.at[rows])
    rows = pl.ds((BX - 1) * BY * BZ * 64, BY * BZ * 64)
    put(couple.at[rows], couple_out.at[rows])
    for finish in ends:
        finish()
    for copy in moves:
        copy.wait()


def inner(prolong, a_face, a_diag):
    any_space = pl.BlockSpec(memory_space=pl.ANY)
    x_face, y_face, z_face = (BY, BZ, NODES * NODES), (BX, BZ, NODES * NODES), (LINES * 32, 128)
    shapes = (
        (BY * 256, 128), (BX * 256, 128), (LINES * 32, 128), x_face, y_face, z_face,
        (CELLS * 64, 256), (CELLS * 64, 128),
        (BY * 512, 128), (BX * 512, 128), (LINES * 64, 128),
        (BY * 256, 128), (BX * 256, 128), z_face,
    )
    return pl.pallas_call(
        inner_kernel,
        out_shape=[jax.ShapeDtypeStruct(shape, BF16) for shape in shapes],
        in_specs=[any_space] * 3,
        out_specs=[any_space] * len(shapes),
        scratch_shapes=[
            pltpu.VMEM(prolong.shape, BF16),
            pltpu.VMEM(a_diag.shape, BF16),
            pltpu.VMEM(a_face.shape, BF16),
            pltpu.VMEM(x_face, BF16),
            pltpu.VMEM((BY * 256, 128), BF16),
            pltpu.VMEM((BY * 256, 128), BF16),
            pltpu.VMEM((BX * 256, 128), BF16),
            pltpu.VMEM((LINES * 32, 128), BF16),
            pltpu.VMEM(z_face, BF16),
            pltpu.VMEM(z_face, BF16),
            pltpu.VMEM((LINES * 256, 128), BF16),
            pltpu.VMEM((LINES * 256, 128), BF16),
            pltpu.VMEM((LINES * 256, 128), BF16),
            pltpu.VMEM((LINES * 288, 128), BF16),
            pltpu.VMEM((CELLS * 64, 128), BF16),
            pltpu.VMEM((LINES * 64, 128), BF16),
            pltpu.VMEM((CELLS * 64, 128), BF16),
            pltpu.VMEM(((CELLS + BZ) * 64, 256), BF16),
            pltpu.VMEM((3, 8 * STEP, 128), F32),
            pltpu.VMEM((2, 8 * STEP_TWICE, 128), F32),
            pltpu.VMEM((2, 8 * STEP_TWICE, 128), F32),
            pltpu.SemaphoreType.DMA((6,)),
            pltpu.SemaphoreType.DMA((6,)),
            pltpu.SemaphoreType.DMA((6,)),
            pltpu.SemaphoreType.DMA((6,)),
            pltpu.SemaphoreType.DMA((5 + 3 * BX,)),
        ],
        compiler_params=pltpu.CompilerParams(collective_id=0, has_side_effects=True, vmem_limit_bytes=63 << 20),
        name="inner",
    )(prolong, a_face, a_diag)


def compute_kernel(
    aggregate, slot, owner,
    m_x, m_y, m_z, p_xp, p_yp, p_zp,
    couple_in, left_in, right_x, right_y, right_z, face_x, face_y, face_z,
    send, keys, key_work, key_sem, in_sems, right, left, couple, work_b,
    acc_f, acc_b, rows, absent, tally, sems, absent_sems,
):
    plane = BY * BZ * 64
    brought = []
    for x in range(BX):
        at = pl.ds(x * plane, plane)
        for k, (source, dest) in enumerate(((couple_in, couple), (left_in, left))):
            copy = pltpu.make_async_copy(source.at[at], dest.at[at], in_sems.at[x, k])
            copy.start()
            brought.append(copy)

    absent[...] = jnp.full(absent.shape, jnp.nan, BF16)
    marks = []
    for k in range(PLACES):
        mark = pltpu.make_async_copy(absent, send.at[:, pl.ds(k * ROW, 16)], absent_sems.at[k])
        mark.start()
        marks.append(mark)

    key_work[...] = aggregate[...][None] * SLOTS + slot[...]
    told_keys = pltpu.make_async_copy(key_work, keys, key_sem)
    told_keys.start()
    acc_f[...] = jnp.zeros_like(acc_f)
    acc_b[...] = jnp.zeros_like(acc_b)

    right_xp, right_yp, right_zp = 0, BY, BY + BX

    for count, after, base in ((BY, p_xp, right_xp), (BX, p_yp, right_yp)):

        @pl.loop(0, count // 2)
        def _(half):
            for k in range(2):
                line = half * 2 + k
                spread_twice(after[line], work_b.at[k], None)
                store_right(right, base + line, work_b.at[k])

    @pl.loop(0, LINES // 2)
    def _(half):
        low = lane_low((32, 128))
        for k in range(2):
            line = half * 2 + k
            here = p_zp[pl.ds(pl.multiple_of(line * 32, 32), 32), :].astype(F32)
            turned = pltpu.roll(here, 64, axis=1)
            work = work_b.at[k]
            work[pl.ds(0, 32, stride=2), :] = jnp.where(low, here, turned)
            work[pl.ds(1, 32, stride=2), :] = jnp.where(low, turned, here)
            at = pl.multiple_of((right_zp * 8 + line) * 64, 64)
            right[pl.ds(at, 64), :] = work[0:64, :].astype(BF16)

    told_keys.wait()

    def add(ref, at, low_side, value):
        low = lane_low((64, 128))
        zero = jnp.zeros((64, 128), F32)
        ref[at] += jnp.where(low, value, zero) if low_side else jnp.where(low, zero, value)

    def rim_terms(weights, cell, m, at, places):
        low = lane_low((64, 128))
        zero = jnp.zeros((64, 128), BF16)
        first, second = (weights[pl.ds(pl.multiple_of((cell + k) * 64, 64), 64), :] for k in range(2))
        weight = jnp.concatenate([jnp.where(low, first, zero), jnp.where(low, zero, second)], axis=0)
        out = jnp.dot(m[pl.ds(pl.multiple_of(at, 64), 64), :], weight, preferred_element_type=F32)
        for k in range(2):
            add(acc_b, places[k], k == 0, out)

    @pl.loop(0, BY)
    def _(y):
        for z in range(0, BZ, 2):
            rim_terms(right_x, y * BZ + z, m_x, y * 256 + z * 32, [keys[1, y, 0, z + k] for k in range(2)])

    @pl.loop(0, BX)
    def _(x):
        for z in range(0, BZ, 2):
            rim_terms(right_y, x * BZ + z, m_y, x * 256 + z * 32, [keys[3, 0, x, z + k] for k in range(2)])

    @pl.loop(0, LINES // 2)
    def _(half):
        line = half * 2
        places = [keys[5, line % BY + k, line // BY, 0] for k in range(2)]
        rim_terms(right_z, line, m_z, half * 64, places)

    for copy in brought:
        copy.wait()

    @pl.loop(0, BY)
    def _(y):
        for z in range(0, BZ, 2):
            e = ((BX - 1) * BY + y) * BZ + z
            at = y * 256 + z * 32
            couples(right, (right_xp + y) * 8 + z, 1, couple, [(1, face_x, [at, at + 32], [e, e + 1])])

    @pl.loop(0, BX)
    def _(x):
        for z in range(0, BZ, 2):
            e = (x * BY + BY - 1) * BZ + z
            at = x * 256 + z * 32
            couples(right, (right_yp + x) * 8 + z, 1, couple, [(2, face_y, [at, at + 32], [e, e + 1])])

    @pl.loop(0, LINES // 2)
    def _(half):
        line = half * 2
        e = line * BZ + BZ - 1
        couples(right, right_zp * 8 + line, 1, couple, [(3, face_z, [line * 32, line * 32 + 32], [e, e + BZ])])

    def terms(cell, places):
        at = pl.multiple_of(cell * 64, 128)
        out = jnp.dot(left[pl.ds(at, 128), :], couple[pl.ds(at, 128), :], preferred_element_type=F32)
        for k in range(2):
            for f, (key_f, key_b) in places[k].items():
                tile = f // 2
                term = out[k * 64 : k * 64 + 64, tile * 128 : tile * 128 + 128]
                if key_f is not None:
                    add(acc_f, key_f, f % 2 == 0, term)
                if key_b is not None:
                    add(acc_b, key_b, f % 2 == 0, term)


    @pl.loop(0, LINES)
    def _(line):
        x, y = line // BY, line % BY
        next_x, next_y = jnp.minimum(x + 1, BX - 1), jnp.minimum(y + 1, BY - 1)
        for z in range(0, BZ, 2):
            places = []
            for k in range(z, z + 2):
                onward_x = jnp.where(x < BX - 1, keys[1, y, next_x, k], KEYS)
                onward_y = jnp.where(y < BY - 1, keys[3, next_y, x, k], KEYS)
                places.append(
                    {
                        0: (keys[0, y, x, k], None),
                        1: (keys[2, y, x, k], onward_x),
                        2: (keys[4, y, x, k], onward_y),
                        3: (keys[6, y, x, k], keys[5, y, x, k + 1] if k < BZ - 1 else None),
                    }
                )
            terms(line * BZ + z, places)

    depth = send.shape[0]
    for copy in marks:
        copy.wait()

    @pl.loop(0, depth)
    def _(c):
        tally[c] = 0

    @pl.loop(0, AGG_DEV)
    def _(r):
        low, low_half = lane_low((64, 128)), lane_low((32, 128))

        for s in range(0, SLOTS, 2):
            first = acc_b[r * SLOTS + s]
            second = acc_b[r * SLOTS + s + 1] if s + 1 < SLOTS else first
            pair = jnp.where(low, first, second)
            pair += pltpu.roll(jnp.where(low, second, first), 64, axis=1)
            flipped = pair.T
            for k in range(min(2, SLOTS - s)):
                acc_f[r * SLOTS + s + k, :, 0:64] += flipped[k * 64 : k * 64 + 64]
        for s in range(SLOTS):
            total = acc_f.at[r * SLOTS + s]
            even = total[pl.ds(0, 32, stride=2), :]
            odd = total[pl.ds(1, 32, stride=2), :]
            row = jnp.where(low_half, even, odd)
            row += pltpu.roll(jnp.where(low_half, odd, even), 64, axis=1)
            rows[pl.ds(pl.multiple_of(r * ROW + s * 32, 32), 32), :] = row.astype(BF16)
        c = owner[r]
        place = tally[c]
        tally[c] = place + 1
        pltpu.make_async_copy(
            rows.at[pl.ds(pl.multiple_of(r * ROW, 32), ROW)],
            send.at[c, pl.ds(pl.multiple_of(place * ROW, 32), ROW)],
            sems.at[r],
        ).start()

    @pl.loop(0, AGG_DEV)
    def _(r):
        pltpu.make_async_copy(rows.at[pl.ds(0, ROW)], send.at[0, pl.ds(0, ROW)], sems.at[r]).wait()


def coarse_rows(aggregate, slot, owner, arrays, depth):
    smem = pl.BlockSpec(memory_space=pltpu.SMEM)
    vmem = pl.BlockSpec(memory_space=pltpu.VMEM)
    any_space = pl.BlockSpec(memory_space=pl.ANY)
    beyond = BY + BX + LINES // 8
    return pl.pallas_call(
        compute_kernel,
        out_shape=jax.ShapeDtypeStruct((depth, PACK, 128), BF16),
        in_specs=[vmem, vmem, smem] + [vmem] * 6 + [any_space] * 2 + [vmem] * 6,
        out_specs=any_space,
        scratch_shapes=[
            pltpu.SMEM((SLOTS, BY, BX, BZ), jnp.int32),
            pltpu.VMEM((SLOTS, BY, BX, BZ), jnp.int32),
            pltpu.SemaphoreType.DMA,
            pltpu.SemaphoreType.DMA((BX, 2)),
            pltpu.VMEM((beyond * 512, 128), BF16),
            pltpu.VMEM((CELLS * 64, 128), BF16),
            pltpu.VMEM((CELLS * 64, 256), BF16),
            pltpu.VMEM((2, 8 * STEP_TWICE, 128), F32),
            pltpu.VMEM((KEYS + 1, 64, 128), F32),
            pltpu.VMEM((KEYS + 1, 64, 128), F32),
            pltpu.VMEM((AGG_DEV * ROW, 128), BF16),
            pltpu.VMEM((depth, 16, 128), BF16),
            pltpu.SMEM((depth,), jnp.int32),
            pltpu.SemaphoreType.DMA((AGG_DEV,)),
            pltpu.SemaphoreType.DMA((PLACES,)),
        ],
        compiler_params=pltpu.CompilerParams(vmem_limit_bytes=63 << 20),
        name="coarse_rows",
    )(aggregate, slot, owner, *arrays)


GROUP, ROW_STEP = 8, ROW + 4


def place_kernel(taken, out, told, counts, tally, source, held, work, shaped, sems, row_sems, out_sems):
    depth, count = taken.shape[0], out.shape[1]
    loads = [
        pltpu.make_async_copy(taken.at[:, pl.ds(k * ROW, 16)], told.at[k], sems.at[k]) for k in range(PLACES)
    ]
    for load in loads:
        load.start()

    @pl.loop(0, count + PLACES)
    def _(t):
        source[t] = 0

    for load in loads:
        load.wait()
    for c in range(depth):
        here = [told[k, c, 0:1, :].astype(F32) for k in range(PLACES)]
        counts[c : c + 1, :] = sum((value == value).astype(jnp.int32) for value in here)
    move = pltpu.make_async_copy(counts, tally, sems.at[PLACES])
    move.start()
    move.wait()

    def order(c, total):
        for k in range(PLACES):
            source[total + k] = c * PLACES + k
        return total + tally[c, 0]

    total = lax.fori_loop(0, depth, order, 0)

    def row_copy(t):
        at = source[t]
        place = pl.multiple_of(lax.rem(at, PLACES) * ROW, 32)
        return pltpu.make_async_copy(taken.at[at // PLACES, pl.ds(place, ROW)], held.at[t], row_sems.at[t])

    @pl.loop(0, count)
    def _(t):
        @pl.when(t >= total)
        def _():
            source[t] = 0

        row_copy(t).start()

    def out_copy(group):
        rows = pl.ds(pl.multiple_of(group * GROUP, GROUP), GROUP)
        return pltpu.make_async_copy(shaped.at[group], out.at[:, rows, :], out_sems.at[group])

    @pl.loop(0, count // GROUP)
    def _(group):
        for k in range(GROUP):
            t = group * GROUP + k
            row_copy(t).wait()
            row = held[t].astype(F32)
            work[k * ROW_STEP : k * ROW_STEP + ROW, :] = jnp.where(t < total, row, jnp.zeros_like(row))
        for s in range(SLOTS):
            for tile in range(32):
                piece = work[pl.ds(s * 32 + tile, GROUP, stride=ROW_STEP), :]
                shaped[group, s, :, tile * 128 : tile * 128 + 128] = piece.astype(BF16)
        out_copy(group).start()

    @pl.loop(0, count // GROUP)
    def _(group):
        out_copy(group).wait()


def place_rows(taken):
    depth = taken.shape[0]
    count = depth * PLACES
    any_space = pl.BlockSpec(memory_space=pl.ANY)
    return pl.pallas_call(
        place_kernel,
        out_shape=jax.ShapeDtypeStruct((SLOTS, count, NODES * NODES), BF16),
        in_specs=[any_space],
        out_specs=any_space,
        scratch_shapes=[
            pltpu.VMEM((PLACES, depth, 16, 128), BF16),
            pltpu.VMEM((depth, 128), jnp.int32),
            pltpu.SMEM((depth, 128), jnp.int32),
            pltpu.SMEM((count + PLACES,), jnp.int32),
            pltpu.VMEM((count, ROW, 128), BF16),
            pltpu.VMEM((GROUP * ROW_STEP, 128), F32),
            pltpu.VMEM((count // GROUP, SLOTS, GROUP, NODES * NODES), BF16),
            pltpu.SemaphoreType.DMA((PLACES + 1,)),
            pltpu.SemaphoreType.DMA((count,)),
            pltpu.SemaphoreType.DMA((count // GROUP,)),
        ],
        compiler_params=pltpu.CompilerParams(vmem_limit_bytes=63 << 20),
        name="place_rows",
    )(taken)


def shards(a_diag, a_face, prolong, aggregate, pair_slot, row_owner):
    block = a_diag.shape[-1]
    depth = lax.axis_size("gz")
    holding = PLACES * depth

    arrays = inner(prolong, a_face, a_diag)
    send = coarse_rows(
        aggregate.transpose(1, 0, 2), pair_slot.transpose(0, 2, 1, 3), row_owner, arrays, depth
    )
    taken = lax.all_to_all(send, "gz", 0, 0, tiled=True)
    coarse = place_rows(taken).transpose(1, 0, 2)
    return coarse.reshape(1, 1, 1, holding, SLOTS, block)


def solution(mesh):
    return jax.shard_map(
        shards,
        mesh=mesh,
        in_specs=(
            P("gx", "gy", "gz", None),
            P(None, "gx", "gy", "gz", None),
            P("gx", "gy", "gz", None),
            P("gx", "gy", "gz"),
            P(None, "gx", "gy", "gz"),
            P(("gx", "gy", "gz")),
        ),
        out_specs=P("gx", "gy", "gz", None, None, None),
        check_vma=False,
    )
```

```python
import jax
import jax.numpy as jnp
from jax import lax
from jax.experimental import pallas as pl
from jax.experimental.pallas import tpu as pltpu
from jax.sharding import PartitionSpec as P

NODES = 64
SLOTS = 7
AGG_DEV = 24
BX, BY, BZ = 4, 6, 8
LINES = BX * BY
PLACES = 2
ROW = SLOTS * NODES * NODES // 128
PACK = PLACES * ROW
KEYS = AGG_DEV * SLOTS
STEP, STEP_TWICE = 36, 68
F32 = jnp.float32
BF16 = jnp.bfloat16


def lane_low(shape):
    return lax.broadcasted_iota(jnp.int32, shape, 1) < 64


def spread(line, scratch):
    values = line.astype(F32)
    for tile in range(32):
        scratch[pl.ds(tile, 8, stride=STEP), :] = values[:, tile * 128 : tile * 128 + 128]


def spread_twice(line, natural, by_parity):
    values = line.astype(F32)
    low = lane_low((8, 128))
    for tile in range(32):
        here = values[:, tile * 128 : tile * 128 + 128]
        swapped = pltpu.roll(here, 64, axis=1)
        even = jnp.where(low, here, swapped)
        odd = jnp.where(low, swapped, here)
        if natural is not None:
            natural[pl.ds(2 * tile, 8, stride=STEP_TWICE), :] = even
            natural[pl.ds(2 * tile + 1, 8, stride=STEP_TWICE), :] = odd
        if by_parity is not None:
            by_parity[pl.ds(tile, 8, stride=STEP_TWICE), :] = even
            by_parity[pl.ds(32 + tile, 8, stride=STEP_TWICE), :] = odd


MESH = pl.DeviceIdType.MESH


def couples(right, cell, stride, couple, blocks):
    low = lane_low((64, 128))
    zero = jnp.zeros((64, 128), BF16)
    wide = jnp.zeros((128, 128), BF16)
    columns = []
    for k in range(2):
        block = right[pl.ds(pl.multiple_of((cell + k * stride) * 64, 64), 64), :]
        corner = jnp.concatenate([jnp.where(low, block, zero), jnp.where(low, zero, block)], axis=0)
        columns.append(jnp.concatenate([corner, wide] if k == 0 else [wide, corner], axis=0))
    weight = jnp.concatenate(columns, axis=1)
    stack = [
        jnp.concatenate([ref[pl.ds(pl.multiple_of(at, 32), 32), :] for at in ats], axis=1)
        for _, ref, ats, _ in blocks
    ]
    stack = jnp.concatenate(stack, axis=0) if len(stack) > 1 else stack[0]
    both = jnp.dot(stack, weight, preferred_element_type=F32)
    for number, (f, _, _, cells) in enumerate(blocks):
        for k in range(2):
            part = both[number * 32 : number * 32 + 32, k * 128 : k * 128 + 128]
            turned = pltpu.roll(part, 64, axis=1)
            side = f % 2 * 64
            for p in range(2):
                value = (part if p == f % 2 else turned)[:, side : side + 64]
                at = pl.multiple_of(cells[k] * 64 + p * 32, 32)
                couple[pl.ds(at, 32), f * 64 : f * 64 + 64] = value.astype(BF16)


def store_spread(line, dest, base, work):
    spread(line, work)
    for z in range(8):
        at = pl.multiple_of(base + z * 32, 32)
        dest[pl.ds(at, 32), :] = work[z * STEP : z * STEP + 32, :].astype(BF16)


def store_right(right, base, work):
    for z in range(8):
        at = pl.multiple_of(base * 512 + z * 64, 64)
        right[pl.ds(at, 64), :] = work[z * STEP_TWICE : z * STEP_TWICE + 64, :].astype(BF16)


def store_left(left, base, work):
    low = lane_low((64, 128))
    zero = jnp.zeros((64, 128), F32)
    for pair in range(4):
        first, second = (work[z * STEP_TWICE : z * STEP_TWICE + 64, :] for z in (2 * pair, 2 * pair + 1))
        block = jnp.concatenate([jnp.where(low, first, zero), jnp.where(low, zero, second)], axis=0)
        at = pl.multiple_of(base * 512 + pair * 128, 128)
        left[pl.ds(at, 128), :] = block.astype(BF16).T


CELLS = LINES * BZ


def inner_kernel(
    prolong, a_face, a_diag,
    m_x, m_y, m_z, p_xp, p_yp, p_zp,
    couple_out, left_out, right_x, right_y, right_z, face_x, face_y, face_z,
    in_p, in_d, in_f, zero, zero_m, out_mx, out_my, out_mz, out_az, out_p_first,
    ra_d, ra_x, ra_y, ra_z, right, first_z, left, couple, work_a, work_b, work_c,
    load_sems, send_sems, recv_sems, zero_sems, out_sems,
):
    depth = lax.axis_size("gz")
    gx, gy, gz = (lax.axis_index(axis) for axis in ("gx", "gy", "gz"))
    next_z, previous_z = lax.rem(gz + 1, depth), lax.rem(gz + depth - 1, depth)
    barrier = pltpu.get_barrier_semaphore()
    for target in ({"gx": 1 - gx}, {"gy": 1 - gy}, {"gz": next_z}, {"gz": previous_z}):
        pl.semaphore_signal(barrier, inc=1, device_id=target, device_id_type=MESH)
    last_x, inner_x = pl.ds(BX - 1, 1), pl.ds(0, BX - 1)
    load_parts = (
        (prolong, in_p),
        (a_face.at[0, last_x], in_f.at[0, last_x]),
        (a_face.at[1], in_f.at[1]),
        (a_face.at[2], in_f.at[2]),
        (a_diag, in_d),
        (a_face.at[0, inner_x], in_f.at[0, inner_x]),
    )
    loads = [pltpu.make_async_copy(*part, load_sems.at[k]) for k, part in enumerate(load_parts)]
    for load in loads:
        load.start()
    zero[...] = jnp.zeros_like(zero)
    zero_m[...] = jnp.zeros_like(zero_m)
    pl.semaphore_wait(barrier, 4)

    def exchange(number, source, dest, target, sends, receives, blank):
        copy = pltpu.make_async_remote_copy(
            source, dest, send_sems.at[number], recv_sems.at[number], device_id=target, device_id_type=MESH
        )
        fill = pltpu.make_async_copy(blank, dest, zero_sems.at[number])

        @pl.when(sends)
        def _():
            copy.start()

        @pl.when(jnp.logical_not(receives))
        def _():
            fill.start()

        def finish():
            @pl.when(sends)
            def _():
                copy.wait_send()

            @pl.when(receives)
            def _():
                copy.wait_recv()

            @pl.when(jnp.logical_not(receives))
            def _():
                fill.wait()

        return finish

    def to_line(axis, step):
        here, count = lax.axis_index(axis), lax.axis_size(axis)
        return {axis: lax.rem(here + (step + count), count)}

    def has_line(axis, step):
        here, count = lax.axis_index(axis), lax.axis_size(axis)
        return here > 0 if step < 0 else here < count - 1

    def pass_up(number, axis, source, dest, blank):
        return exchange(number, source, dest, to_line(axis, 1), has_line(axis, 1), has_line(axis, -1), blank)

    def pass_down(number, axis, source, dest, blank):
        return exchange(number, source, dest, to_line(axis, -1), has_line(axis, -1), has_line(axis, 1), blank)

    ends = [
        pass_down(0, "gy", prolong.at[:, 0], p_yp, zero.at[pl.ds(0, BX)]),
        pass_down(1, "gx", prolong.at[0], p_xp, zero),
    ]
    loads[0].wait()

    @pl.loop(0, LINES // 2)
    def _(half):
        low = lane_low((32, 128))
        for k in range(2):
            line = half * 2 + k
            x, y = line // BY, line % BY
            at = pl.ds(pl.multiple_of(line * 32, 32), 32)
            natural, by_parity = work_b.at[k], work_c.at[k]
            spread_twice(in_p[x, y], natural, by_parity)
            even, odd = by_parity[0:32, :], by_parity[32:64, :]
            out_p_first[at, :] = jnp.where(low, even, odd).astype(BF16)
            ra_z[pl.ds(pl.multiple_of(line * 288, 32), 32), :] = jnp.zeros((32, 128), BF16)
            store_right(right, line, natural)
            first_z[pl.ds(pl.multiple_of(line * 64, 64), 64), :] = natural[0:64, :].astype(BF16)
            store_left(left, line, by_parity)

    ends.append(pass_down(2, "gz", out_p_first, p_zp, zero_m.at[pl.ds(0, LINES * 32)]))
    loads[1].wait()
    loads[2].wait()
    loads[3].wait()

    def outgoing(work, pair, line):
        blocks = []
        for z in (2 * pair, 2 * pair + 1):
            block = work[z * STEP : z * STEP + 32, :]
            blocks += [block, pltpu.roll(block, 64, axis=1)]
        block = jnp.concatenate(blocks, axis=0).astype(BF16)
        at = pl.multiple_of(line * 512 + pair * 128, 128)
        return jnp.dot(left[pl.ds(at, 128), :], block, preferred_element_type=F32)

    def side_by_side(first, second):
        return jnp.where(lane_low((64, 128)), first, pltpu.roll(second, 64, axis=1)).astype(BF16)

    for f, count, out, line_of in (
        (0, BY, out_mx, lambda k: (BX - 1) * BY + k),
        (1, BX, out_my, lambda k: k * BY + BY - 1),
    ):

        @pl.loop(0, count // 2)
        def _(half):
            for k in range(2):
                row = half * 2 + k
                line = line_of(row)
                work = work_a.at[k]
                store_spread(in_f[f, line // BY, line % BY], (ra_x, ra_y)[f], line * 256, work)
                for pair in range(4):
                    both = outgoing(work, pair, line)
                    at = pl.multiple_of(row * 256 + pair * 64, 64)
                    out[pl.ds(at, 64), :] = side_by_side(both[0:64], both[64:128])

    @pl.loop(0, LINES // 2)
    def _(half):
        last = []
        for k in range(2):
            line = half * 2 + k
            work = work_a.at[k]
            store_spread(in_f[2, line // BY, line % BY], ra_z, line * 288 + 32, work)
            at = pl.ds(pl.multiple_of(line * 32, 32), 32)
            out_az[at, :] = work[(BZ - 1) * STEP : (BZ - 1) * STEP + 32, :].astype(BF16)
            last.append(outgoing(work, BZ // 2 - 1, line)[64:128])
        out_mz[pl.ds(pl.multiple_of(half * 64, 64), 64), :] = side_by_side(*last)

    for number, axis, source, dest in ((3, "gy", out_my, m_y), (4, "gz", out_mz, m_z), (5, "gx", out_mx, m_x)):
        ends.append(pass_up(number, axis, source, dest, zero_m.at[pl.ds(0, source.shape[0])]))
    loads[4].wait()
    loads[5].wait()

    @pl.loop(0, LINES // 2)
    def _(half):
        for k in range(2):
            line = half * 2 + k
            store_spread(in_d[line // BY, line % BY], ra_d, line * 256, work_a.at[k])

    @pl.loop(0, (LINES - BY) // 2)
    def _(half):
        for k in range(2):
            line = half * 2 + k
            store_spread(in_f[0, line // BY, line % BY], ra_x, line * 256, work_a.at[k])

    @pl.loop(0, BX)
    def _(x):
        for y in range(BY - 1):
            store_spread(in_f[1, x, y], ra_y, (x * BY + y) * 256, work_a.at[y % 3])

    moves = []

    def put(source, dest):
        copy = pltpu.make_async_copy(source, dest, out_sems.at[len(moves)])
        copy.start()
        moves.append(copy)

    put(left, left_out)
    put(right.at[pl.ds(0, BY * 512)], right_x)
    put(first_z, right_z)
    put(ra_x.at[pl.ds((LINES - BY) * 256, BY * 256)], face_x)
    put(out_az, face_z)
    for x in range(BX):
        put(right.at[pl.ds(x * BY * 512, 512)], right_y.at[pl.ds(x * 512, 512)])
        put(ra_y.at[pl.ds((x * BY + BY - 1) * 256, 256)], face_y.at[pl.ds(x * 256, 256)])

    for x in range(BX):

        @pl.loop(0, BY // 2)
        def _(half):
            for y in (half * 2, half * 2 + 1):
                line = x * BY + y
                from_y = jnp.where(y > 0, line - 1, line)
                into_y = jnp.where(y > 0, (line - 1) * BZ, CELLS)
                for z in range(0, BZ, 2):
                    n = line * BZ + z
                    both = range(2)
                    blocks = [
                        (0, ra_d, [(n + k) * 32 for k in both], [n, n + 1]),
                        (2, ra_y, [from_y * 256 + (z + k) * 32 for k in both], [into_y + z, into_y + z + 1]),
                        (3, ra_z, [line * 288 + (z + k) * 32 for k in both], [CELLS if z == 0 else n - 1, n]),
                    ]
                    if x > 0:
                        e = n - BY * BZ
                        blocks.append((1, ra_x, [(e + k) * 32 for k in both], [e, e + 1]))
                    couples(right, n, 1, couple, blocks)

        if x > 0:
            rows = pl.ds((x - 1) * BY * BZ * 64, BY * BZ * 64)
            put(couple.at[rows], couple_out.at[rows])
    rows = pl.ds((BX - 1) * BY * BZ * 64, BY * BZ * 64)
    put(couple.at[rows], couple_out.at[rows])
    for finish in ends:
        finish()
    for copy in moves:
        copy.wait()


def inner(prolong, a_face, a_diag):
    any_space = pl.BlockSpec(memory_space=pl.ANY)
    x_face, y_face, z_face = (BY, BZ, NODES * NODES), (BX, BZ, NODES * NODES), (LINES * 32, 128)
    shapes = (
        (BY * 256, 128), (BX * 256, 128), (LINES * 32, 128), x_face, y_face, z_face,
        (CELLS * 64, 256), (CELLS * 64, 128),
        (BY * 512, 128), (BX * 512, 128), (LINES * 64, 128),
        (BY * 256, 128), (BX * 256, 128), z_face,
    )
    return pl.pallas_call(
        inner_kernel,
        out_shape=[jax.ShapeDtypeStruct(shape, BF16) for shape in shapes],
        in_specs=[any_space] * 3,
        out_specs=[any_space] * len(shapes),
        scratch_shapes=[
            pltpu.VMEM(prolong.shape, BF16),
            pltpu.VMEM(a_diag.shape, BF16),
            pltpu.VMEM(a_face.shape, BF16),
            pltpu.VMEM(x_face, BF16),
            pltpu.VMEM((BY * 256, 128), BF16),
            pltpu.VMEM((BY * 256, 128), BF16),
            pltpu.VMEM((BX * 256, 128), BF16),
            pltpu.VMEM((LINES * 32, 128), BF16),
            pltpu.VMEM(z_face, BF16),
            pltpu.VMEM(z_face, BF16),
            pltpu.VMEM((LINES * 256, 128), BF16),
            pltpu.VMEM((LINES * 256, 128), BF16),
            pltpu.VMEM((LINES * 256, 128), BF16),
            pltpu.VMEM((LINES * 288, 128), BF16),
            pltpu.VMEM((CELLS * 64, 128), BF16),
            pltpu.VMEM((LINES * 64, 128), BF16),
            pltpu.VMEM((CELLS * 64, 128), BF16),
            pltpu.VMEM(((CELLS + BZ) * 64, 256), BF16),
            pltpu.VMEM((3, 8 * STEP, 128), F32),
            pltpu.VMEM((2, 8 * STEP_TWICE, 128), F32),
            pltpu.VMEM((2, 8 * STEP_TWICE, 128), F32),
            pltpu.SemaphoreType.DMA((6,)),
            pltpu.SemaphoreType.DMA((6,)),
            pltpu.SemaphoreType.DMA((6,)),
            pltpu.SemaphoreType.DMA((6,)),
            pltpu.SemaphoreType.DMA((5 + 3 * BX,)),
        ],
        compiler_params=pltpu.CompilerParams(collective_id=0, has_side_effects=True, vmem_limit_bytes=63 << 20),
        name="inner",
    )(prolong, a_face, a_diag)


def compute_kernel(
    aggregate, slot, owner, *refs
):
    arrays, refs = refs[:14], refs[14:]
    small, couple_in, left_in = arrays[:6] + arrays[8:], arrays[6], arrays[7]
    send, held, refs = refs[0], refs[1:13], refs[13:]
    m_x, m_y, m_z, p_xp, p_yp, p_zp, right_x, right_y, right_z, face_x, face_y, face_z = held
    (
    small_sems, keys, key_work, key_sem, in_sems, right, left, couple, work_b,
    f_low, f_high, b_low, b_high, rows, absent, tally, sems, absent_sems,
    ) = refs
    fetched = [pltpu.make_async_copy(*pair, small_sems.at[k]) for k, pair in enumerate(zip(small, held))]
    for copy in fetched:
        copy.start()
    plane = BY * BZ * 64
    brought = []
    for x in range(BX):
        at = pl.ds(x * plane, plane)
        for k, (source, dest) in enumerate(((couple_in, couple), (left_in, left))):
            copy = pltpu.make_async_copy(source.at[at], dest.at[at], in_sems.at[x, k])
            copy.start()
            brought.append(copy)

    absent[...] = jnp.full(absent.shape, jnp.nan, BF16)
    marks = []
    for k in range(PLACES):
        mark = pltpu.make_async_copy(absent, send.at[:, pl.ds(k * ROW, 16)], absent_sems.at[k])
        mark.start()
        marks.append(mark)

    key_work[...] = aggregate[...][None] * SLOTS + slot[...]
    told_keys = pltpu.make_async_copy(key_work, keys, key_sem)
    told_keys.start()
    for ref in (f_low, f_high, b_low, b_high):
        ref[...] = jnp.zeros_like(ref)

    for copy in fetched:
        copy.wait()

    right_xp, right_yp, right_zp = 0, BY, BY + BX

    for count, after, base in ((BY, p_xp, right_xp), (BX, p_yp, right_yp)):

        @pl.loop(0, count // 2)
        def _(half):
            for k in range(2):
                line = half * 2 + k
                spread_twice(after[line], work_b.at[k], None)
                store_right(right, base + line, work_b.at[k])

    @pl.loop(0, LINES // 2)
    def _(half):
        low = lane_low((32, 128))
        for k in range(2):
            line = half * 2 + k
            here = p_zp[pl.ds(pl.multiple_of(line * 32, 32), 32), :].astype(F32)
            turned = pltpu.roll(here, 64, axis=1)
            work = work_b.at[k]
            work[pl.ds(0, 32, stride=2), :] = jnp.where(low, here, turned)
            work[pl.ds(1, 32, stride=2), :] = jnp.where(low, turned, here)
            at = pl.multiple_of((right_zp * 8 + line) * 64, 64)
            right[pl.ds(at, 64), :] = work[0:64, :].astype(BF16)

    told_keys.wait()

    def rim_terms(weights, cell, m, at, places):
        low = lane_low((64, 128))
        zero = jnp.zeros((64, 128), BF16)
        first, second = (weights[pl.ds(pl.multiple_of((cell + k) * 64, 64), 64), :] for k in range(2))
        weight = jnp.concatenate([jnp.where(low, first, zero), jnp.where(low, zero, second)], axis=0)
        out = jnp.dot(m[pl.ds(pl.multiple_of(at, 64), 64), :], weight, preferred_element_type=F32)
        b_low[places[0]] += out
        b_high[places[1]] += out

    @pl.loop(0, BY)
    def _(y):
        for z in range(0, BZ, 2):
            rim_terms(right_x, y * BZ + z, m_x, y * 256 + z * 32, [keys[1, y, 0, z + k] for k in range(2)])

    @pl.loop(0, BX)
    def _(x):
        for z in range(0, BZ, 2):
            rim_terms(right_y, x * BZ + z, m_y, x * 256 + z * 32, [keys[3, 0, x, z + k] for k in range(2)])

    @pl.loop(0, LINES // 2)
    def _(half):
        line = half * 2
        places = [keys[5, line % BY + k, line // BY, 0] for k in range(2)]
        rim_terms(right_z, line, m_z, half * 64, places)

    for copy in brought:
        copy.wait()

    @pl.loop(0, BY)
    def _(y):
        for z in range(0, BZ, 2):
            e = ((BX - 1) * BY + y) * BZ + z
            at = y * 256 + z * 32
            couples(right, (right_xp + y) * 8 + z, 1, couple, [(1, face_x, [at, at + 32], [e, e + 1])])

    @pl.loop(0, BX)
    def _(x):
        for z in range(0, BZ, 2):
            e = (x * BY + BY - 1) * BZ + z
            at = x * 256 + z * 32
            couples(right, (right_yp + x) * 8 + z, 1, couple, [(2, face_y, [at, at + 32], [e, e + 1])])

    @pl.loop(0, LINES // 2)
    def _(half):
        line = half * 2
        e = line * BZ + BZ - 1
        couples(right, right_zp * 8 + line, 1, couple, [(3, face_z, [line * 32, line * 32 + 32], [e, e + BZ])])

    def terms(cell, places):
        at = pl.multiple_of(cell * 64, 128)
        out = jnp.dot(left[pl.ds(at, 128), :], couple[pl.ds(at, 128), :], preferred_element_type=F32)
        for k in range(2):
            for f, (key_f, key_b) in places[k].items():
                tile = f // 2
                term = out[k * 64 : k * 64 + 64, tile * 128 : tile * 128 + 128]
                if key_f is not None:
                    (f_low, f_high)[f % 2][key_f] += term
                if key_b is not None:
                    (b_low, b_high)[f % 2][key_b] += term


    @pl.loop(0, LINES)
    def _(line):
        x, y = line // BY, line % BY
        next_x, next_y = jnp.minimum(x + 1, BX - 1), jnp.minimum(y + 1, BY - 1)
        for z in range(0, BZ, 2):
            places = []
            for k in range(z, z + 2):
                onward_x = jnp.where(x < BX - 1, keys[1, y, next_x, k], KEYS)
                onward_y = jnp.where(y < BY - 1, keys[3, next_y, x, k], KEYS)
                places.append(
                    {
                        0: (keys[0, y, x, k], None),
                        1: (keys[2, y, x, k], onward_x),
                        2: (keys[4, y, x, k], onward_y),
                        3: (keys[6, y, x, k], keys[5, y, x, k + 1] if k < BZ - 1 else None),
                    }
                )
            terms(line * BZ + z, places)

    depth = send.shape[0]
    for copy in marks:
        copy.wait()

    @pl.loop(0, depth)
    def _(c):
        tally[c] = 0

    def fold(r):
        low = lane_low((64, 128))
        for s in range(0, SLOTS, 4):
            blocks = []
            for k in (s, s + 2):
                at = [r * SLOTS + min(k + side, SLOTS - 1) for side in range(2)]
                pair = jnp.where(low, b_low[at[0]], b_high[at[1]])
                pair += pltpu.roll(jnp.where(low, b_low[at[1]], b_high[at[0]]), 64, axis=1)
                blocks.append(pair)
            flipped = jnp.concatenate(blocks, axis=0).T
            for k in range(s, min(s + 4, SLOTS)):
                ref = f_low if k < s + 2 else f_high
                ref[r * SLOTS + k] += flipped[k % 2 * 64 : k % 2 * 64 + 64]

    def lay_out(r):
        low_half = lane_low((32, 128))
        for s in range(SLOTS):
            parts = f_low.at[r * SLOTS + s], f_high.at[r * SLOTS + s]
            even, odd = ([ref[pl.ds(p, 32, stride=2), :] for ref in parts] for p in range(2))
            row = jnp.where(low_half, even[0], odd[1])
            row += pltpu.roll(jnp.where(low_half, odd[0], even[1]), 64, axis=1)
            rows[pl.ds(pl.multiple_of(r * ROW + s * 32, 32), 32), :] = row.astype(BF16)

    def hand_out(r):
        c = owner[r]
        place = tally[c]
        tally[c] = place + 1
        pltpu.make_async_copy(
            rows.at[pl.ds(pl.multiple_of(r * ROW, 32), ROW)],
            send.at[c, pl.ds(pl.multiple_of(place * ROW, 32), ROW)],
            sems.at[r],
        ).start()

    @pl.loop(0, AGG_DEV // 2)
    def _(half):
        pair = (half * 2, half * 2 + 1)
        for step in (fold, lay_out, hand_out):
            for r in pair:
                step(r)

    @pl.loop(0, AGG_DEV)
    def _(r):
        pltpu.make_async_copy(rows.at[pl.ds(0, ROW)], send.at[0, pl.ds(0, ROW)], sems.at[r]).wait()


def coarse_rows(aggregate, slot, owner, arrays, depth):
    smem = pl.BlockSpec(memory_space=pltpu.SMEM)
    vmem = pl.BlockSpec(memory_space=pltpu.VMEM)
    any_space = pl.BlockSpec(memory_space=pl.ANY)
    beyond = BY + BX + LINES // 8
    return pl.pallas_call(
        compute_kernel,
        out_shape=jax.ShapeDtypeStruct((depth, PACK, 128), BF16),
        in_specs=[vmem, vmem, smem] + [any_space] * len(arrays),
        out_specs=any_space,
        scratch_shapes=[pltpu.VMEM(array.shape, BF16) for array in arrays[:6] + arrays[8:]]
        + [
            pltpu.SemaphoreType.DMA((12,)),
            pltpu.SMEM((SLOTS, BY, BX, BZ), jnp.int32),
            pltpu.VMEM((SLOTS, BY, BX, BZ), jnp.int32),
            pltpu.SemaphoreType.DMA,
            pltpu.SemaphoreType.DMA((BX, 2)),
            pltpu.VMEM((beyond * 512, 128), BF16),
            pltpu.VMEM((CELLS * 64, 128), BF16),
            pltpu.VMEM((CELLS * 64, 256), BF16),
            pltpu.VMEM((2, 8 * STEP_TWICE, 128), F32),
            pltpu.VMEM((KEYS + 1, 64, 128), F32),
            pltpu.VMEM((KEYS + 1, 64, 128), F32),
            pltpu.VMEM((KEYS + 1, 64, 128), F32),
            pltpu.VMEM((KEYS + 1, 64, 128), F32),
            pltpu.VMEM((AGG_DEV * ROW, 128), BF16),
            pltpu.VMEM((depth, 16, 128), BF16),
            pltpu.SMEM((depth,), jnp.int32),
            pltpu.SemaphoreType.DMA((AGG_DEV,)),
            pltpu.SemaphoreType.DMA((PLACES,)),
        ],
        compiler_params=pltpu.CompilerParams(vmem_limit_bytes=63 << 20),
        name="coarse_rows",
    )(aggregate, slot, owner, *arrays)


GROUP, ROW_STEP, ROW_PARTS = 8, ROW + 4, 4


def place_kernel(taken, out, told, counts, tally, source, held, work, shaped, sems, row_sems, out_sems):
    depth, count = taken.shape[0], out.shape[1]
    loads = [
        pltpu.make_async_copy(taken.at[:, pl.ds(k * ROW, 16)], told.at[k], sems.at[k]) for k in range(PLACES)
    ]
    for load in loads:
        load.start()
    part = depth // ROW_PARTS
    brought = []
    for k in range(ROW_PARTS):
        at = pl.ds(k * part, part)
        copy = pltpu.make_async_copy(taken.at[at], held.at[at], row_sems.at[k])
        copy.start()
        brought.append(copy)

    @pl.loop(0, count + PLACES)
    def _(t):
        source[t] = 0

    for load in loads:
        load.wait()
    for c in range(depth):
        here = [told[k, c, 0:1, :].astype(F32) for k in range(PLACES)]
        counts[c : c + 1, :] = sum((value == value).astype(jnp.int32) for value in here)
    move = pltpu.make_async_copy(counts, tally, sems.at[PLACES])
    move.start()
    move.wait()

    def order(c, total):
        for k in range(PLACES):
            source[total + k] = c * PLACES + k
        return total + tally[c, 0]

    total = lax.fori_loop(0, depth, order, 0)

    for copy in brought:
        copy.wait()

    def out_copy(group):
        rows = pl.ds(pl.multiple_of(group * GROUP, GROUP), GROUP)
        return pltpu.make_async_copy(shaped.at[group], out.at[:, rows, :], out_sems.at[group])

    @pl.loop(0, count // GROUP)
    def _(group):
        for k in range(GROUP):
            t = group * GROUP + k
            at = jnp.where(t < total, source[t], 0)
            place = pl.multiple_of(lax.rem(at, PLACES) * ROW, 32)
            row = held[at // PLACES, pl.ds(place, ROW), :].astype(F32)
            work[k * ROW_STEP : k * ROW_STEP + ROW, :] = jnp.where(t < total, row, jnp.zeros_like(row))
        for s in range(SLOTS):
            for tile in range(32):
                piece = work[pl.ds(s * 32 + tile, GROUP, stride=ROW_STEP), :]
                shaped[group, s, :, tile * 128 : tile * 128 + 128] = piece.astype(BF16)
        out_copy(group).start()

    @pl.loop(0, count // GROUP)
    def _(group):
        out_copy(group).wait()


def place_rows(taken):
    depth = taken.shape[0]
    count = depth * PLACES
    any_space = pl.BlockSpec(memory_space=pl.ANY)
    return pl.pallas_call(
        place_kernel,
        out_shape=jax.ShapeDtypeStruct((SLOTS, count, NODES * NODES), BF16),
        in_specs=[any_space],
        out_specs=any_space,
        scratch_shapes=[
            pltpu.VMEM((PLACES, depth, 16, 128), BF16),
            pltpu.VMEM((depth, 128), jnp.int32),
            pltpu.SMEM((depth, 128), jnp.int32),
            pltpu.SMEM((count + PLACES,), jnp.int32),
            pltpu.VMEM((depth, PACK, 128), BF16),
            pltpu.VMEM((GROUP * ROW_STEP, 128), F32),
            pltpu.VMEM((count // GROUP, SLOTS, GROUP, NODES * NODES), BF16),
            pltpu.SemaphoreType.DMA((PLACES + 1,)),
            pltpu.SemaphoreType.DMA((ROW_PARTS,)),
            pltpu.SemaphoreType.DMA((count // GROUP,)),
        ],
        compiler_params=pltpu.CompilerParams(vmem_limit_bytes=63 << 20),
        name="place_rows",
    )(taken)


def shards(a_diag, a_face, prolong, aggregate, pair_slot, row_owner):
    block = a_diag.shape[-1]
    depth = lax.axis_size("gz")
    holding = PLACES * depth

    arrays = inner(prolong, a_face, a_diag)
    send = coarse_rows(
        aggregate.transpose(1, 0, 2), pair_slot.transpose(0, 2, 1, 3), row_owner, arrays, depth
    )
    taken = lax.all_to_all(send, "gz", 0, 0, tiled=True)
    coarse = place_rows(taken).transpose(1, 0, 2)
    return coarse.reshape(1, 1, 1, holding, SLOTS, block)


def solution(mesh):
    return jax.shard_map(
        shards,
        mesh=mesh,
        in_specs=(
            P("gx", "gy", "gz", None),
            P(None, "gx", "gy", "gz", None),
            P("gx", "gy", "gz", None),
            P("gx", "gy", "gz"),
            P(None, "gx", "gy", "gz"),
            P(("gx", "gy", "gz")),
        ),
        out_specs=P("gx", "gy", "gz", None, None, None),
        check_vma=False,
    )
```

```python
import jax
import jax.numpy as jnp
from jax import lax
from jax.experimental import pallas as pl
from jax.experimental.pallas import tpu as pltpu
from jax.sharding import PartitionSpec as P

NODES = 64
SLOTS = 7
AGG_DEV = 24
BX, BY, BZ = 4, 6, 8
LINES = BX * BY
PLACES = 2
ROW = SLOTS * NODES * NODES // 128
PACK = PLACES * ROW
KEYS = AGG_DEV * SLOTS
STEP, STEP_TWICE = 36, 68
F32 = jnp.float32
BF16 = jnp.bfloat16


def sweep(count, by):
    def run(body):
        @pl.loop(0, count // by)
        def _(turn):
            for k in range(by):
                body(turn * by + k, k)

    return run


def lane_low(shape):
    return lax.broadcasted_iota(jnp.int32, shape, 1) < 64


def spread(line, scratch):
    values = line.astype(F32)
    for tile in range(32):
        scratch[pl.ds(tile, 8, stride=STEP), :] = values[:, tile * 128 : tile * 128 + 128]


def spread_twice(line, natural):
    values = line.astype(F32)
    low = lane_low((8, 128))
    for tile in range(32):
        here = values[:, tile * 128 : tile * 128 + 128]
        swapped = pltpu.roll(here, 64, axis=1)
        natural[pl.ds(2 * tile, 8, stride=STEP_TWICE), :] = jnp.where(low, here, swapped)
        natural[pl.ds(2 * tile + 1, 8, stride=STEP_TWICE), :] = jnp.where(low, swapped, here)


MESH = pl.DeviceIdType.MESH


def couples(right, cell, stride, couple, blocks):
    low = lane_low((64, 128))
    zero = jnp.zeros((64, 128), BF16)
    wide = jnp.zeros((128, 128), BF16)
    columns = []
    for k in range(2):
        block = right[pl.ds(pl.multiple_of((cell + k * stride) * 64, 64), 64), :]
        corner = jnp.concatenate([jnp.where(low, block, zero), jnp.where(low, zero, block)], axis=0)
        columns.append(jnp.concatenate([corner, wide] if k == 0 else [wide, corner], axis=0))
    weight = jnp.concatenate(columns, axis=1)
    stack = [
        jnp.concatenate([ref[pl.ds(pl.multiple_of(at, 32), 32), :] for at in ats], axis=1)
        for _, ref, ats, _ in blocks
    ]
    stack = jnp.concatenate(stack, axis=0) if len(stack) > 1 else stack[0]
    both = jnp.dot(stack, weight, preferred_element_type=F32)
    for number, (f, _, _, cells) in enumerate(blocks):
        for k in range(2):
            part = both[number * 32 : number * 32 + 32, k * 128 : k * 128 + 128]
            turned = pltpu.roll(part, 64, axis=1)
            side = f % 2 * 64
            for p in range(2):
                value = (part if p == f % 2 else turned)[:, side : side + 64]
                at = pl.multiple_of(cells[k] * 64 + p * 32, 32)
                couple[pl.ds(at, 32), f * 64 : f * 64 + 64] = value.astype(BF16)


def store_spread(line, dest, base, work):
    spread(line, work)
    for z in range(8):
        at = pl.multiple_of(base + z * 32, 32)
        dest[pl.ds(at, 32), :] = work[z * STEP : z * STEP + 32, :].astype(BF16)


def store_right(right, base, work):
    for z in range(8):
        at = pl.multiple_of(base * 512 + z * 64, 64)
        right[pl.ds(at, 64), :] = work[z * STEP_TWICE : z * STEP_TWICE + 64, :].astype(BF16)


def store_left(left, base, work):
    low = lane_low((64, 128))
    zero = jnp.zeros((64, 128), F32)

    def by_parity(z):
        return jnp.concatenate([work[pl.ds(z * STEP_TWICE + p, 32, stride=2), :] for p in range(2)], axis=0)

    for pair in range(4):
        first, second = by_parity(2 * pair), by_parity(2 * pair + 1)
        block = jnp.concatenate([jnp.where(low, first, zero), jnp.where(low, zero, second)], axis=0)
        at = pl.multiple_of(base * 512 + pair * 128, 128)
        left[pl.ds(at, 128), :] = block.astype(BF16).T


CELLS = LINES * BZ


def inner_kernel(
    prolong, a_face, a_diag,
    m_x, m_y, m_z, p_xp, p_yp, p_zp,
    couple_out, left_out, right_x, right_y, right_z, face_x, face_y, face_z,
    in_p, in_d, in_f, zero, zero_m, out_mx, out_my, out_mz, out_az, out_p_first,
    ra_d, ra_x, ra_y, ra_z, right, first_z, left, couple, work_a, work_b,
    load_sems, send_sems, recv_sems, zero_sems, out_sems,
):
    depth = lax.axis_size("gz")
    gx, gy, gz = (lax.axis_index(axis) for axis in ("gx", "gy", "gz"))
    next_z, previous_z = lax.rem(gz + 1, depth), lax.rem(gz + depth - 1, depth)
    barrier = pltpu.get_barrier_semaphore()
    for target in ({"gx": 1 - gx}, {"gy": 1 - gy}, {"gz": next_z}, {"gz": previous_z}):
        pl.semaphore_signal(barrier, inc=1, device_id=target, device_id_type=MESH)
    last_x, inner_x = pl.ds(BX - 1, 1), pl.ds(0, BX - 1)
    load_parts = (
        (prolong, in_p),
        (a_face.at[0, last_x], in_f.at[0, last_x]),
        (a_face.at[1], in_f.at[1]),
        (a_face.at[2], in_f.at[2]),
        (a_diag, in_d),
        (a_face.at[0, inner_x], in_f.at[0, inner_x]),
    )
    loads = [pltpu.make_async_copy(*part, load_sems.at[k]) for k, part in enumerate(load_parts)]
    for load in loads:
        load.start()
    zero[...] = jnp.zeros_like(zero)
    zero_m[...] = jnp.zeros_like(zero_m)
    pl.semaphore_wait(barrier, 4)

    def exchange(number, source, dest, target, sends, receives, blank):
        copy = pltpu.make_async_remote_copy(
            source, dest, send_sems.at[number], recv_sems.at[number], device_id=target, device_id_type=MESH
        )
        fill = pltpu.make_async_copy(blank, dest, zero_sems.at[number])

        @pl.when(sends)
        def _():
            copy.start()

        @pl.when(jnp.logical_not(receives))
        def _():
            fill.start()

        def finish():
            @pl.when(sends)
            def _():
                copy.wait_send()

            @pl.when(receives)
            def _():
                copy.wait_recv()

            @pl.when(jnp.logical_not(receives))
            def _():
                fill.wait()

        return finish

    def to_line(axis, step):
        here, count = lax.axis_index(axis), lax.axis_size(axis)
        return {axis: lax.rem(here + (step + count), count)}

    def has_line(axis, step):
        here, count = lax.axis_index(axis), lax.axis_size(axis)
        return here > 0 if step < 0 else here < count - 1

    def pass_up(number, axis, source, dest, blank):
        return exchange(number, source, dest, to_line(axis, 1), has_line(axis, 1), has_line(axis, -1), blank)

    def pass_down(number, axis, source, dest, blank):
        return exchange(number, source, dest, to_line(axis, -1), has_line(axis, -1), has_line(axis, 1), blank)

    ends = [
        pass_down(0, "gy", prolong.at[:, 0], p_yp, zero.at[pl.ds(0, BX)]),
        pass_down(1, "gx", prolong.at[0], p_xp, zero),
    ]
    loads[0].wait()

    @pl.loop(0, BX)
    def _(x):
        low = lane_low((32, 128))
        for y in range(BY):
            line = x * BY + y
            at = pl.ds(pl.multiple_of(line * 32, 32), 32)
            natural = work_b.at[y]
            spread_twice(in_p[x, y], natural)
            even, odd = (natural[pl.ds(p, 32, stride=2), :] for p in range(2))
            out_p_first[at, :] = jnp.where(low, even, odd).astype(BF16)
            ra_z[pl.ds(pl.multiple_of(line * 288, 32), 32), :] = jnp.zeros((32, 128), BF16)
            store_right(right, line, natural)
            first_z[pl.ds(pl.multiple_of(line * 64, 64), 64), :] = natural[0:64, :].astype(BF16)
            store_left(left, line, natural)

    ends.append(pass_down(2, "gz", out_p_first, p_zp, zero_m.at[pl.ds(0, LINES * 32)]))
    loads[1].wait()
    loads[2].wait()
    loads[3].wait()

    def outgoing(work, pair, line):
        blocks = []
        for z in (2 * pair, 2 * pair + 1):
            block = work[z * STEP : z * STEP + 32, :]
            blocks += [block, pltpu.roll(block, 64, axis=1)]
        block = jnp.concatenate(blocks, axis=0).astype(BF16)
        at = pl.multiple_of(line * 512 + pair * 128, 128)
        return jnp.dot(left[pl.ds(at, 128), :], block, preferred_element_type=F32)

    def side_by_side(first, second):
        return jnp.where(lane_low((64, 128)), first, pltpu.roll(second, 64, axis=1)).astype(BF16)

    for f, count, out, line_of in (
        (0, BY, out_mx, lambda k: (BX - 1) * BY + k),
        (1, BX, out_my, lambda k: k * BY + BY - 1),
    ):

        @pl.loop(0, count // 2)
        def _(half):
            for k in range(2):
                row = half * 2 + k
                line = line_of(row)
                work = work_a.at[k]
                store_spread(in_f[f, line // BY, line % BY], (ra_x, ra_y)[f], line * 256, work)
                for pair in range(4):
                    both = outgoing(work, pair, line)
                    at = pl.multiple_of(row * 256 + pair * 64, 64)
                    out[pl.ds(at, 64), :] = side_by_side(both[0:64], both[64:128])

    @pl.loop(0, BX)
    def _(x):
        for y in range(0, BY, 2):
            last = []
            for k in range(2):
                line = x * BY + y + k
                work = work_a.at[y + k]
                store_spread(in_f[2, x, y + k], ra_z, line * 288 + 32, work)
                at = pl.ds(pl.multiple_of(line * 32, 32), 32)
                out_az[at, :] = work[(BZ - 1) * STEP : (BZ - 1) * STEP + 32, :].astype(BF16)
                last.append(outgoing(work, BZ // 2 - 1, line)[64:128])
            at = pl.multiple_of((x * BY + y) * 32, 64)
            out_mz[pl.ds(at, 64), :] = side_by_side(*last)

    for number, axis, source, dest in ((3, "gy", out_my, m_y), (4, "gz", out_mz, m_z), (5, "gx", out_mx, m_x)):
        ends.append(pass_up(number, axis, source, dest, zero_m.at[pl.ds(0, source.shape[0])]))
    loads[4].wait()
    loads[5].wait()

    @pl.loop(0, BX)
    def _(x):
        for y in range(BY):
            store_spread(in_d[x, y], ra_d, (x * BY + y) * 256, work_a.at[y])
        for y in range(BY - 1):
            store_spread(in_f[1, x, y], ra_y, (x * BY + y) * 256, work_a.at[y])

    @pl.loop(0, BX - 1)
    def _(x):
        for y in range(BY):
            store_spread(in_f[0, x, y], ra_x, (x * BY + y) * 256, work_a.at[y])

    moves = []

    def put(source, dest):
        copy = pltpu.make_async_copy(source, dest, out_sems.at[len(moves)])
        copy.start()
        moves.append(copy)

    put(left, left_out)
    put(right.at[pl.ds(0, BY * 512)], right_x)
    put(first_z, right_z)
    put(ra_x.at[pl.ds((LINES - BY) * 256, BY * 256)], face_x)
    put(out_az, face_z)
    for x in range(BX):
        put(right.at[pl.ds(x * BY * 512, 512)], right_y.at[pl.ds(x * 512, 512)])
        put(ra_y.at[pl.ds((x * BY + BY - 1) * 256, 256)], face_y.at[pl.ds(x * 256, 256)])

    for x in range(BX):

        @pl.loop(0, BY // 2)
        def _(half):
            for y in (half * 2, half * 2 + 1):
                line = x * BY + y
                from_y = jnp.where(y > 0, line - 1, line)
                into_y = jnp.where(y > 0, (line - 1) * BZ, CELLS)
                for z in range(0, BZ, 2):
                    n = line * BZ + z
                    both = range(2)
                    blocks = [
                        (0, ra_d, [(n + k) * 32 for k in both], [n, n + 1]),
                        (2, ra_y, [from_y * 256 + (z + k) * 32 for k in both], [into_y + z, into_y + z + 1]),
                        (3, ra_z, [line * 288 + (z + k) * 32 for k in both], [CELLS if z == 0 else n - 1, n]),
                    ]
                    if x > 0:
                        e = n - BY * BZ
                        blocks.append((1, ra_x, [(e + k) * 32 for k in both], [e, e + 1]))
                    couples(right, n, 1, couple, blocks)

        if x > 0:
            rows = pl.ds((x - 1) * BY * BZ * 64, BY * BZ * 64)
            put(couple.at[rows], couple_out.at[rows])
    rows = pl.ds((BX - 1) * BY * BZ * 64, BY * BZ * 64)
    put(couple.at[rows], couple_out.at[rows])
    for finish in ends:
        finish()
    for copy in moves:
        copy.wait()


def inner(prolong, a_face, a_diag):
    any_space = pl.BlockSpec(memory_space=pl.ANY)
    x_face, y_face, z_face = (BY, BZ, NODES * NODES), (BX, BZ, NODES * NODES), (LINES * 32, 128)
    shapes = (
        (BY * 256, 128), (BX * 256, 128), (LINES * 32, 128), x_face, y_face, z_face,
        (CELLS * 64, 256), (CELLS * 64, 128),
        (BY * 512, 128), (BX * 512, 128), (LINES * 64, 128),
        (BY * 256, 128), (BX * 256, 128), z_face,
    )
    return pl.pallas_call(
        inner_kernel,
        out_shape=[jax.ShapeDtypeStruct(shape, BF16) for shape in shapes],
        in_specs=[any_space] * 3,
        out_specs=[any_space] * len(shapes),
        scratch_shapes=[
            pltpu.VMEM(prolong.shape, BF16),
            pltpu.VMEM(a_diag.shape, BF16),
            pltpu.VMEM(a_face.shape, BF16),
            pltpu.VMEM(x_face, BF16),
            pltpu.VMEM((BY * 256, 128), BF16),
            pltpu.VMEM((BY * 256, 128), BF16),
            pltpu.VMEM((BX * 256, 128), BF16),
            pltpu.VMEM((LINES * 32, 128), BF16),
            pltpu.VMEM(z_face, BF16),
            pltpu.VMEM(z_face, BF16),
            pltpu.VMEM((LINES * 256, 128), BF16),
            pltpu.VMEM((LINES * 256, 128), BF16),
            pltpu.VMEM((LINES * 256, 128), BF16),
            pltpu.VMEM((LINES * 288, 128), BF16),
            pltpu.VMEM((CELLS * 64, 128), BF16),
            pltpu.VMEM((LINES * 64, 128), BF16),
            pltpu.VMEM((CELLS * 64, 128), BF16),
            pltpu.VMEM(((CELLS + BZ) * 64, 256), BF16),
            pltpu.VMEM((BY, 8 * STEP, 128), F32),
            pltpu.VMEM((BY, 8 * STEP_TWICE, 128), F32),
            pltpu.SemaphoreType.DMA((6,)),
            pltpu.SemaphoreType.DMA((6,)),
            pltpu.SemaphoreType.DMA((6,)),
            pltpu.SemaphoreType.DMA((6,)),
            pltpu.SemaphoreType.DMA((5 + 3 * BX,)),
        ],
        compiler_params=pltpu.CompilerParams(collective_id=0, has_side_effects=True, vmem_limit_bytes=63 << 20),
        name="inner",
    )(prolong, a_face, a_diag)


def compute_kernel(
    aggregate, slot, owner, *refs
):
    arrays, refs = refs[:14], refs[14:]
    small, couple_in, left_in = arrays[:6] + arrays[8:], arrays[6], arrays[7]
    send, held, refs = refs[0], refs[1:13], refs[13:]
    m_x, m_y, m_z, p_xp, p_yp, p_zp, right_x, right_y, right_z, face_x, face_y, face_z = held
    (
    small_sems, keys, key_work, key_sem, in_sems, right, left, couple, work_b,
    f_low, f_high, b_low, b_high, rows, absent, tally, sems, absent_sems,
    ) = refs
    fetched = [pltpu.make_async_copy(*pair, small_sems.at[k]) for k, pair in enumerate(zip(small, held))]
    for copy in fetched:
        copy.start()
    plane = BY * BZ * 64
    brought = []
    for x in range(BX):
        at = pl.ds(x * plane, plane)
        for k, (source, dest) in enumerate(((couple_in, couple), (left_in, left))):
            copy = pltpu.make_async_copy(source.at[at], dest.at[at], in_sems.at[x, k])
            copy.start()
            brought.append(copy)

    absent[...] = jnp.full(absent.shape, jnp.nan, BF16)
    marks = []
    for k in range(PLACES):
        mark = pltpu.make_async_copy(absent, send.at[:, pl.ds(k * ROW, 16)], absent_sems.at[k])
        mark.start()
        marks.append(mark)

    key_work[...] = aggregate[...][None] * SLOTS + slot[...]
    told_keys = pltpu.make_async_copy(key_work, keys, key_sem)
    told_keys.start()
    for ref in (f_low, f_high, b_low, b_high):
        ref[...] = jnp.zeros_like(ref)

    for copy in fetched:
        copy.wait()

    right_xp, right_yp, right_zp = 0, BY, BY + BX

    for count, after, base in ((BY, p_xp, right_xp), (BX, p_yp, right_yp)):

        @sweep(count, 2)
        def _(line, k):
            spread_twice(after[line], work_b.at[k])
            store_right(right, base + line, work_b.at[k])

    @sweep(LINES, 8)
    def _(line, k):
        low = lane_low((32, 128))
        here = p_zp[pl.ds(pl.multiple_of(line * 32, 32), 32), :].astype(F32)
        turned = pltpu.roll(here, 64, axis=1)
        work = work_b.at[k % 2, pl.ds(k // 2 * 64, 64)]
        work[pl.ds(0, 32, stride=2), :] = jnp.where(low, here, turned)
        work[pl.ds(1, 32, stride=2), :] = jnp.where(low, turned, here)
        at = pl.multiple_of((right_zp * 8 + line) * 64, 64)
        right[pl.ds(at, 64), :] = work[...].astype(BF16)

    told_keys.wait()

    def rim_terms(weights, cell, m, at, places):
        low = lane_low((64, 128))
        zero = jnp.zeros((64, 128), BF16)
        first, second = (weights[pl.ds(pl.multiple_of((cell + k) * 64, 64), 64), :] for k in range(2))
        weight = jnp.concatenate([jnp.where(low, first, zero), jnp.where(low, zero, second)], axis=0)
        out = jnp.dot(m[pl.ds(pl.multiple_of(at, 64), 64), :], weight, preferred_element_type=F32)
        b_low[places[0]] += out
        b_high[places[1]] += out

    @sweep(BY, 2)
    def _(y, _turn):
        for z in range(0, BZ, 2):
            rim_terms(right_x, y * BZ + z, m_x, y * 256 + z * 32, [keys[1, y, 0, z + k] for k in range(2)])

    @sweep(BX, 2)
    def _(x, _turn):
        for z in range(0, BZ, 2):
            rim_terms(right_y, x * BZ + z, m_y, x * 256 + z * 32, [keys[3, 0, x, z + k] for k in range(2)])

    @sweep(LINES // 2, 4)
    def _(half, _turn):
        line = half * 2
        places = [keys[5, line % BY + k, line // BY, 0] for k in range(2)]
        rim_terms(right_z, line, m_z, half * 64, places)

    for copy in brought:
        copy.wait()

    @sweep(BY, 3)
    def _(y, _turn):
        for z in range(0, BZ, 2):
            e = ((BX - 1) * BY + y) * BZ + z
            at = y * 256 + z * 32
            couples(right, (right_xp + y) * 8 + z, 1, couple, [(1, face_x, [at, at + 32], [e, e + 1])])

    @sweep(BX, 2)
    def _(x, _turn):
        for z in range(0, BZ, 2):
            e = (x * BY + BY - 1) * BZ + z
            at = x * 256 + z * 32
            couples(right, (right_yp + x) * 8 + z, 1, couple, [(2, face_y, [at, at + 32], [e, e + 1])])

    @sweep(LINES // 2, 6)
    def _(half, _turn):
        line = half * 2
        e = line * BZ + BZ - 1
        couples(right, right_zp * 8 + line, 1, couple, [(3, face_z, [line * 32, line * 32 + 32], [e, e + BZ])])

    def terms(cell, places):
        at = pl.multiple_of(cell * 64, 128)
        out = jnp.dot(left[pl.ds(at, 128), :], couple[pl.ds(at, 128), :], preferred_element_type=F32)
        for k in range(2):
            for f, (key_f, key_b) in places[k].items():
                tile = f // 2
                term = out[k * 64 : k * 64 + 64, tile * 128 : tile * 128 + 128]
                if key_f is not None:
                    (f_low, f_high)[f % 2][key_f] += term
                if key_b is not None:
                    (b_low, b_high)[f % 2][key_b] += term


    @sweep(LINES, 2)
    def _(line, _turn):
        x, y = line // BY, line % BY
        next_x, next_y = jnp.minimum(x + 1, BX - 1), jnp.minimum(y + 1, BY - 1)
        for z in range(0, BZ, 2):
            places = []
            for k in range(z, z + 2):
                onward_x = jnp.where(x < BX - 1, keys[1, y, next_x, k], KEYS)
                onward_y = jnp.where(y < BY - 1, keys[3, next_y, x, k], KEYS)
                places.append(
                    {
                        0: (keys[0, y, x, k], None),
                        1: (keys[2, y, x, k], onward_x),
                        2: (keys[4, y, x, k], onward_y),
                        3: (keys[6, y, x, k], keys[5, y, x, k + 1] if k < BZ - 1 else None),
                    }
                )
            terms(line * BZ + z, places)

    depth = send.shape[0]
    for copy in marks:
        copy.wait()

    @pl.loop(0, depth)
    def _(c):
        tally[c] = 0

    def fold(r):
        low = lane_low((64, 128))
        for s in range(0, SLOTS, 4):
            blocks = []
            for k in (s, s + 2):
                at = [r * SLOTS + min(k + side, SLOTS - 1) for side in range(2)]
                pair = jnp.where(low, b_low[at[0]], b_high[at[1]])
                pair += pltpu.roll(jnp.where(low, b_low[at[1]], b_high[at[0]]), 64, axis=1)
                blocks.append(pair)
            flipped = jnp.concatenate(blocks, axis=0).T
            for k in range(s, min(s + 4, SLOTS)):
                ref = f_low if k < s + 2 else f_high
                ref[r * SLOTS + k] += flipped[k % 2 * 64 : k % 2 * 64 + 64]

    def lay_out(r):
        low_half = lane_low((32, 128))
        for s in range(SLOTS):
            parts = f_low.at[r * SLOTS + s], f_high.at[r * SLOTS + s]
            even, odd = ([ref[pl.ds(p, 32, stride=2), :] for ref in parts] for p in range(2))
            row = jnp.where(low_half, even[0], odd[1])
            row += pltpu.roll(jnp.where(low_half, odd[0], even[1]), 64, axis=1)
            rows[pl.ds(pl.multiple_of(r * ROW + s * 32, 32), 32), :] = row.astype(BF16)

    def hand_out(r):
        c = owner[r]
        place = tally[c]
        tally[c] = place + 1
        pltpu.make_async_copy(
            rows.at[pl.ds(pl.multiple_of(r * ROW, 32), ROW)],
            send.at[c, pl.ds(pl.multiple_of(place * ROW, 32), ROW)],
            sems.at[r],
        ).start()

    @pl.loop(0, AGG_DEV // 2)
    def _(half):
        pair = (half * 2, half * 2 + 1)
        for step in (fold, lay_out, hand_out):
            for r in pair:
                step(r)

    @pl.loop(0, AGG_DEV)
    def _(r):
        pltpu.make_async_copy(rows.at[pl.ds(0, ROW)], send.at[0, pl.ds(0, ROW)], sems.at[r]).wait()


def coarse_rows(aggregate, slot, owner, arrays, depth):
    smem = pl.BlockSpec(memory_space=pltpu.SMEM)
    vmem = pl.BlockSpec(memory_space=pltpu.VMEM)
    any_space = pl.BlockSpec(memory_space=pl.ANY)
    beyond = BY + BX + LINES // 8
    return pl.pallas_call(
        compute_kernel,
        out_shape=jax.ShapeDtypeStruct((depth, PACK, 128), BF16),
        in_specs=[vmem, vmem, smem] + [any_space] * len(arrays),
        out_specs=any_space,
        scratch_shapes=[pltpu.VMEM(array.shape, BF16) for array in arrays[:6] + arrays[8:]]
        + [
            pltpu.SemaphoreType.DMA((12,)),
            pltpu.SMEM((SLOTS, BY, BX, BZ), jnp.int32),
            pltpu.VMEM((SLOTS, BY, BX, BZ), jnp.int32),
            pltpu.SemaphoreType.DMA,
            pltpu.SemaphoreType.DMA((BX, 2)),
            pltpu.VMEM((beyond * 512, 128), BF16),
            pltpu.VMEM((CELLS * 64, 128), BF16),
            pltpu.VMEM((CELLS * 64, 256), BF16),
            pltpu.VMEM((2, 8 * STEP_TWICE, 128), F32),
            pltpu.VMEM((KEYS + 1, 64, 128), F32),
            pltpu.VMEM((KEYS + 1, 64, 128), F32),
            pltpu.VMEM((KEYS + 1, 64, 128), F32),
            pltpu.VMEM((KEYS + 1, 64, 128), F32),
            pltpu.VMEM((AGG_DEV * ROW, 128), BF16),
            pltpu.VMEM((depth, 16, 128), BF16),
            pltpu.SMEM((depth,), jnp.int32),
            pltpu.SemaphoreType.DMA((AGG_DEV,)),
            pltpu.SemaphoreType.DMA((PLACES,)),
        ],
        compiler_params=pltpu.CompilerParams(vmem_limit_bytes=63 << 20),
        name="coarse_rows",
    )(aggregate, slot, owner, *arrays)


GROUP, ROW_STEP, ROW_PARTS = 8, ROW + 4, 4


def place_kernel(taken, out, told, counts, tally, source, held, work, shaped, sems, row_sems, out_sems):
    depth, count = taken.shape[0], out.shape[1]
    loads = [
        pltpu.make_async_copy(taken.at[:, pl.ds(k * ROW, 16)], told.at[k], sems.at[k]) for k in range(PLACES)
    ]
    for load in loads:
        load.start()
    part = depth // ROW_PARTS
    brought = []
    for k in range(ROW_PARTS):
        at = pl.ds(k * part, part)
        copy = pltpu.make_async_copy(taken.at[at], held.at[at], row_sems.at[k])
        copy.start()
        brought.append(copy)

    @pl.loop(0, count + PLACES)
    def _(t):
        source[t] = 0

    for load in loads:
        load.wait()
    for c in range(depth):
        here = [told[k, c, 0:1, :].astype(F32) for k in range(PLACES)]
        counts[c : c + 1, :] = sum((value == value).astype(jnp.int32) for value in here)
    move = pltpu.make_async_copy(counts, tally, sems.at[PLACES])
    move.start()
    move.wait()

    def order(c, total):
        for k in range(PLACES):
            source[total + k] = c * PLACES + k
        return total + tally[c, 0]

    total = lax.fori_loop(0, depth, order, 0)

    for copy in brought:
        copy.wait()

    def out_copy(group):
        rows = pl.ds(pl.multiple_of(group * GROUP, GROUP), GROUP)
        return pltpu.make_async_copy(shaped.at[group], out.at[:, rows, :], out_sems.at[group])

    @pl.loop(0, count // GROUP)
    def _(group):
        for k in range(GROUP):
            t = group * GROUP + k
            at = jnp.where(t < total, source[t], 0)
            place = pl.multiple_of(lax.rem(at, PLACES) * ROW, 32)
            row = held[at // PLACES, pl.ds(place, ROW), :].astype(F32)
            work[k * ROW_STEP : k * ROW_STEP + ROW, :] = jnp.where(t < total, row, jnp.zeros_like(row))
        for s in range(SLOTS):
            for tile in range(32):
                piece = work[pl.ds(s * 32 + tile, GROUP, stride=ROW_STEP), :]
                shaped[group, s, :, tile * 128 : tile * 128 + 128] = piece.astype(BF16)
        out_copy(group).start()

    @pl.loop(0, count // GROUP)
    def _(group):
        out_copy(group).wait()


def place_rows(taken):
    depth = taken.shape[0]
    count = depth * PLACES
    any_space = pl.BlockSpec(memory_space=pl.ANY)
    return pl.pallas_call(
        place_kernel,
        out_shape=jax.ShapeDtypeStruct((SLOTS, count, NODES * NODES), BF16),
        in_specs=[any_space],
        out_specs=any_space,
        scratch_shapes=[
            pltpu.VMEM((PLACES, depth, 16, 128), BF16),
            pltpu.VMEM((depth, 128), jnp.int32),
            pltpu.SMEM((depth, 128), jnp.int32),
            pltpu.SMEM((count + PLACES,), jnp.int32),
            pltpu.VMEM((depth, PACK, 128), BF16),
            pltpu.VMEM((GROUP * ROW_STEP, 128), F32),
            pltpu.VMEM((count // GROUP, SLOTS, GROUP, NODES * NODES), BF16),
            pltpu.SemaphoreType.DMA((PLACES + 1,)),
            pltpu.SemaphoreType.DMA((ROW_PARTS,)),
            pltpu.SemaphoreType.DMA((count // GROUP,)),
        ],
        compiler_params=pltpu.CompilerParams(vmem_limit_bytes=63 << 20),
        name="place_rows",
    )(taken)


def shards(a_diag, a_face, prolong, aggregate, pair_slot, row_owner):
    block = a_diag.shape[-1]
    depth = lax.axis_size("gz")
    holding = PLACES * depth

    arrays = inner(prolong, a_face, a_diag)
    send = coarse_rows(
        aggregate.transpose(1, 0, 2), pair_slot.transpose(0, 2, 1, 3), row_owner, arrays, depth
    )
    taken = lax.all_to_all(send, "gz", 0, 0, tiled=True)
    coarse = place_rows(taken).transpose(1, 0, 2)
    return coarse.reshape(1, 1, 1, holding, SLOTS, block)


def solution(mesh):
    return jax.shard_map(
        shards,
        mesh=mesh,
        in_specs=(
            P("gx", "gy", "gz", None),
            P(None, "gx", "gy", "gz", None),
            P("gx", "gy", "gz", None),
            P("gx", "gy", "gz"),
            P(None, "gx", "gy", "gz"),
            P(("gx", "gy", "gz")),
        ),
        out_specs=P("gx", "gy", "gz", None, None, None),
        check_vma=False,
    )
```

```python
import jax
import jax.numpy as jnp
from jax import lax
from jax.experimental import pallas as pl
from jax.experimental.pallas import tpu as pltpu
from jax.sharding import PartitionSpec as P

NODES = 64
SLOTS = 7
AGG_DEV = 24
BX, BY, BZ = 4, 6, 8
LINES = BX * BY
PLACES = 2
ROW = SLOTS * NODES * NODES // 128
PACK = PLACES * ROW
KEYS = AGG_DEV * SLOTS
STEP, STEP_TWICE = 36, 68
F32 = jnp.float32
BF16 = jnp.bfloat16


def sweep(count, by):
    def run(body):
        @pl.loop(0, count // by)
        def _(turn):
            for k in range(by):
                body(turn * by + k, k)

    return run


def lane_low(shape):
    return lax.broadcasted_iota(jnp.int32, shape, 1) < 64


def spread(line, scratch):
    values = line.astype(F32)
    for tile in range(32):
        scratch[pl.ds(tile, 8, stride=STEP), :] = values[:, tile * 128 : tile * 128 + 128]


def spread_twice(line, natural):
    values = line.astype(F32)
    low = lane_low((8, 128))
    for tile in range(32):
        here = values[:, tile * 128 : tile * 128 + 128]
        swapped = pltpu.roll(here, 64, axis=1)
        natural[pl.ds(2 * tile, 8, stride=STEP_TWICE), :] = jnp.where(low, here, swapped)
        natural[pl.ds(2 * tile + 1, 8, stride=STEP_TWICE), :] = jnp.where(low, swapped, here)


MESH = pl.DeviceIdType.MESH


def couples(right, cell, stride, couple, blocks):
    low = lane_low((64, 128))
    zero = jnp.zeros((64, 128), BF16)
    wide = jnp.zeros((128, 128), BF16)
    columns = []
    for k in range(2):
        block = right[pl.ds(pl.multiple_of((cell + k * stride) * 64, 64), 64), :]
        corner = jnp.concatenate([jnp.where(low, block, zero), jnp.where(low, zero, block)], axis=0)
        columns.append(jnp.concatenate([corner, wide] if k == 0 else [wide, corner], axis=0))
    weight = jnp.concatenate(columns, axis=1)
    stack = [
        jnp.concatenate([ref[pl.ds(pl.multiple_of(at, 32), 32), :] for at in ats], axis=1)
        for _, ref, ats, _ in blocks
    ]
    stack = jnp.concatenate(stack, axis=0) if len(stack) > 1 else stack[0]
    both = jnp.dot(stack, weight, preferred_element_type=F32)
    for number, (f, _, _, cells) in enumerate(blocks):
        for k in range(2):
            part = both[number * 32 : number * 32 + 32, k * 128 : k * 128 + 128]
            turned = pltpu.roll(part, 64, axis=1)
            side = f % 2 * 64
            for p in range(2):
                value = (part if p == f % 2 else turned)[:, side : side + 64]
                at = pl.multiple_of(cells[k] * 64 + p * 32, 32)
                couple[pl.ds(at, 32), f * 64 : f * 64 + 64] = value.astype(BF16)


def store_spread(line, dest, base, work):
    spread(line, work)
    for z in range(8):
        at = pl.multiple_of(base + z * 32, 32)
        dest[pl.ds(at, 32), :] = work[z * STEP : z * STEP + 32, :].astype(BF16)


def store_right(right, base, work):
    for z in range(8):
        at = pl.multiple_of(base * 512 + z * 64, 64)
        right[pl.ds(at, 64), :] = work[z * STEP_TWICE : z * STEP_TWICE + 64, :].astype(BF16)


def store_left(left, base, work):
    low = lane_low((64, 128))
    zero = jnp.zeros((64, 128), F32)

    def by_parity(z):
        return jnp.concatenate([work[pl.ds(z * STEP_TWICE + p, 32, stride=2), :] for p in range(2)], axis=0)

    for pair in range(4):
        first, second = by_parity(2 * pair), by_parity(2 * pair + 1)
        block = jnp.concatenate([jnp.where(low, first, zero), jnp.where(low, zero, second)], axis=0)
        at = pl.multiple_of(base * 512 + pair * 128, 128)
        left[pl.ds(at, 128), :] = block.astype(BF16).T


CELLS = LINES * BZ


def inner_kernel(
    prolong, a_face, a_diag,
    m_x, m_y, m_z, p_xp, p_yp, p_zp,
    couple_out, left_out, right_x, right_y, right_z, face_x, face_y, face_z,
    in_p, in_d, in_f, zero, zero_m, out_mx, out_my, out_mz, out_az, out_p_first,
    ra_d, ra_x, ra_y, ra_z, right, first_z, left, couple, work_a, work_b,
    load_sems, send_sems, recv_sems, zero_sems, out_sems,
):
    depth = lax.axis_size("gz")
    gx, gy, gz = (lax.axis_index(axis) for axis in ("gx", "gy", "gz"))
    next_z, previous_z = lax.rem(gz + 1, depth), lax.rem(gz + depth - 1, depth)
    barrier = pltpu.get_barrier_semaphore()
    for target in ({"gx": 1 - gx}, {"gy": 1 - gy}, {"gz": next_z}, {"gz": previous_z}):
        pl.semaphore_signal(barrier, inc=1, device_id=target, device_id_type=MESH)
    last_x, inner_x = pl.ds(BX - 1, 1), pl.ds(0, BX - 1)
    load_parts = (
        (prolong, in_p),
        (a_face.at[0, last_x], in_f.at[0, last_x]),
        (a_face.at[1], in_f.at[1]),
        (a_face.at[2], in_f.at[2]),
        (a_diag, in_d),
        (a_face.at[0, inner_x], in_f.at[0, inner_x]),
    )
    loads = [pltpu.make_async_copy(*part, load_sems.at[k]) for k, part in enumerate(load_parts)]
    for load in loads:
        load.start()
    zero[...] = jnp.zeros_like(zero)
    zero_m[...] = jnp.zeros_like(zero_m)
    pl.semaphore_wait(barrier, 4)

    def exchange(number, source, dest, target, sends, receives, blank):
        copy = pltpu.make_async_remote_copy(
            source, dest, send_sems.at[number], recv_sems.at[number], device_id=target, device_id_type=MESH
        )
        fill = pltpu.make_async_copy(blank, dest, zero_sems.at[number])

        @pl.when(sends)
        def _():
            copy.start()

        @pl.when(jnp.logical_not(receives))
        def _():
            fill.start()

        def finish():
            @pl.when(sends)
            def _():
                copy.wait_send()

            @pl.when(receives)
            def _():
                copy.wait_recv()

            @pl.when(jnp.logical_not(receives))
            def _():
                fill.wait()

        return finish

    def to_line(axis, step):
        here, count = lax.axis_index(axis), lax.axis_size(axis)
        return {axis: lax.rem(here + (step + count), count)}

    def has_line(axis, step):
        here, count = lax.axis_index(axis), lax.axis_size(axis)
        return here > 0 if step < 0 else here < count - 1

    def pass_up(number, axis, source, dest, blank):
        return exchange(number, source, dest, to_line(axis, 1), has_line(axis, 1), has_line(axis, -1), blank)

    def pass_down(number, axis, source, dest, blank):
        return exchange(number, source, dest, to_line(axis, -1), has_line(axis, -1), has_line(axis, 1), blank)

    ends = [
        pass_down(0, "gy", prolong.at[:, 0], p_yp, zero.at[pl.ds(0, BX)]),
        pass_down(1, "gx", prolong.at[0], p_xp, zero),
    ]
    loads[0].wait()

    @pl.loop(0, BX)
    def _(x):
        low = lane_low((32, 128))
        for y in range(BY):
            line = x * BY + y
            at = pl.ds(pl.multiple_of(line * 32, 32), 32)
            natural = work_b.at[y]
            spread_twice(in_p[x, y], natural)
            even, odd = (natural[pl.ds(p, 32, stride=2), :] for p in range(2))
            out_p_first[at, :] = jnp.where(low, even, odd).astype(BF16)
            ra_z[pl.ds(pl.multiple_of(line * 288, 32), 32), :] = jnp.zeros((32, 128), BF16)
            store_right(right, line, natural)
            first_z[pl.ds(pl.multiple_of(line * 64, 64), 64), :] = natural[0:64, :].astype(BF16)
            store_left(left, line, natural)

    ends.append(pass_down(2, "gz", out_p_first, p_zp, zero_m.at[pl.ds(0, LINES * 32)]))
    loads[1].wait()
    loads[2].wait()
    loads[3].wait()

    def outgoing(work, pair, line):
        blocks = []
        for z in (2 * pair, 2 * pair + 1):
            block = work[z * STEP : z * STEP + 32, :]
            blocks += [block, pltpu.roll(block, 64, axis=1)]
        block = jnp.concatenate(blocks, axis=0).astype(BF16)
        at = pl.multiple_of(line * 512 + pair * 128, 128)
        return jnp.dot(left[pl.ds(at, 128), :], block, preferred_element_type=F32)

    def side_by_side(first, second):
        return jnp.where(lane_low((64, 128)), first, pltpu.roll(second, 64, axis=1)).astype(BF16)

    for f, count, out, line_of in (
        (0, BY, out_mx, lambda k: (BX - 1) * BY + k),
        (1, BX, out_my, lambda k: k * BY + BY - 1),
    ):

        for row in range(count):
            line = line_of(row)
            work = work_a.at[row]
            store_spread(in_f[f, line // BY, line % BY], (ra_x, ra_y)[f], line * 256, work)
            for pair in range(4):
                both = outgoing(work, pair, line)
                out[row * 256 + pair * 64 : row * 256 + pair * 64 + 64, :] = side_by_side(both[0:64], both[64:128])

    @pl.loop(0, BX)
    def _(x):
        for y in range(0, BY, 2):
            last = []
            for k in range(2):
                line = x * BY + y + k
                work = work_a.at[y + k]
                store_spread(in_f[2, x, y + k], ra_z, line * 288 + 32, work)
                at = pl.ds(pl.multiple_of(line * 32, 32), 32)
                out_az[at, :] = work[(BZ - 1) * STEP : (BZ - 1) * STEP + 32, :].astype(BF16)
                last.append(outgoing(work, BZ // 2 - 1, line)[64:128])
            at = pl.multiple_of((x * BY + y) * 32, 64)
            out_mz[pl.ds(at, 64), :] = side_by_side(*last)

    for number, axis, source, dest in ((3, "gy", out_my, m_y), (4, "gz", out_mz, m_z), (5, "gx", out_mx, m_x)):
        ends.append(pass_up(number, axis, source, dest, zero_m.at[pl.ds(0, source.shape[0])]))
    loads[4].wait()
    loads[5].wait()

    @pl.loop(0, BX)
    def _(x):
        for y in range(BY):
            store_spread(in_d[x, y], ra_d, (x * BY + y) * 256, work_a.at[y])
        for y in range(BY - 1):
            store_spread(in_f[1, x, y], ra_y, (x * BY + y) * 256, work_a.at[y])

    @pl.loop(0, BX - 1)
    def _(x):
        for y in range(BY):
            store_spread(in_f[0, x, y], ra_x, (x * BY + y) * 256, work_a.at[y])

    moves = []

    def put(source, dest):
        copy = pltpu.make_async_copy(source, dest, out_sems.at[len(moves)])
        copy.start()
        moves.append(copy)

    put(left, left_out)
    put(right.at[pl.ds(0, BY * 512)], right_x)
    put(first_z, right_z)
    put(ra_x.at[pl.ds((LINES - BY) * 256, BY * 256)], face_x)
    put(out_az, face_z)
    for x in range(BX):
        put(right.at[pl.ds(x * BY * 512, 512)], right_y.at[pl.ds(x * 512, 512)])
        put(ra_y.at[pl.ds((x * BY + BY - 1) * 256, 256)], face_y.at[pl.ds(x * 256, 256)])

    for x in range(BX):

        @pl.loop(0, 2)
        def _(half):
            for k in range(BY // 2):
                y = half * (BY // 2) + k
                line = x * BY + y
                from_y = jnp.where(y > 0, line - 1, line)
                into_y = jnp.where(y > 0, (line - 1) * BZ, CELLS)
                for z in range(0, BZ, 2):
                    n = line * BZ + z
                    both = range(2)
                    blocks = [
                        (0, ra_d, [(n + k) * 32 for k in both], [n, n + 1]),
                        (2, ra_y, [from_y * 256 + (z + k) * 32 for k in both], [into_y + z, into_y + z + 1]),
                        (3, ra_z, [line * 288 + (z + k) * 32 for k in both], [CELLS if z == 0 else n - 1, n]),
                    ]
                    if x > 0:
                        e = n - BY * BZ
                        blocks.append((1, ra_x, [(e + k) * 32 for k in both], [e, e + 1]))
                    couples(right, n, 1, couple, blocks)

        if x > 0:
            rows = pl.ds((x - 1) * BY * BZ * 64, BY * BZ * 64)
            put(couple.at[rows], couple_out.at[rows])
    rows = pl.ds((BX - 1) * BY * BZ * 64, BY * BZ * 64)
    put(couple.at[rows], couple_out.at[rows])
    for finish in ends:
        finish()
    for copy in moves:
        copy.wait()


def inner(prolong, a_face, a_diag):
    any_space = pl.BlockSpec(memory_space=pl.ANY)
    x_face, y_face, z_face = (BY, BZ, NODES * NODES), (BX, BZ, NODES * NODES), (LINES * 32, 128)
    shapes = (
        (BY * 256, 128), (BX * 256, 128), (LINES * 32, 128), x_face, y_face, z_face,
        (CELLS * 64, 256), (CELLS * 64, 128),
        (BY * 512, 128), (BX * 512, 128), (LINES * 64, 128),
        (BY * 256, 128), (BX * 256, 128), z_face,
    )
    return pl.pallas_call(
        inner_kernel,
        out_shape=[jax.ShapeDtypeStruct(shape, BF16) for shape in shapes],
        in_specs=[any_space] * 3,
        out_specs=[any_space] * len(shapes),
        scratch_shapes=[
            pltpu.VMEM(prolong.shape, BF16),
            pltpu.VMEM(a_diag.shape, BF16),
            pltpu.VMEM(a_face.shape, BF16),
            pltpu.VMEM(x_face, BF16),
            pltpu.VMEM((BY * 256, 128), BF16),
            pltpu.VMEM((BY * 256, 128), BF16),
            pltpu.VMEM((BX * 256, 128), BF16),
            pltpu.VMEM((LINES * 32, 128), BF16),
            pltpu.VMEM(z_face, BF16),
            pltpu.VMEM(z_face, BF16),
            pltpu.VMEM((LINES * 256, 128), BF16),
            pltpu.VMEM((LINES * 256, 128), BF16),
            pltpu.VMEM((LINES * 256, 128), BF16),
            pltpu.VMEM((LINES * 288, 128), BF16),
            pltpu.VMEM((CELLS * 64, 128), BF16),
            pltpu.VMEM((LINES * 64, 128), BF16),
            pltpu.VMEM((CELLS * 64, 128), BF16),
            pltpu.VMEM(((CELLS + BZ) * 64, 256), BF16),
            pltpu.VMEM((BY, 8 * STEP, 128), F32),
            pltpu.VMEM((BY, 8 * STEP_TWICE, 128), F32),
            pltpu.SemaphoreType.DMA((6,)),
            pltpu.SemaphoreType.DMA((6,)),
            pltpu.SemaphoreType.DMA((6,)),
            pltpu.SemaphoreType.DMA((6,)),
            pltpu.SemaphoreType.DMA((5 + 3 * BX,)),
        ],
        compiler_params=pltpu.CompilerParams(collective_id=0, has_side_effects=True, vmem_limit_bytes=63 << 20),
        name="inner",
    )(prolong, a_face, a_diag)


def compute_kernel(
    aggregate, slot, owner, *refs
):
    arrays, refs = refs[:14], refs[14:]
    small, couple_in, left_in = arrays[:6] + arrays[8:], arrays[6], arrays[7]
    send, held, refs = refs[0], refs[1:13], refs[13:]
    m_x, m_y, m_z, p_xp, p_yp, p_zp, right_x, right_y, right_z, face_x, face_y, face_z = held
    (
    small_sems, keys, key_work, key_sem, in_sems, right, left, couple, work_b,
    f_low, f_high, b_low, b_high, rows, absent, tally, sems, absent_sems,
    ) = refs
    fetched = [pltpu.make_async_copy(*pair, small_sems.at[k]) for k, pair in enumerate(zip(small, held))]
    for copy in fetched:
        copy.start()
    plane = BY * BZ * 64
    brought = []
    for x in range(BX):
        at = pl.ds(x * plane, plane)
        for k, (source, dest) in enumerate(((couple_in, couple), (left_in, left))):
            copy = pltpu.make_async_copy(source.at[at], dest.at[at], in_sems.at[x, k])
            copy.start()
            brought.append(copy)

    absent[...] = jnp.full(absent.shape, jnp.nan, BF16)
    marks = []
    for k in range(PLACES):
        mark = pltpu.make_async_copy(absent, send.at[:, pl.ds(k * ROW, 16)], absent_sems.at[k])
        mark.start()
        marks.append(mark)

    key_work[...] = aggregate[...][None] * SLOTS + slot[...]
    told_keys = pltpu.make_async_copy(key_work, keys, key_sem)
    told_keys.start()
    for ref in (f_low, f_high, b_low, b_high):
        ref[...] = jnp.zeros_like(ref)

    for copy in fetched:
        copy.wait()

    right_xp, right_yp, right_zp = 0, BY, BY + BX

    for count, after, base in ((BY, p_xp, right_xp), (BX, p_yp, right_yp)):

        for line in range(count):
            k = line
            spread_twice(after[line], work_b.at[k])
            store_right(right, base + line, work_b.at[k])

    @sweep(LINES, 12)
    def _(line, k):
        low = lane_low((32, 128))
        here = p_zp[pl.ds(pl.multiple_of(line * 32, 32), 32), :].astype(F32)
        turned = pltpu.roll(here, 64, axis=1)
        work = work_b.at[k % BY, pl.ds(k // BY * 64, 64)]
        work[pl.ds(0, 32, stride=2), :] = jnp.where(low, here, turned)
        work[pl.ds(1, 32, stride=2), :] = jnp.where(low, turned, here)
        at = pl.multiple_of((right_zp * 8 + line) * 64, 64)
        right[pl.ds(at, 64), :] = work[...].astype(BF16)

    told_keys.wait()

    def rim_terms(weights, cell, m, at, places):
        low = lane_low((64, 128))
        zero = jnp.zeros((64, 128), BF16)
        first, second = (weights[pl.ds(pl.multiple_of((cell + k) * 64, 64), 64), :] for k in range(2))
        weight = jnp.concatenate([jnp.where(low, first, zero), jnp.where(low, zero, second)], axis=0)
        out = jnp.dot(m[pl.ds(pl.multiple_of(at, 64), 64), :], weight, preferred_element_type=F32)
        b_low[places[0]] += out
        b_high[places[1]] += out

    @sweep(BY, 6)
    def _(y, _turn):
        for z in range(0, BZ, 2):
            rim_terms(right_x, y * BZ + z, m_x, y * 256 + z * 32, [keys[1, y, 0, z + k] for k in range(2)])

    @sweep(BX, 4)
    def _(x, _turn):
        for z in range(0, BZ, 2):
            rim_terms(right_y, x * BZ + z, m_y, x * 256 + z * 32, [keys[3, 0, x, z + k] for k in range(2)])

    @sweep(LINES // 2, 12)
    def _(half, _turn):
        line = half * 2
        places = [keys[5, line % BY + k, line // BY, 0] for k in range(2)]
        rim_terms(right_z, line, m_z, half * 64, places)

    for copy in brought:
        copy.wait()

    @sweep(BY, 6)
    def _(y, _turn):
        for z in range(0, BZ, 2):
            e = ((BX - 1) * BY + y) * BZ + z
            at = y * 256 + z * 32
            couples(right, (right_xp + y) * 8 + z, 1, couple, [(1, face_x, [at, at + 32], [e, e + 1])])

    @sweep(BX, 4)
    def _(x, _turn):
        for z in range(0, BZ, 2):
            e = (x * BY + BY - 1) * BZ + z
            at = x * 256 + z * 32
            couples(right, (right_yp + x) * 8 + z, 1, couple, [(2, face_y, [at, at + 32], [e, e + 1])])

    @sweep(LINES // 2, 12)
    def _(half, _turn):
        line = half * 2
        e = line * BZ + BZ - 1
        couples(right, right_zp * 8 + line, 1, couple, [(3, face_z, [line * 32, line * 32 + 32], [e, e + BZ])])

    def terms(cell, places):
        at = pl.multiple_of(cell * 64, 128)
        out = jnp.dot(left[pl.ds(at, 128), :], couple[pl.ds(at, 128), :], preferred_element_type=F32)
        for k in range(2):
            for f, (key_f, key_b) in places[k].items():
                tile = f // 2
                term = out[k * 64 : k * 64 + 64, tile * 128 : tile * 128 + 128]
                if key_f is not None:
                    (f_low, f_high)[f % 2][key_f] += term
                if key_b is not None:
                    (b_low, b_high)[f % 2][key_b] += term


    @sweep(LINES, 4)
    def _(line, _turn):
        x, y = line // BY, line % BY
        next_x, next_y = jnp.minimum(x + 1, BX - 1), jnp.minimum(y + 1, BY - 1)
        for z in range(0, BZ, 2):
            places = []
            for k in range(z, z + 2):
                onward_x = jnp.where(x < BX - 1, keys[1, y, next_x, k], KEYS)
                onward_y = jnp.where(y < BY - 1, keys[3, next_y, x, k], KEYS)
                places.append(
                    {
                        0: (keys[0, y, x, k], None),
                        1: (keys[2, y, x, k], onward_x),
                        2: (keys[4, y, x, k], onward_y),
                        3: (keys[6, y, x, k], keys[5, y, x, k + 1] if k < BZ - 1 else None),
                    }
                )
            terms(line * BZ + z, places)

    depth = send.shape[0]
    for copy in marks:
        copy.wait()

    for c in range(depth):
        tally[c] = 0

    def fold(r):
        low = lane_low((64, 128))
        for s in range(0, SLOTS, 4):
            blocks = []
            for k in (s, s + 2):
                at = [r * SLOTS + min(k + side, SLOTS - 1) for side in range(2)]
                pair = jnp.where(low, b_low[at[0]], b_high[at[1]])
                pair += pltpu.roll(jnp.where(low, b_low[at[1]], b_high[at[0]]), 64, axis=1)
                blocks.append(pair)
            flipped = jnp.concatenate(blocks, axis=0).T
            for k in range(s, min(s + 4, SLOTS)):
                ref = f_low if k < s + 2 else f_high
                ref[r * SLOTS + k] += flipped[k % 2 * 64 : k % 2 * 64 + 64]

    def lay_out(r):
        low_half = lane_low((32, 128))
        for s in range(SLOTS):
            parts = f_low.at[r * SLOTS + s], f_high.at[r * SLOTS + s]
            even, odd = ([ref[pl.ds(p, 32, stride=2), :] for ref in parts] for p in range(2))
            row = jnp.where(low_half, even[0], odd[1])
            row += pltpu.roll(jnp.where(low_half, odd[0], even[1]), 64, axis=1)
            rows[pl.ds(pl.multiple_of(r * ROW + s * 32, 32), 32), :] = row.astype(BF16)

    def hand_out(r):
        c = owner[r]
        place = tally[c]
        tally[c] = place + 1
        pltpu.make_async_copy(
            rows.at[pl.ds(pl.multiple_of(r * ROW, 32), ROW)],
            send.at[c, pl.ds(pl.multiple_of(place * ROW, 32), ROW)],
            sems.at[r],
        ).start()

    @pl.loop(0, AGG_DEV // 4)
    def _(turn):
        for step in (fold, lay_out, hand_out):
            for k in range(4):
                step(turn * 4 + k)

    for r in range(AGG_DEV):
        pltpu.make_async_copy(rows.at[pl.ds(0, ROW)], send.at[0, pl.ds(0, ROW)], sems.at[r]).wait()


def coarse_rows(aggregate, slot, owner, arrays, depth):
    smem = pl.BlockSpec(memory_space=pltpu.SMEM)
    vmem = pl.BlockSpec(memory_space=pltpu.VMEM)
    any_space = pl.BlockSpec(memory_space=pl.ANY)
    beyond = BY + BX + LINES // 8
    return pl.pallas_call(
        compute_kernel,
        out_shape=jax.ShapeDtypeStruct((depth, PACK, 128), BF16),
        in_specs=[vmem, vmem, smem] + [any_space] * len(arrays),
        out_specs=any_space,
        scratch_shapes=[pltpu.VMEM(array.shape, BF16) for array in arrays[:6] + arrays[8:]]
        + [
            pltpu.SemaphoreType.DMA((12,)),
            pltpu.SMEM((SLOTS, BY, BX, BZ), jnp.int32),
            pltpu.VMEM((SLOTS, BY, BX, BZ), jnp.int32),
            pltpu.SemaphoreType.DMA,
            pltpu.SemaphoreType.DMA((BX, 2)),
            pltpu.VMEM((beyond * 512, 128), BF16),
            pltpu.VMEM((CELLS * 64, 128), BF16),
            pltpu.VMEM((CELLS * 64, 256), BF16),
            pltpu.VMEM((BY, 8 * STEP_TWICE, 128), F32),
            pltpu.VMEM((KEYS + 1, 64, 128), F32),
            pltpu.VMEM((KEYS + 1, 64, 128), F32),
            pltpu.VMEM((KEYS + 1, 64, 128), F32),
            pltpu.VMEM((KEYS + 1, 64, 128), F32),
            pltpu.VMEM((AGG_DEV * ROW, 128), BF16),
            pltpu.VMEM((depth, 16, 128), BF16),
            pltpu.SMEM((depth,), jnp.int32),
            pltpu.SemaphoreType.DMA((AGG_DEV,)),
            pltpu.SemaphoreType.DMA((PLACES,)),
        ],
        compiler_params=pltpu.CompilerParams(vmem_limit_bytes=63 << 20),
        name="coarse_rows",
    )(aggregate, slot, owner, *arrays)


GROUP, ROW_STEP, ROW_PARTS = 8, ROW + 4, 4


def place_kernel(taken, out, told, counts, tally, source, held, works, shaped, sems, row_sems, out_sems):
    depth, count = taken.shape[0], out.shape[1]
    loads = [
        pltpu.make_async_copy(taken.at[:, pl.ds(k * ROW, 16)], told.at[k], sems.at[k]) for k in range(PLACES)
    ]
    for load in loads:
        load.start()
    part = depth // ROW_PARTS
    brought = []
    for k in range(ROW_PARTS):
        at = pl.ds(k * part, part)
        copy = pltpu.make_async_copy(taken.at[at], held.at[at], row_sems.at[k])
        copy.start()
        brought.append(copy)

    for load in loads:
        load.wait()
    for c in range(depth):
        here = [told[k, c, 0:1, :].astype(F32) for k in range(PLACES)]
        counts[c : c + 1, :] = sum((value == value).astype(jnp.int32) for value in here)
    move = pltpu.make_async_copy(counts, tally, sems.at[PLACES])
    move.start()
    move.wait()

    total = 0
    for c in range(depth):
        for k in range(PLACES):
            source[total + k] = c * PLACES + k
        total += tally[c, 0]

    for copy in brought:
        copy.wait()

    def out_copy(group):
        rows = pl.ds(pl.multiple_of(group * GROUP, GROUP), GROUP)
        return pltpu.make_async_copy(shaped.at[group], out.at[:, rows, :], out_sems.at[group])

    @sweep(count // GROUP, 2)
    def _(group, side):
        work = works.at[side]
        for k in range(GROUP):
            t = group * GROUP + k
            at = jnp.where(t < total, source[t], 0)
            place = pl.multiple_of(lax.rem(at, PLACES) * ROW, 32)
            row = held[at // PLACES, pl.ds(place, ROW), :].astype(F32)
            work[k * ROW_STEP : k * ROW_STEP + ROW, :] = jnp.where(t < total, row, jnp.zeros_like(row))
        for s in range(SLOTS):
            for tile in range(32):
                piece = work[pl.ds(s * 32 + tile, GROUP, stride=ROW_STEP), :]
                shaped[group, s, :, tile * 128 : tile * 128 + 128] = piece.astype(BF16)
        out_copy(group).start()

    for group in range(count // GROUP):
        out_copy(group).wait()


def place_rows(taken):
    depth = taken.shape[0]
    count = depth * PLACES
    any_space = pl.BlockSpec(memory_space=pl.ANY)
    return pl.pallas_call(
        place_kernel,
        out_shape=jax.ShapeDtypeStruct((SLOTS, count, NODES * NODES), BF16),
        in_specs=[any_space],
        out_specs=any_space,
        scratch_shapes=[
            pltpu.VMEM((PLACES, depth, 16, 128), BF16),
            pltpu.VMEM((depth, 128), jnp.int32),
            pltpu.SMEM((depth, 128), jnp.int32),
            pltpu.SMEM((count + PLACES,), jnp.int32),
            pltpu.VMEM((depth, PACK, 128), BF16),
            pltpu.VMEM((2, GROUP * ROW_STEP, 128), F32),
            pltpu.VMEM((count // GROUP, SLOTS, GROUP, NODES * NODES), BF16),
            pltpu.SemaphoreType.DMA((PLACES + 1,)),
            pltpu.SemaphoreType.DMA((ROW_PARTS,)),
            pltpu.SemaphoreType.DMA((count // GROUP,)),
        ],
        compiler_params=pltpu.CompilerParams(vmem_limit_bytes=63 << 20),
        name="place_rows",
    )(taken)


def shards(a_diag, a_face, prolong, aggregate, pair_slot, row_owner):
    block = a_diag.shape[-1]
    depth = lax.axis_size("gz")
    holding = PLACES * depth

    arrays = inner(prolong, a_face, a_diag)
    send = coarse_rows(
        aggregate.transpose(1, 0, 2), pair_slot.transpose(0, 2, 1, 3), row_owner, arrays, depth
    )
    taken = lax.all_to_all(send, "gz", 0, 0, tiled=True)
    coarse = place_rows(taken).transpose(1, 0, 2)
    return coarse.reshape(1, 1, 1, holding, SLOTS, block)


def solution(mesh):
    return jax.shard_map(
        shards,
        mesh=mesh,
        in_specs=(
            P("gx", "gy", "gz", None),
            P(None, "gx", "gy", "gz", None),
            P("gx", "gy", "gz", None),
            P("gx", "gy", "gz"),
            P(None, "gx", "gy", "gz"),
            P(("gx", "gy", "gz")),
        ),
        out_specs=P("gx", "gy", "gz", None, None, None),
        check_vma=False,
    )
```

```python
import jax
import jax.numpy as jnp
from jax import lax
from jax.experimental import pallas as pl
from jax.experimental.pallas import tpu as pltpu
from jax.sharding import PartitionSpec as P

NODES = 64
SLOTS = 7
AGG_DEV = 24
BX, BY, BZ = 4, 6, 8
LINES = BX * BY
PLACES = 2
ROW = SLOTS * NODES * NODES // 128
PACK = PLACES * ROW
KEYS = AGG_DEV * SLOTS
STEP, STEP_TWICE = 36, 68
F32 = jnp.float32
BF16 = jnp.bfloat16


def sweep(count, by):
    def run(body):
        @pl.loop(0, count // by)
        def _(turn):
            for k in range(by):
                body(turn * by + k, k)

    return run


def lane_low(shape):
    return lax.broadcasted_iota(jnp.int32, shape, 1) < 64


def spread(line, scratch):
    values = line.astype(F32)
    for tile in range(32):
        scratch[pl.ds(tile, 8, stride=STEP), :] = values[:, tile * 128 : tile * 128 + 128]


def spread_twice(line, natural):
    values = line.astype(F32)
    low = lane_low((8, 128))
    for tile in range(32):
        here = values[:, tile * 128 : tile * 128 + 128]
        swapped = pltpu.roll(here, 64, axis=1)
        natural[pl.ds(2 * tile, 8, stride=STEP_TWICE), :] = jnp.where(low, here, swapped)
        natural[pl.ds(2 * tile + 1, 8, stride=STEP_TWICE), :] = jnp.where(low, swapped, here)


MESH = pl.DeviceIdType.MESH


def couples(right, cell, stride, couple, blocks):
    low = lane_low((64, 128))
    zero = jnp.zeros((64, 128), BF16)
    wide = jnp.zeros((128, 128), BF16)
    columns = []
    for k in range(2):
        block = right[pl.ds(pl.multiple_of((cell + k * stride) * 64, 64), 64), :]
        corner = jnp.concatenate([jnp.where(low, block, zero), jnp.where(low, zero, block)], axis=0)
        columns.append(jnp.concatenate([corner, wide] if k == 0 else [wide, corner], axis=0))
    weight = jnp.concatenate(columns, axis=1)
    stack = [
        jnp.concatenate([ref[pl.ds(pl.multiple_of(at, 32), 32), :] for at in ats], axis=1)
        for _, ref, ats, _ in blocks
    ]
    stack = jnp.concatenate(stack, axis=0) if len(stack) > 1 else stack[0]
    both = jnp.dot(stack, weight, preferred_element_type=F32)
    for number, (f, _, _, cells) in enumerate(blocks):
        for k in range(2):
            part = both[number * 32 : number * 32 + 32, k * 128 : k * 128 + 128]
            turned = pltpu.roll(part, 64, axis=1)
            side = f % 2 * 64
            for p in range(2):
                value = (part if p == f % 2 else turned)[:, side : side + 64]
                at = pl.multiple_of(cells[k] * 64 + p * 32, 32)
                couple[pl.ds(at, 32), f * 64 : f * 64 + 64] = value.astype(BF16)


def store_spread(line, dest, base, work):
    spread(line, work)
    for z in range(8):
        at = pl.multiple_of(base + z * 32, 32)
        dest[pl.ds(at, 32), :] = work[z * STEP : z * STEP + 32, :].astype(BF16)


def store_right(right, base, work):
    for z in range(8):
        at = pl.multiple_of(base * 512 + z * 64, 64)
        right[pl.ds(at, 64), :] = work[z * STEP_TWICE : z * STEP_TWICE + 64, :].astype(BF16)


def store_left(left, base, work):
    low = lane_low((64, 128))
    zero = jnp.zeros((64, 128), F32)

    def by_parity(z):
        return jnp.concatenate([work[pl.ds(z * STEP_TWICE + p, 32, stride=2), :] for p in range(2)], axis=0)

    for pair in range(4):
        first, second = by_parity(2 * pair), by_parity(2 * pair + 1)
        block = jnp.concatenate([jnp.where(low, first, zero), jnp.where(low, zero, second)], axis=0)
        at = pl.multiple_of(base * 512 + pair * 128, 128)
        left[pl.ds(at, 128), :] = block.astype(BF16).T


CELLS = LINES * BZ


def inner_kernel(
    prolong, a_face, a_diag,
    m_x, m_y, m_z, p_xp, p_yp, p_zp,
    couple_out, left_out, right_x, right_y, right_z, face_x, face_y, face_z,
    in_p, in_d, in_f, zero, zero_m, out_mx, out_my, out_mz, out_az, out_p_first,
    ra_d, ra_x, ra_y, ra_z, right, first_z, left, couple, work_a, work_b,
    load_sems, send_sems, recv_sems, zero_sems, out_sems,
):
    depth = lax.axis_size("gz")
    gx, gy, gz = (lax.axis_index(axis) for axis in ("gx", "gy", "gz"))
    next_z, previous_z = lax.rem(gz + 1, depth), lax.rem(gz + depth - 1, depth)
    barrier = pltpu.get_barrier_semaphore()
    for target in ({"gx": 1 - gx}, {"gy": 1 - gy}, {"gz": next_z}, {"gz": previous_z}):
        pl.semaphore_signal(barrier, inc=1, device_id=target, device_id_type=MESH)
    last_x, inner_x, inner_y = pl.ds(BX - 1, 1), pl.ds(0, BX - 1), pl.ds(0, BY - 1)
    load_parts = (
        (prolong, in_p),
        (a_face.at[1, :, BY - 1], in_f.at[1, :, BY - 1]),
        (a_face.at[2], in_f.at[2]),
        (a_face.at[0, last_x], in_f.at[0, last_x]),
        (a_diag, in_d),
        (a_face.at[1, :, inner_y], in_f.at[1, :, inner_y]),
        (a_face.at[0, inner_x], in_f.at[0, inner_x]),
    )
    loads = [pltpu.make_async_copy(*part, load_sems.at[k]) for k, part in enumerate(load_parts)]
    for load in loads:
        load.start()
    zero[...] = jnp.zeros_like(zero)
    zero_m[...] = jnp.zeros_like(zero_m)

    def exchange(number, source, dest, target, sends, receives, blank):
        copy = pltpu.make_async_remote_copy(
            source, dest, send_sems.at[number], recv_sems.at[number], device_id=target, device_id_type=MESH
        )
        fill = pltpu.make_async_copy(blank, dest, zero_sems.at[number])

        @pl.when(sends)
        def _():
            copy.start()

        @pl.when(jnp.logical_not(receives))
        def _():
            fill.start()

        def finish():
            @pl.when(sends)
            def _():
                copy.wait_send()

            @pl.when(receives)
            def _():
                copy.wait_recv()

            @pl.when(jnp.logical_not(receives))
            def _():
                fill.wait()

        return finish

    def to_line(axis, step):
        here, count = lax.axis_index(axis), lax.axis_size(axis)
        return {axis: lax.rem(here + (step + count), count)}

    def has_line(axis, step):
        here, count = lax.axis_index(axis), lax.axis_size(axis)
        return here > 0 if step < 0 else here < count - 1

    def pass_up(number, axis, source, dest, blank):
        return exchange(number, source, dest, to_line(axis, 1), has_line(axis, 1), has_line(axis, -1), blank)

    def pass_down(number, axis, source, dest, blank):
        return exchange(number, source, dest, to_line(axis, -1), has_line(axis, -1), has_line(axis, 1), blank)

    def outgoing(work, pair, line):
        blocks = []
        for z in (2 * pair, 2 * pair + 1):
            block = work[z * STEP : z * STEP + 32, :]
            blocks += [block, pltpu.roll(block, 64, axis=1)]
        block = jnp.concatenate(blocks, axis=0).astype(BF16)
        at = pl.multiple_of(line * 512 + pair * 128, 128)
        return jnp.dot(left[pl.ds(at, 128), :], block, preferred_element_type=F32)

    def side_by_side(first, second):
        return jnp.where(lane_low((64, 128)), first, pltpu.roll(second, 64, axis=1)).astype(BF16)

    def face(f, count, out, line_of):
        for row in range(count):
            line = line_of(row)
            work = work_a.at[row]
            store_spread(in_f[f, line // BY, line % BY], (ra_x, ra_y)[f], line * 256, work)
            for pair in range(4):
                both = outgoing(work, pair, line)
                out[row * 256 + pair * 64 : row * 256 + pair * 64 + 64, :] = side_by_side(both[0:64], both[64:128])

    def factors(x, y, natural):
        line = x * BY + y
        at = pl.ds(pl.multiple_of(line * 32, 32), 32)
        spread_twice(in_p[x, y], natural)
        even, odd = (natural[pl.ds(p, 32, stride=2), :] for p in range(2))
        out_p_first[at, :] = jnp.where(lane_low((32, 128)), even, odd).astype(BF16)
        ra_z[pl.ds(pl.multiple_of(line * 288, 32), 32), :] = jnp.zeros((32, 128), BF16)
        store_right(right, line, natural)
        first_z[pl.ds(pl.multiple_of(line * 64, 64), 64), :] = natural[0:64, :].astype(BF16)
        store_left(left, line, natural)

    loads[0].wait()
    for x in range(BX):
        factors(x, BY - 1, work_b.at[x])
    loads[1].wait()
    face(1, BX, out_my, lambda k: k * BY + BY - 1)
    pl.semaphore_wait(barrier, 4)
    ends = [
        pass_up(3, "gy", out_my, m_y, zero_m.at[pl.ds(0, BX * 256)]),
        pass_down(0, "gy", prolong.at[:, 0], p_yp, zero.at[pl.ds(0, BX)]),
        pass_down(1, "gx", prolong.at[0], p_xp, zero),
    ]

    @pl.loop(0, BX)
    def _(x):
        for y in range(BY - 1):
            factors(x, y, work_b.at[y])

    ends.append(pass_down(2, "gz", out_p_first, p_zp, zero_m.at[pl.ds(0, LINES * 32)]))
    loads[2].wait()

    @pl.loop(0, BX)
    def _(x):
        for y in range(0, BY, 2):
            last = []
            for k in range(2):
                line = x * BY + y + k
                work = work_a.at[y + k]
                store_spread(in_f[2, x, y + k], ra_z, line * 288 + 32, work)
                at = pl.ds(pl.multiple_of(line * 32, 32), 32)
                out_az[at, :] = work[(BZ - 1) * STEP : (BZ - 1) * STEP + 32, :].astype(BF16)
                last.append(outgoing(work, BZ // 2 - 1, line)[64:128])
            at = pl.multiple_of((x * BY + y) * 32, 64)
            out_mz[pl.ds(at, 64), :] = side_by_side(*last)

    ends.append(pass_up(4, "gz", out_mz, m_z, zero_m.at[pl.ds(0, LINES * 32)]))
    loads[3].wait()
    face(0, BY, out_mx, lambda k: (BX - 1) * BY + k)
    ends.append(pass_up(5, "gx", out_mx, m_x, zero_m))
    for load in loads[4:]:
        load.wait()

    @pl.loop(0, BX)
    def _(x):
        for y in range(BY):
            store_spread(in_d[x, y], ra_d, (x * BY + y) * 256, work_a.at[y])
        for y in range(BY - 1):
            store_spread(in_f[1, x, y], ra_y, (x * BY + y) * 256, work_a.at[y])

    @pl.loop(0, BX - 1)
    def _(x):
        for y in range(BY):
            store_spread(in_f[0, x, y], ra_x, (x * BY + y) * 256, work_a.at[y])

    moves = []

    def put(source, dest):
        copy = pltpu.make_async_copy(source, dest, out_sems.at[len(moves)])
        copy.start()
        moves.append(copy)

    put(left, left_out)
    put(right.at[pl.ds(0, BY * 512)], right_x)
    put(first_z, right_z)
    put(ra_x.at[pl.ds((LINES - BY) * 256, BY * 256)], face_x)
    put(out_az, face_z)
    for x in range(BX):
        put(right.at[pl.ds(x * BY * 512, 512)], right_y.at[pl.ds(x * 512, 512)])
        put(ra_y.at[pl.ds((x * BY + BY - 1) * 256, 256)], face_y.at[pl.ds(x * 256, 256)])

    for x in range(BX):

        @pl.loop(0, 2)
        def _(half):
            for k in range(BY // 2):
                y = half * (BY // 2) + k
                line = x * BY + y
                from_y = jnp.where(y > 0, line - 1, line)
                into_y = jnp.where(y > 0, (line - 1) * BZ, CELLS)
                for z in range(0, BZ, 2):
                    n = line * BZ + z
                    both = range(2)
                    blocks = [
                        (0, ra_d, [(n + k) * 32 for k in both], [n, n + 1]),
                        (2, ra_y, [from_y * 256 + (z + k) * 32 for k in both], [into_y + z, into_y + z + 1]),
                        (3, ra_z, [line * 288 + (z + k) * 32 for k in both], [CELLS if z == 0 else n - 1, n]),
                    ]
                    if x > 0:
                        e = n - BY * BZ
                        blocks.append((1, ra_x, [(e + k) * 32 for k in both], [e, e + 1]))
                    couples(right, n, 1, couple, blocks)

        if x > 0:
            rows = pl.ds((x - 1) * BY * BZ * 64, BY * BZ * 64)
            put(couple.at[rows], couple_out.at[rows])
    rows = pl.ds((BX - 1) * BY * BZ * 64, BY * BZ * 64)
    put(couple.at[rows], couple_out.at[rows])
    for finish in ends:
        finish()
    for copy in moves:
        copy.wait()


def inner(prolong, a_face, a_diag):
    any_space = pl.BlockSpec(memory_space=pl.ANY)
    x_face, y_face, z_face = (BY, BZ, NODES * NODES), (BX, BZ, NODES * NODES), (LINES * 32, 128)
    shapes = (
        (BY * 256, 128), (BX * 256, 128), (LINES * 32, 128), x_face, y_face, z_face,
        (CELLS * 64, 256), (CELLS * 64, 128),
        (BY * 512, 128), (BX * 512, 128), (LINES * 64, 128),
        (BY * 256, 128), (BX * 256, 128), z_face,
    )
    return pl.pallas_call(
        inner_kernel,
        out_shape=[jax.ShapeDtypeStruct(shape, BF16) for shape in shapes],
        in_specs=[any_space] * 3,
        out_specs=[any_space] * len(shapes),
        scratch_shapes=[
            pltpu.VMEM(prolong.shape, BF16),
            pltpu.VMEM(a_diag.shape, BF16),
            pltpu.VMEM(a_face.shape, BF16),
            pltpu.VMEM(x_face, BF16),
            pltpu.VMEM((BY * 256, 128), BF16),
            pltpu.VMEM((BY * 256, 128), BF16),
            pltpu.VMEM((BX * 256, 128), BF16),
            pltpu.VMEM((LINES * 32, 128), BF16),
            pltpu.VMEM(z_face, BF16),
            pltpu.VMEM(z_face, BF16),
            pltpu.VMEM((LINES * 256, 128), BF16),
            pltpu.VMEM((LINES * 256, 128), BF16),
            pltpu.VMEM((LINES * 256, 128), BF16),
            pltpu.VMEM((LINES * 288, 128), BF16),
            pltpu.VMEM((CELLS * 64, 128), BF16),
            pltpu.VMEM((LINES * 64, 128), BF16),
            pltpu.VMEM((CELLS * 64, 128), BF16),
            pltpu.VMEM(((CELLS + BZ) * 64, 256), BF16),
            pltpu.VMEM((BY, 8 * STEP, 128), F32),
            pltpu.VMEM((BY, 8 * STEP_TWICE, 128), F32),
            pltpu.SemaphoreType.DMA((7,)),
            pltpu.SemaphoreType.DMA((6,)),
            pltpu.SemaphoreType.DMA((6,)),
            pltpu.SemaphoreType.DMA((6,)),
            pltpu.SemaphoreType.DMA((5 + 3 * BX,)),
        ],
        compiler_params=pltpu.CompilerParams(collective_id=0, has_side_effects=True, vmem_limit_bytes=63 << 20),
        name="inner",
    )(prolong, a_face, a_diag)


def compute_kernel(
    aggregate, slot, owner, *refs
):
    arrays, refs = refs[:14], refs[14:]
    small, couple_in, left_in = arrays[:6] + arrays[8:], arrays[6], arrays[7]
    send, held, refs = refs[0], refs[1:13], refs[13:]
    m_x, m_y, m_z, p_xp, p_yp, p_zp, right_x, right_y, right_z, face_x, face_y, face_z = held
    (
    small_sems, keys, key_work, key_sem, in_sems, right, left, couple, work_b,
    f_low, f_high, b_low, b_high, rows, absent, tally, sems, absent_sems,
    ) = refs
    fetched = [pltpu.make_async_copy(*pair, small_sems.at[k]) for k, pair in enumerate(zip(small, held))]
    for copy in fetched:
        copy.start()
    plane = BY * BZ * 64
    brought = []
    for x in range(BX):
        at = pl.ds(x * plane, plane)
        for k, (source, dest) in enumerate(((couple_in, couple), (left_in, left))):
            copy = pltpu.make_async_copy(source.at[at], dest.at[at], in_sems.at[x, k])
            copy.start()
            brought.append(copy)

    absent[...] = jnp.full(absent.shape, jnp.nan, BF16)
    marks = []
    for k in range(PLACES):
        mark = pltpu.make_async_copy(absent, send.at[:, pl.ds(k * ROW, 16)], absent_sems.at[k])
        mark.start()
        marks.append(mark)

    key_work[...] = aggregate[...][None] * SLOTS + slot[...]
    told_keys = pltpu.make_async_copy(key_work, keys, key_sem)
    told_keys.start()
    for ref in (f_low, f_high, b_low, b_high):
        ref[...] = jnp.zeros_like(ref)

    for copy in fetched:
        copy.wait()

    right_xp, right_yp, right_zp = 0, BY, BY + BX

    for count, after, base in ((BY, p_xp, right_xp), (BX, p_yp, right_yp)):

        for line in range(count):
            k = line
            spread_twice(after[line], work_b.at[k])
            store_right(right, base + line, work_b.at[k])

    @sweep(LINES, 12)
    def _(line, k):
        low = lane_low((32, 128))
        here = p_zp[pl.ds(pl.multiple_of(line * 32, 32), 32), :].astype(F32)
        turned = pltpu.roll(here, 64, axis=1)
        work = work_b.at[k % BY, pl.ds(k // BY * 64, 64)]
        work[pl.ds(0, 32, stride=2), :] = jnp.where(low, here, turned)
        work[pl.ds(1, 32, stride=2), :] = jnp.where(low, turned, here)
        at = pl.multiple_of((right_zp * 8 + line) * 64, 64)
        right[pl.ds(at, 64), :] = work[...].astype(BF16)

    told_keys.wait()

    def rim_terms(weights, cell, m, at, places):
        low = lane_low((64, 128))
        zero = jnp.zeros((64, 128), BF16)
        first, second = (weights[pl.ds(pl.multiple_of((cell + k) * 64, 64), 64), :] for k in range(2))
        weight = jnp.concatenate([jnp.where(low, first, zero), jnp.where(low, zero, second)], axis=0)
        out = jnp.dot(m[pl.ds(pl.multiple_of(at, 64), 64), :], weight, preferred_element_type=F32)
        b_low[places[0]] += out
        b_high[places[1]] += out

    @sweep(BY, 6)
    def _(y, _turn):
        for z in range(0, BZ, 2):
            rim_terms(right_x, y * BZ + z, m_x, y * 256 + z * 32, [keys[1, y, 0, z + k] for k in range(2)])

    @sweep(BX, 4)
    def _(x, _turn):
        for z in range(0, BZ, 2):
            rim_terms(right_y, x * BZ + z, m_y, x * 256 + z * 32, [keys[3, 0, x, z + k] for k in range(2)])

    @sweep(LINES // 2, 12)
    def _(half, _turn):
        line = half * 2
        places = [keys[5, line % BY + k, line // BY, 0] for k in range(2)]
        rim_terms(right_z, line, m_z, half * 64, places)

    for copy in brought:
        copy.wait()

    @sweep(BY, 6)
    def _(y, _turn):
        for z in range(0, BZ, 2):
            e = ((BX - 1) * BY + y) * BZ + z
            at = y * 256 + z * 32
            couples(right, (right_xp + y) * 8 + z, 1, couple, [(1, face_x, [at, at + 32], [e, e + 1])])

    @sweep(BX, 4)
    def _(x, _turn):
        for z in range(0, BZ, 2):
            e = (x * BY + BY - 1) * BZ + z
            at = x * 256 + z * 32
            couples(right, (right_yp + x) * 8 + z, 1, couple, [(2, face_y, [at, at + 32], [e, e + 1])])

    @sweep(LINES // 2, 12)
    def _(half, _turn):
        line = half * 2
        e = line * BZ + BZ - 1
        couples(right, right_zp * 8 + line, 1, couple, [(3, face_z, [line * 32, line * 32 + 32], [e, e + BZ])])

    def terms(cell, places):
        at = pl.multiple_of(cell * 64, 128)
        out = jnp.dot(left[pl.ds(at, 128), :], couple[pl.ds(at, 128), :], preferred_element_type=F32)
        for k in range(2):
            for f, (key_f, key_b) in places[k].items():
                tile = f // 2
                term = out[k * 64 : k * 64 + 64, tile * 128 : tile * 128 + 128]
                if key_f is not None:
                    (f_low, f_high)[f % 2][key_f] += term
                if key_b is not None:
                    (b_low, b_high)[f % 2][key_b] += term


    @sweep(LINES, 4)
    def _(line, _turn):
        x, y = line // BY, line % BY
        next_x, next_y = jnp.minimum(x + 1, BX - 1), jnp.minimum(y + 1, BY - 1)
        for z in range(0, BZ, 2):
            places = []
            for k in range(z, z + 2):
                onward_x = jnp.where(x < BX - 1, keys[1, y, next_x, k], KEYS)
                onward_y = jnp.where(y < BY - 1, keys[3, next_y, x, k], KEYS)
                places.append(
                    {
                        0: (keys[0, y, x, k], None),
                        1: (keys[2, y, x, k], onward_x),
                        2: (keys[4, y, x, k], onward_y),
                        3: (keys[6, y, x, k], keys[5, y, x, k + 1] if k < BZ - 1 else None),
                    }
                )
            terms(line * BZ + z, places)

    depth = send.shape[0]
    for copy in marks:
        copy.wait()

    for c in range(depth):
        tally[c] = 0

    def fold(r):
        low = lane_low((64, 128))
        for s in range(0, SLOTS, 4):
            blocks = []
            for k in (s, s + 2):
                at = [r * SLOTS + min(k + side, SLOTS - 1) for side in range(2)]
                pair = jnp.where(low, b_low[at[0]], b_high[at[1]])
                pair += pltpu.roll(jnp.where(low, b_low[at[1]], b_high[at[0]]), 64, axis=1)
                blocks.append(pair)
            flipped = jnp.concatenate(blocks, axis=0).T
            for k in range(s, min(s + 4, SLOTS)):
                ref = f_low if k < s + 2 else f_high
                ref[r * SLOTS + k] += flipped[k % 2 * 64 : k % 2 * 64 + 64]

    def lay_out(r):
        low_half = lane_low((32, 128))
        for s in range(SLOTS):
            parts = f_low.at[r * SLOTS + s], f_high.at[r * SLOTS + s]
            even, odd = ([ref[pl.ds(p, 32, stride=2), :] for ref in parts] for p in range(2))
            row = jnp.where(low_half, even[0], odd[1])
            row += pltpu.roll(jnp.where(low_half, odd[0], even[1]), 64, axis=1)
            rows[pl.ds(pl.multiple_of(r * ROW + s * 32, 32), 32), :] = row.astype(BF16)

    def hand_out(r):
        c = owner[r]
        place = tally[c]
        tally[c] = place + 1
        pltpu.make_async_copy(
            rows.at[pl.ds(pl.multiple_of(r * ROW, 32), ROW)],
            send.at[c, pl.ds(pl.multiple_of(place * ROW, 32), ROW)],
            sems.at[r],
        ).start()

    @pl.loop(0, AGG_DEV // 4)
    def _(turn):
        for step in (fold, lay_out, hand_out):
            for k in range(4):
                step(turn * 4 + k)

    for r in range(AGG_DEV):
        pltpu.make_async_copy(rows.at[pl.ds(0, ROW)], send.at[0, pl.ds(0, ROW)], sems.at[r]).wait()


def coarse_rows(aggregate, slot, owner, arrays, depth):
    smem = pl.BlockSpec(memory_space=pltpu.SMEM)
    vmem = pl.BlockSpec(memory_space=pltpu.VMEM)
    any_space = pl.BlockSpec(memory_space=pl.ANY)
    beyond = BY + BX + LINES // 8
    return pl.pallas_call(
        compute_kernel,
        out_shape=jax.ShapeDtypeStruct((depth, PACK, 128), BF16),
        in_specs=[vmem, vmem, smem] + [any_space] * len(arrays),
        out_specs=any_space,
        scratch_shapes=[pltpu.VMEM(array.shape, BF16) for array in arrays[:6] + arrays[8:]]
        + [
            pltpu.SemaphoreType.DMA((12,)),
            pltpu.SMEM((SLOTS, BY, BX, BZ), jnp.int32),
            pltpu.VMEM((SLOTS, BY, BX, BZ), jnp.int32),
            pltpu.SemaphoreType.DMA,
            pltpu.SemaphoreType.DMA((BX, 2)),
            pltpu.VMEM((beyond * 512, 128), BF16),
            pltpu.VMEM((CELLS * 64, 128), BF16),
            pltpu.VMEM((CELLS * 64, 256), BF16),
            pltpu.VMEM((BY, 8 * STEP_TWICE, 128), F32),
            pltpu.VMEM((KEYS + 1, 64, 128), F32),
            pltpu.VMEM((KEYS + 1, 64, 128), F32),
            pltpu.VMEM((KEYS + 1, 64, 128), F32),
            pltpu.VMEM((KEYS + 1, 64, 128), F32),
            pltpu.VMEM((AGG_DEV * ROW, 128), BF16),
            pltpu.VMEM((depth, 16, 128), BF16),
            pltpu.SMEM((depth,), jnp.int32),
            pltpu.SemaphoreType.DMA((AGG_DEV,)),
            pltpu.SemaphoreType.DMA((PLACES,)),
        ],
        compiler_params=pltpu.CompilerParams(vmem_limit_bytes=63 << 20),
        name="coarse_rows",
    )(aggregate, slot, owner, *arrays)


GROUP, ROW_STEP, ROW_PARTS = 8, ROW + 4, 4


def place_kernel(taken, out, told, counts, tally, source, held, works, shaped, sems, row_sems, out_sems):
    depth, count = taken.shape[0], out.shape[1]
    loads = [
        pltpu.make_async_copy(taken.at[:, pl.ds(k * ROW, 16)], told.at[k], sems.at[k]) for k in range(PLACES)
    ]
    for load in loads:
        load.start()
    part = depth // ROW_PARTS
    brought = []
    for k in range(ROW_PARTS):
        at = pl.ds(k * part, part)
        copy = pltpu.make_async_copy(taken.at[at], held.at[at], row_sems.at[k])
        copy.start()
        brought.append(copy)

    for load in loads:
        load.wait()
    for c in range(depth):
        here = [told[k, c, 0:1, :].astype(F32) for k in range(PLACES)]
        counts[c : c + 1, :] = sum((value == value).astype(jnp.int32) for value in here)
    move = pltpu.make_async_copy(counts, tally, sems.at[PLACES])
    move.start()
    move.wait()

    total = 0
    for c in range(depth):
        for k in range(PLACES):
            source[total + k] = c * PLACES + k
        total += tally[c, 0]

    for copy in brought:
        copy.wait()

    def out_copy(group):
        rows = pl.ds(pl.multiple_of(group * GROUP, GROUP), GROUP)
        return pltpu.make_async_copy(shaped.at[group], out.at[:, rows, :], out_sems.at[group])

    @sweep(count // GROUP, 2)
    def _(group, side):
        work = works.at[side]
        for k in range(GROUP):
            t = group * GROUP + k
            at = jnp.where(t < total, source[t], 0)
            place = pl.multiple_of(lax.rem(at, PLACES) * ROW, 32)
            row = held[at // PLACES, pl.ds(place, ROW), :].astype(F32)
            work[k * ROW_STEP : k * ROW_STEP + ROW, :] = jnp.where(t < total, row, jnp.zeros_like(row))
        for s in range(SLOTS):
            for tile in range(32):
                piece = work[pl.ds(s * 32 + tile, GROUP, stride=ROW_STEP), :]
                shaped[group, s, :, tile * 128 : tile * 128 + 128] = piece.astype(BF16)
        out_copy(group).start()

    for group in range(count // GROUP):
        out_copy(group).wait()


def place_rows(taken):
    depth = taken.shape[0]
    count = depth * PLACES
    any_space = pl.BlockSpec(memory_space=pl.ANY)
    return pl.pallas_call(
        place_kernel,
        out_shape=jax.ShapeDtypeStruct((SLOTS, count, NODES * NODES), BF16),
        in_specs=[any_space],
        out_specs=any_space,
        scratch_shapes=[
            pltpu.VMEM((PLACES, depth, 16, 128), BF16),
            pltpu.VMEM((depth, 128), jnp.int32),
            pltpu.SMEM((depth, 128), jnp.int32),
            pltpu.SMEM((count + PLACES,), jnp.int32),
            pltpu.VMEM((depth, PACK, 128), BF16),
            pltpu.VMEM((2, GROUP * ROW_STEP, 128), F32),
            pltpu.VMEM((count // GROUP, SLOTS, GROUP, NODES * NODES), BF16),
            pltpu.SemaphoreType.DMA((PLACES + 1,)),
            pltpu.SemaphoreType.DMA((ROW_PARTS,)),
            pltpu.SemaphoreType.DMA((count // GROUP,)),
        ],
        compiler_params=pltpu.CompilerParams(vmem_limit_bytes=63 << 20),
        name="place_rows",
    )(taken)


def shards(a_diag, a_face, prolong, aggregate, pair_slot, row_owner):
    block = a_diag.shape[-1]
    depth = lax.axis_size("gz")
    holding = PLACES * depth

    arrays = inner(prolong, a_face, a_diag)
    send = coarse_rows(
        aggregate.transpose(1, 0, 2), pair_slot.transpose(0, 2, 1, 3), row_owner, arrays, depth
    )
    taken = lax.all_to_all(send, "gz", 0, 0, tiled=True)
    coarse = place_rows(taken).transpose(1, 0, 2)
    return coarse.reshape(1, 1, 1, holding, SLOTS, block)


def solution(mesh):
    return jax.shard_map(
        shards,
        mesh=mesh,
        in_specs=(
            P("gx", "gy", "gz", None),
            P(None, "gx", "gy", "gz", None),
            P("gx", "gy", "gz", None),
            P("gx", "gy", "gz"),
            P(None, "gx", "gy", "gz"),
            P(("gx", "gy", "gz")),
        ),
        out_specs=P("gx", "gy", "gz", None, None, None),
        check_vma=False,
    )
```

```python
import jax
import jax.numpy as jnp
from jax import lax
from jax.experimental import pallas as pl
from jax.experimental.pallas import tpu as pltpu
from jax.sharding import PartitionSpec as P

NODES = 64
SLOTS = 7
AGG_DEV = 24
BX, BY, BZ = 4, 6, 8
LINES = BX * BY
PLACES = 2
ROW = SLOTS * NODES * NODES // 128
PACK = PLACES * ROW
KEYS = AGG_DEV * SLOTS
STEP, STEP_TWICE = 36, 68
F32 = jnp.float32
BF16 = jnp.bfloat16


def sweep(count, by):
    def run(body):
        @pl.loop(0, count // by)
        def _(turn):
            for k in range(by):
                body(turn * by + k, k)

    return run


def lane_low(shape):
    return lax.broadcasted_iota(jnp.int32, shape, 1) < 64


def spread(line, scratch):
    values = line.astype(F32)
    for tile in range(32):
        scratch[pl.ds(tile, 8, stride=STEP), :] = values[:, tile * 128 : tile * 128 + 128]


def spread_twice(line, natural):
    values = line.astype(F32)
    low = lane_low((8, 128))
    for tile in range(32):
        here = values[:, tile * 128 : tile * 128 + 128]
        swapped = pltpu.roll(here, 64, axis=1)
        natural[pl.ds(2 * tile, 8, stride=STEP_TWICE), :] = jnp.where(low, here, swapped)
        natural[pl.ds(2 * tile + 1, 8, stride=STEP_TWICE), :] = jnp.where(low, swapped, here)


MESH = pl.DeviceIdType.MESH


def couples(right, cell, stride, couple, blocks):
    low = lane_low((64, 128))
    zero = jnp.zeros((64, 128), BF16)
    for k in range(2):
        block = right[pl.ds(pl.multiple_of((cell + k * stride) * 64, 64), 64), :]
        weight = jnp.concatenate([jnp.where(low, block, zero), jnp.where(low, zero, block)], axis=0)
        stack = [ref[pl.ds(pl.multiple_of(ats[k], 32), 32), :] for _, ref, ats, _ in blocks]
        stack = jnp.concatenate(stack, axis=0) if len(stack) > 1 else stack[0]
        both = jnp.dot(stack, weight, preferred_element_type=F32)
        for number, (f, _, _, cells) in enumerate(blocks):
            part = both[number * 32 : number * 32 + 32]
            turned = pltpu.roll(part, 64, axis=1)
            side = f % 2 * 64
            for p in range(2):
                value = (part if p == f % 2 else turned)[:, side : side + 64]
                at = pl.multiple_of(cells[k] * 64 + p * 32, 32)
                couple[pl.ds(at, 32), f * 64 : f * 64 + 64] = value.astype(BF16)


def store_spread(line, dest, base, work):
    spread(line, work)
    for z in range(8):
        at = pl.multiple_of(base + z * 32, 32)
        dest[pl.ds(at, 32), :] = work[z * STEP : z * STEP + 32, :].astype(BF16)


def store_right(right, base, work):
    for z in range(8):
        at = pl.multiple_of(base * 512 + z * 64, 64)
        right[pl.ds(at, 64), :] = work[z * STEP_TWICE : z * STEP_TWICE + 64, :].astype(BF16)


def store_left(left, base, work):
    low = lane_low((64, 128))
    zero = jnp.zeros((64, 128), F32)

    def by_parity(z):
        return jnp.concatenate([work[pl.ds(z * STEP_TWICE + p, 32, stride=2), :] for p in range(2)], axis=0)

    for pair in range(4):
        first, second = by_parity(2 * pair), by_parity(2 * pair + 1)
        block = jnp.concatenate([jnp.where(low, first, zero), jnp.where(low, zero, second)], axis=0)
        at = pl.multiple_of(base * 512 + pair * 128, 128)
        left[pl.ds(at, 128), :] = block.astype(BF16).T


CELLS = LINES * BZ


def inner_kernel(
    prolong, a_face, a_diag,
    m_x, m_y, m_z, p_xp, p_yp, p_zp,
    couple_out, left_out, right_x, right_y, right_z, face_x, face_y, face_z,
    in_p, in_d, in_f, zero, zero_m, out_mx, out_my, out_mz, out_az, out_p_first,
    ra_d, ra_x, ra_y, ra_z, right, first_z, left, couple, work_a, work_b,
    load_sems, send_sems, recv_sems, zero_sems, out_sems,
):
    depth = lax.axis_size("gz")
    gx, gy, gz = (lax.axis_index(axis) for axis in ("gx", "gy", "gz"))
    next_z, previous_z = lax.rem(gz + 1, depth), lax.rem(gz + depth - 1, depth)
    barrier = pltpu.get_barrier_semaphore()
    for target in ({"gx": 1 - gx}, {"gy": 1 - gy}, {"gz": next_z}, {"gz": previous_z}):
        pl.semaphore_signal(barrier, inc=1, device_id=target, device_id_type=MESH)
    last_x, inner_x, inner_y = pl.ds(BX - 1, 1), pl.ds(0, BX - 1), pl.ds(0, BY - 1)
    load_parts = (
        (prolong.at[:, BY - 1], in_p.at[:, BY - 1]),
        (a_face.at[1, :, BY - 1], in_f.at[1, :, BY - 1]),
        (prolong.at[:, inner_y], in_p.at[:, inner_y]),
        (a_face.at[2], in_f.at[2]),
        (a_face.at[0, last_x], in_f.at[0, last_x]),
        (a_diag, in_d),
        (a_face.at[1, :, inner_y], in_f.at[1, :, inner_y]),
        (a_face.at[0, inner_x], in_f.at[0, inner_x]),
    )
    loads = [pltpu.make_async_copy(*part, load_sems.at[k]) for k, part in enumerate(load_parts)]
    for load in loads:
        load.start()
    zero[...] = jnp.zeros_like(zero)
    zero_m[...] = jnp.zeros_like(zero_m)

    def exchange(number, source, dest, target, sends, receives, blank):
        copy = pltpu.make_async_remote_copy(
            source, dest, send_sems.at[number], recv_sems.at[number], device_id=target, device_id_type=MESH
        )
        fill = pltpu.make_async_copy(blank, dest, zero_sems.at[number])

        @pl.when(sends)
        def _():
            copy.start()

        @pl.when(jnp.logical_not(receives))
        def _():
            fill.start()

        def finish():
            @pl.when(sends)
            def _():
                copy.wait_send()

            @pl.when(receives)
            def _():
                copy.wait_recv()

            @pl.when(jnp.logical_not(receives))
            def _():
                fill.wait()

        return finish

    def to_line(axis, step):
        here, count = lax.axis_index(axis), lax.axis_size(axis)
        return {axis: lax.rem(here + (step + count), count)}

    def has_line(axis, step):
        here, count = lax.axis_index(axis), lax.axis_size(axis)
        return here > 0 if step < 0 else here < count - 1

    def pass_up(number, axis, source, dest, blank):
        return exchange(number, source, dest, to_line(axis, 1), has_line(axis, 1), has_line(axis, -1), blank)

    def pass_down(number, axis, source, dest, blank):
        return exchange(number, source, dest, to_line(axis, -1), has_line(axis, -1), has_line(axis, 1), blank)

    def outgoing(work, pair, line):
        blocks = []
        for z in (2 * pair, 2 * pair + 1):
            block = work[z * STEP : z * STEP + 32, :]
            blocks += [block, pltpu.roll(block, 64, axis=1)]
        block = jnp.concatenate(blocks, axis=0).astype(BF16)
        at = pl.multiple_of(line * 512 + pair * 128, 128)
        return jnp.dot(left[pl.ds(at, 128), :], block, preferred_element_type=F32)

    def side_by_side(first, second):
        return jnp.where(lane_low((64, 128)), first, pltpu.roll(second, 64, axis=1)).astype(BF16)

    def face(f, count, out, line_of):
        for row in range(count):
            line = line_of(row)
            work = work_a.at[row]
            store_spread(in_f[f, line // BY, line % BY], (ra_x, ra_y)[f], line * 256, work)
            for pair in range(4):
                both = outgoing(work, pair, line)
                out[row * 256 + pair * 64 : row * 256 + pair * 64 + 64, :] = side_by_side(both[0:64], both[64:128])

    def factors(x, y, natural):
        line = x * BY + y
        at = pl.ds(pl.multiple_of(line * 32, 32), 32)
        spread_twice(in_p[x, y], natural)
        even, odd = (natural[pl.ds(p, 32, stride=2), :] for p in range(2))
        out_p_first[at, :] = jnp.where(lane_low((32, 128)), even, odd).astype(BF16)
        ra_z[pl.ds(pl.multiple_of(line * 288, 32), 32), :] = jnp.zeros((32, 128), BF16)
        store_right(right, line, natural)
        first_z[pl.ds(pl.multiple_of(line * 64, 64), 64), :] = natural[0:64, :].astype(BF16)
        store_left(left, line, natural)

    loads[0].wait()
    for x in range(BX):
        factors(x, BY - 1, work_b.at[x])
    loads[1].wait()
    face(1, BX, out_my, lambda k: k * BY + BY - 1)
    pl.semaphore_wait(barrier, 4)
    ends = [
        pass_up(3, "gy", out_my, m_y, zero_m.at[pl.ds(0, BX * 256)]),
        pass_down(0, "gy", prolong.at[:, 0], p_yp, zero.at[pl.ds(0, BX)]),
        pass_down(1, "gx", prolong.at[0], p_xp, zero),
    ]

    loads[2].wait()

    @pl.loop(0, BX)
    def _(x):
        for y in range(BY - 1):
            factors(x, y, work_b.at[y])

    ends.append(pass_down(2, "gz", out_p_first, p_zp, zero_m.at[pl.ds(0, LINES * 32)]))
    loads[3].wait()

    @pl.loop(0, BX)
    def _(x):
        for y in range(0, BY, 2):
            last = []
            for k in range(2):
                line = x * BY + y + k
                work = work_a.at[y + k]
                store_spread(in_f[2, x, y + k], ra_z, line * 288 + 32, work)
                at = pl.ds(pl.multiple_of(line * 32, 32), 32)
                out_az[at, :] = work[(BZ - 1) * STEP : (BZ - 1) * STEP + 32, :].astype(BF16)
                last.append(outgoing(work, BZ // 2 - 1, line)[64:128])
            at = pl.multiple_of((x * BY + y) * 32, 64)
            out_mz[pl.ds(at, 64), :] = side_by_side(*last)

    ends.append(pass_up(4, "gz", out_mz, m_z, zero_m.at[pl.ds(0, LINES * 32)]))
    loads[4].wait()
    face(0, BY, out_mx, lambda k: (BX - 1) * BY + k)
    ends.append(pass_up(5, "gx", out_mx, m_x, zero_m))
    for load in loads[5:]:
        load.wait()

    @pl.loop(0, BX)
    def _(x):
        for y in range(BY):
            store_spread(in_d[x, y], ra_d, (x * BY + y) * 256, work_a.at[y])
        for y in range(BY - 1):
            store_spread(in_f[1, x, y], ra_y, (x * BY + y) * 256, work_a.at[y])

    @pl.loop(0, BX - 1)
    def _(x):
        for y in range(BY):
            store_spread(in_f[0, x, y], ra_x, (x * BY + y) * 256, work_a.at[y])

    moves = []

    def put(source, dest):
        copy = pltpu.make_async_copy(source, dest, out_sems.at[len(moves)])
        copy.start()
        moves.append(copy)

    put(left, left_out)
    put(right.at[pl.ds(0, BY * 512)], right_x)
    put(first_z, right_z)
    put(ra_x.at[pl.ds((LINES - BY) * 256, BY * 256)], face_x)
    put(out_az, face_z)
    for x in range(BX):
        put(right.at[pl.ds(x * BY * 512, 512)], right_y.at[pl.ds(x * 512, 512)])
        put(ra_y.at[pl.ds((x * BY + BY - 1) * 256, 256)], face_y.at[pl.ds(x * 256, 256)])

    for x in range(BX):

        @pl.loop(0, 2)
        def _(half):
            for k in range(BY // 2):
                y = half * (BY // 2) + k
                line = x * BY + y
                from_y = jnp.where(y > 0, line - 1, line)
                into_y = jnp.where(y > 0, (line - 1) * BZ, CELLS)
                for z in range(0, BZ, 2):
                    n = line * BZ + z
                    both = range(2)
                    blocks = [
                        (0, ra_d, [(n + k) * 32 for k in both], [n, n + 1]),
                        (2, ra_y, [from_y * 256 + (z + k) * 32 for k in both], [into_y + z, into_y + z + 1]),
                        (3, ra_z, [line * 288 + (z + k) * 32 for k in both], [CELLS if z == 0 else n - 1, n]),
                    ]
                    if x > 0:
                        e = n - BY * BZ
                        blocks.append((1, ra_x, [(e + k) * 32 for k in both], [e, e + 1]))
                    couples(right, n, 1, couple, blocks)

        if x > 0:
            rows = pl.ds((x - 1) * BY * BZ * 64, BY * BZ * 64)
            put(couple.at[rows], couple_out.at[rows])
    rows = pl.ds((BX - 1) * BY * BZ * 64, BY * BZ * 64)
    put(couple.at[rows], couple_out.at[rows])
    for finish in ends:
        finish()
    for copy in moves:
        copy.wait()


def inner(prolong, a_face, a_diag):
    any_space = pl.BlockSpec(memory_space=pl.ANY)
    x_face, y_face, z_face = (BY, BZ, NODES * NODES), (BX, BZ, NODES * NODES), (LINES * 32, 128)
    shapes = (
        (BY * 256, 128), (BX * 256, 128), (LINES * 32, 128), x_face, y_face, z_face,
        (CELLS * 64, 256), (CELLS * 64, 128),
        (BY * 512, 128), (BX * 512, 128), (LINES * 64, 128),
        (BY * 256, 128), (BX * 256, 128), z_face,
    )
    return pl.pallas_call(
        inner_kernel,
        out_shape=[jax.ShapeDtypeStruct(shape, BF16) for shape in shapes],
        in_specs=[any_space] * 3,
        out_specs=[any_space] * len(shapes),
        scratch_shapes=[
            pltpu.VMEM(prolong.shape, BF16),
            pltpu.VMEM(a_diag.shape, BF16),
            pltpu.VMEM(a_face.shape, BF16),
            pltpu.VMEM(x_face, BF16),
            pltpu.VMEM((BY * 256, 128), BF16),
            pltpu.VMEM((BY * 256, 128), BF16),
            pltpu.VMEM((BX * 256, 128), BF16),
            pltpu.VMEM((LINES * 32, 128), BF16),
            pltpu.VMEM(z_face, BF16),
            pltpu.VMEM(z_face, BF16),
            pltpu.VMEM((LINES * 256, 128), BF16),
            pltpu.VMEM((LINES * 256, 128), BF16),
            pltpu.VMEM((LINES * 256, 128), BF16),
            pltpu.VMEM((LINES * 288, 128), BF16),
            pltpu.VMEM((CELLS * 64, 128), BF16),
            pltpu.VMEM((LINES * 64, 128), BF16),
            pltpu.VMEM((CELLS * 64, 128), BF16),
            pltpu.VMEM(((CELLS + BZ) * 64, 256), BF16),
            pltpu.VMEM((BY, 8 * STEP, 128), F32),
            pltpu.VMEM((BY, 8 * STEP_TWICE, 128), F32),
            pltpu.SemaphoreType.DMA((8,)),
            pltpu.SemaphoreType.DMA((6,)),
            pltpu.SemaphoreType.DMA((6,)),
            pltpu.SemaphoreType.DMA((6,)),
            pltpu.SemaphoreType.DMA((5 + 3 * BX,)),
        ],
        compiler_params=pltpu.CompilerParams(collective_id=0, has_side_effects=True, vmem_limit_bytes=63 << 20),
        name="inner",
    )(prolong, a_face, a_diag)


def compute_kernel(
    aggregate, slot, owner, *refs
):
    arrays, refs = refs[:14], refs[14:]
    small, couple_in, left_in = arrays[:6] + arrays[8:], arrays[6], arrays[7]
    send, held, refs = refs[0], refs[1:13], refs[13:]
    m_x, m_y, m_z, p_xp, p_yp, p_zp, right_x, right_y, right_z, face_x, face_y, face_z = held
    (
    small_sems, keys, key_work, key_sem, in_sems, right, left, couple, work_b,
    f_low, f_high, b_low, b_high, rows, absent, tally, sems, absent_sems,
    ) = refs
    fetched = [pltpu.make_async_copy(*pair, small_sems.at[k]) for k, pair in enumerate(zip(small, held))]
    for copy in fetched:
        copy.start()
    plane = BY * BZ * 64
    brought = []
    for x in range(BX):
        at = pl.ds(x * plane, plane)
        for k, (source, dest) in enumerate(((couple_in, couple), (left_in, left))):
            copy = pltpu.make_async_copy(source.at[at], dest.at[at], in_sems.at[x, k])
            copy.start()
            brought.append(copy)

    absent[...] = jnp.full(absent.shape, jnp.nan, BF16)
    marks = []
    for k in range(PLACES):
        mark = pltpu.make_async_copy(absent, send.at[:, pl.ds(k * ROW, 16)], absent_sems.at[k])
        mark.start()
        marks.append(mark)

    key_work[...] = aggregate[...][None] * SLOTS + slot[...]
    told_keys = pltpu.make_async_copy(key_work, keys, key_sem)
    told_keys.start()
    for ref in (f_low, f_high, b_low, b_high):
        ref[...] = jnp.zeros_like(ref)

    for copy in fetched:
        copy.wait()

    right_xp, right_yp, right_zp = 0, BY, BY + BX

    for count, after, base in ((BY, p_xp, right_xp), (BX, p_yp, right_yp)):

        for line in range(count):
            k = line
            spread_twice(after[line], work_b.at[k])
            store_right(right, base + line, work_b.at[k])

    @sweep(LINES, 12)
    def _(line, k):
        low = lane_low((32, 128))
        here = p_zp[pl.ds(pl.multiple_of(line * 32, 32), 32), :].astype(F32)
        turned = pltpu.roll(here, 64, axis=1)
        work = work_b.at[k % BY, pl.ds(k // BY * 64, 64)]
        work[pl.ds(0, 32, stride=2), :] = jnp.where(low, here, turned)
        work[pl.ds(1, 32, stride=2), :] = jnp.where(low, turned, here)
        at = pl.multiple_of((right_zp * 8 + line) * 64, 64)
        right[pl.ds(at, 64), :] = work[...].astype(BF16)

    told_keys.wait()

    def rim_terms(weights, cell, m, at, places):
        low = lane_low((64, 128))
        zero = jnp.zeros((64, 128), BF16)
        first, second = (weights[pl.ds(pl.multiple_of((cell + k) * 64, 64), 64), :] for k in range(2))
        weight = jnp.concatenate([jnp.where(low, first, zero), jnp.where(low, zero, second)], axis=0)
        out = jnp.dot(m[pl.ds(pl.multiple_of(at, 64), 64), :], weight, preferred_element_type=F32)
        b_low[places[0]] += out
        b_high[places[1]] += out

    @sweep(BY, 6)
    def _(y, _turn):
        for z in range(0, BZ, 2):
            rim_terms(right_x, y * BZ + z, m_x, y * 256 + z * 32, [keys[1, y, 0, z + k] for k in range(2)])

    @sweep(BX, 4)
    def _(x, _turn):
        for z in range(0, BZ, 2):
            rim_terms(right_y, x * BZ + z, m_y, x * 256 + z * 32, [keys[3, 0, x, z + k] for k in range(2)])

    @sweep(LINES // 2, 12)
    def _(half, _turn):
        line = half * 2
        places = [keys[5, line % BY + k, line // BY, 0] for k in range(2)]
        rim_terms(right_z, line, m_z, half * 64, places)

    for copy in brought:
        copy.wait()

    @sweep(BY, 6)
    def _(y, _turn):
        for z in range(0, BZ, 2):
            e = ((BX - 1) * BY + y) * BZ + z
            at = y * 256 + z * 32
            couples(right, (right_xp + y) * 8 + z, 1, couple, [(1, face_x, [at, at + 32], [e, e + 1])])

    @sweep(BX, 4)
    def _(x, _turn):
        for z in range(0, BZ, 2):
            e = (x * BY + BY - 1) * BZ + z
            at = x * 256 + z * 32
            couples(right, (right_yp + x) * 8 + z, 1, couple, [(2, face_y, [at, at + 32], [e, e + 1])])

    @sweep(LINES // 2, 12)
    def _(half, _turn):
        line = half * 2
        e = line * BZ + BZ - 1
        couples(right, right_zp * 8 + line, 1, couple, [(3, face_z, [line * 32, line * 32 + 32], [e, e + BZ])])

    def terms(cell, places):
        at = pl.multiple_of(cell * 64, 128)
        out = jnp.dot(left[pl.ds(at, 128), :], couple[pl.ds(at, 128), :], preferred_element_type=F32)
        for k in range(2):
            for f, (key_f, key_b) in places[k].items():
                tile = f // 2
                term = out[k * 64 : k * 64 + 64, tile * 128 : tile * 128 + 128]
                if key_f is not None:
                    (f_low, f_high)[f % 2][key_f] += term
                if key_b is not None:
                    (b_low, b_high)[f % 2][key_b] += term


    @sweep(LINES, 4)
    def _(line, _turn):
        x, y = line // BY, line % BY
        next_x, next_y = jnp.minimum(x + 1, BX - 1), jnp.minimum(y + 1, BY - 1)
        for z in range(0, BZ, 2):
            places = []
            for k in range(z, z + 2):
                onward_x = jnp.where(x < BX - 1, keys[1, y, next_x, k], KEYS)
                onward_y = jnp.where(y < BY - 1, keys[3, next_y, x, k], KEYS)
                places.append(
                    {
                        0: (keys[0, y, x, k], None),
                        1: (keys[2, y, x, k], onward_x),
                        2: (keys[4, y, x, k], onward_y),
                        3: (keys[6, y, x, k], keys[5, y, x, k + 1] if k < BZ - 1 else None),
                    }
                )
            terms(line * BZ + z, places)

    depth = send.shape[0]
    for copy in marks:
        copy.wait()

    for c in range(depth):
        tally[c] = 0

    def fold(r):
        low = lane_low((64, 128))
        for s in range(0, SLOTS, 4):
            blocks = []
            for k in (s, s + 2):
                at = [r * SLOTS + min(k + side, SLOTS - 1) for side in range(2)]
                pair = jnp.where(low, b_low[at[0]], b_high[at[1]])
                pair += pltpu.roll(jnp.where(low, b_low[at[1]], b_high[at[0]]), 64, axis=1)
                blocks.append(pair)
            flipped = jnp.concatenate(blocks, axis=0).astype(BF16).T.astype(F32)
            for k in range(s, min(s + 4, SLOTS)):
                ref = f_low if k < s + 2 else f_high
                ref[r * SLOTS + k] += flipped[k % 2 * 64 : k % 2 * 64 + 64]

    def lay_out(r):
        low_half = lane_low((32, 128))
        for s in range(SLOTS):
            parts = f_low.at[r * SLOTS + s], f_high.at[r * SLOTS + s]
            even, odd = ([ref[pl.ds(p, 32, stride=2), :] for ref in parts] for p in range(2))
            row = jnp.where(low_half, even[0], odd[1])
            row += pltpu.roll(jnp.where(low_half, odd[0], even[1]), 64, axis=1)
            rows[pl.ds(pl.multiple_of(r * ROW + s * 32, 32), 32), :] = row.astype(BF16)

    def hand_out(r):
        c = owner[r]
        place = tally[c]
        tally[c] = place + 1
        pltpu.make_async_copy(
            rows.at[pl.ds(pl.multiple_of(r * ROW, 32), ROW)],
            send.at[c, pl.ds(pl.multiple_of(place * ROW, 32), ROW)],
            sems.at[r],
        ).start()

    @pl.loop(0, AGG_DEV // 4)
    def _(turn):
        for step in (fold, lay_out, hand_out):
            for k in range(4):
                step(turn * 4 + k)

    for r in range(AGG_DEV):
        pltpu.make_async_copy(rows.at[pl.ds(0, ROW)], send.at[0, pl.ds(0, ROW)], sems.at[r]).wait()


def coarse_rows(aggregate, slot, owner, arrays, depth):
    smem = pl.BlockSpec(memory_space=pltpu.SMEM)
    vmem = pl.BlockSpec(memory_space=pltpu.VMEM)
    any_space = pl.BlockSpec(memory_space=pl.ANY)
    beyond = BY + BX + LINES // 8
    return pl.pallas_call(
        compute_kernel,
        out_shape=jax.ShapeDtypeStruct((depth, PACK, 128), BF16),
        in_specs=[vmem, vmem, smem] + [any_space] * len(arrays),
        out_specs=any_space,
        scratch_shapes=[pltpu.VMEM(array.shape, BF16) for array in arrays[:6] + arrays[8:]]
        + [
            pltpu.SemaphoreType.DMA((12,)),
            pltpu.SMEM((SLOTS, BY, BX, BZ), jnp.int32),
            pltpu.VMEM((SLOTS, BY, BX, BZ), jnp.int32),
            pltpu.SemaphoreType.DMA,
            pltpu.SemaphoreType.DMA((BX, 2)),
            pltpu.VMEM((beyond * 512, 128), BF16),
            pltpu.VMEM((CELLS * 64, 128), BF16),
            pltpu.VMEM((CELLS * 64, 256), BF16),
            pltpu.VMEM((BY, 8 * STEP_TWICE, 128), F32),
            pltpu.VMEM((KEYS + 1, 64, 128), F32),
            pltpu.VMEM((KEYS + 1, 64, 128), F32),
            pltpu.VMEM((KEYS + 1, 64, 128), F32),
            pltpu.VMEM((KEYS + 1, 64, 128), F32),
            pltpu.VMEM((AGG_DEV * ROW, 128), BF16),
            pltpu.VMEM((depth, 16, 128), BF16),
            pltpu.SMEM((depth,), jnp.int32),
            pltpu.SemaphoreType.DMA((AGG_DEV,)),
            pltpu.SemaphoreType.DMA((PLACES,)),
        ],
        compiler_params=pltpu.CompilerParams(vmem_limit_bytes=63 << 20),
        name="coarse_rows",
    )(aggregate, slot, owner, *arrays)


GROUP, ROW_STEP, ROW_PARTS = 8, ROW + 4, 4


def place_kernel(taken, out, told, counts, tally, source, held, works, shaped, sems, row_sems, out_sems):
    depth, count = taken.shape[0], out.shape[1]
    loads = [
        pltpu.make_async_copy(taken.at[:, pl.ds(k * ROW, 16)], told.at[k], sems.at[k]) for k in range(PLACES)
    ]
    for load in loads:
        load.start()
    part = depth // ROW_PARTS
    brought = []
    for k in range(ROW_PARTS):
        at = pl.ds(k * part, part)
        copy = pltpu.make_async_copy(taken.at[at], held.at[at], row_sems.at[k])
        copy.start()
        brought.append(copy)

    for load in loads:
        load.wait()
    for c in range(depth):
        here = [told[k, c, 0:1, :].astype(F32) for k in range(PLACES)]
        counts[c : c + 1, :] = sum((value == value).astype(jnp.int32) for value in here)
    move = pltpu.make_async_copy(counts, tally, sems.at[PLACES])
    move.start()
    move.wait()

    total = 0
    for c in range(depth):
        for k in range(PLACES):
            source[total + k] = c * PLACES + k
        total += tally[c, 0]

    for copy in brought:
        copy.wait()

    def out_copy(group):
        rows = pl.ds(pl.multiple_of(group * GROUP, GROUP), GROUP)
        return pltpu.make_async_copy(shaped.at[group], out.at[:, rows, :], out_sems.at[group])

    @sweep(count // GROUP, 2)
    def _(group, side):
        work = works.at[side]
        for k in range(GROUP):
            t = group * GROUP + k
            at = jnp.where(t < total, source[t], 0)
            place = pl.multiple_of(lax.rem(at, PLACES) * ROW, 32)
            row = held[at // PLACES, pl.ds(place, ROW), :].astype(F32)
            work[k * ROW_STEP : k * ROW_STEP + ROW, :] = jnp.where(t < total, row, jnp.zeros_like(row))
        for s in range(SLOTS):
            for tile in range(32):
                piece = work[pl.ds(s * 32 + tile, GROUP, stride=ROW_STEP), :]
                shaped[group, s, :, tile * 128 : tile * 128 + 128] = piece.astype(BF16)
        out_copy(group).start()

    for group in range(count // GROUP):
        out_copy(group).wait()


def place_rows(taken):
    depth = taken.shape[0]
    count = depth * PLACES
    any_space = pl.BlockSpec(memory_space=pl.ANY)
    return pl.pallas_call(
        place_kernel,
        out_shape=jax.ShapeDtypeStruct((SLOTS, count, NODES * NODES), BF16),
        in_specs=[any_space],
        out_specs=any_space,
        scratch_shapes=[
            pltpu.VMEM((PLACES, depth, 16, 128), BF16),
            pltpu.VMEM((depth, 128), jnp.int32),
            pltpu.SMEM((depth, 128), jnp.int32),
            pltpu.SMEM((count + PLACES,), jnp.int32),
            pltpu.VMEM((depth, PACK, 128), BF16),
            pltpu.VMEM((2, GROUP * ROW_STEP, 128), F32),
            pltpu.VMEM((count // GROUP, SLOTS, GROUP, NODES * NODES), BF16),
            pltpu.SemaphoreType.DMA((PLACES + 1,)),
            pltpu.SemaphoreType.DMA((ROW_PARTS,)),
            pltpu.SemaphoreType.DMA((count // GROUP,)),
        ],
        compiler_params=pltpu.CompilerParams(vmem_limit_bytes=63 << 20),
        name="place_rows",
    )(taken)


def shards(a_diag, a_face, prolong, aggregate, pair_slot, row_owner):
    block = a_diag.shape[-1]
    depth = lax.axis_size("gz")
    holding = PLACES * depth

    arrays = inner(prolong, a_face, a_diag)
    send = coarse_rows(
        aggregate.transpose(1, 0, 2), pair_slot.transpose(0, 2, 1, 3), row_owner, arrays, depth
    )
    taken = lax.all_to_all(send, "gz", 0, 0, tiled=True)
    coarse = place_rows(taken).transpose(1, 0, 2)
    return coarse.reshape(1, 1, 1, holding, SLOTS, block)


def solution(mesh):
    return jax.shard_map(
        shards,
        mesh=mesh,
        in_specs=(
            P("gx", "gy", "gz", None),
            P(None, "gx", "gy", "gz", None),
            P("gx", "gy", "gz", None),
            P("gx", "gy", "gz"),
            P(None, "gx", "gy", "gz"),
            P(("gx", "gy", "gz")),
        ),
        out_specs=P("gx", "gy", "gz", None, None, None),
        check_vma=False,
    )
```
